256 devices in a mesh: seq: 32 (over z, x), head: 8 (over y, core).
Axes of the slice: x: 4, y: 4, z: 8, core: 2. Of those that a mesh axis runs over, the one named last changes fastest.
Arguments:
- corpus: bfloat16 [128, 128, 4096], P('seq'), may hold values from -8 to 8
- enc_qkv: bfloat16 [4096, 16, 3, 128], P(None, 'head'), may hold values from -0.1015625 to 0.1015625
- enc_out: bfloat16 [16, 128, 4096], P('head'), may hold values from -0.375 to 0.375
- cca_kv: bfloat16 [4096, 16, 2, 128], P('seq', 'head'), may hold values from -0.09375 to 0.09375
- gain_in: float32 [4096], replicated, may hold values from 0.5 to 2
- gain_out: float32 [4096], replicated, may hold values from 0.5 to 2
- queries: bfloat16 [16384, 16, 128], P('seq', 'head'), may hold values from -100 to 100
- nbr_ids: int32 [256, 2], P('seq'), may hold values from 0 to 127, as said below
Outputs:
- cca_out: bfloat16 [16384, 16, 128], P('seq', 'head')
The draws below stay inside these ranges and needn't reach their ends.
Inputs may be any that keep to these rules, and one draw needn't show every extreme that they name: `nbr_ids`: entry [u, n] is the corpus row of group u's n-th neighbour; row r is held by index r // 4 of seq. The neighbours of one group differ. Among the requests of the 8 groups of one index of seq no owner is named more than 2 times, and in every draw some owner is named exactly 2 times by every index of seq.
All inputs are finite; a program needn't handle non-finite values.
Results may differ from the reference program's by a relative error of at most 0.03.
Values may be sent and summed in bfloat16 or wider, within the bound.
No kernel may reach another device: no remote copies, remote signals or barrier semaphores. Data moves between devices by JAX's collectives and lax.ppermute only.
A program may use at most 128 MiB of HBM per device.

```python
import math
import jax
import jax.numpy as jnp
from jax import lax

D = 4096
HEADS = 16
HS = 128
GROUP = 64
NLEN = 128
NBRS = 2
CAP = 2
C_DEV = 8
CORP_DEV = 4
TOKENS = 16384
GROUPS = 256
CORPUS = 128
N_SEQ = 32


def draw_corpus(key, part):
    noise_key = jax.random.fold_in(jax.random.fold_in(key, 5), 0)
    values = jax.random.normal(noise_key, (CORPUS, NLEN, D), jnp.float32)
    values = jnp.clip(values, -6.0, 6.0)
    return values.astype(jnp.bfloat16)


def draw_enc_qkv(key, part):
    noise_key = jax.random.fold_in(jax.random.fold_in(key, 9), 0)
    spread = D ** (-0.5)
    limit = 6.5 * spread
    values = jnp.clip(jax.random.normal(noise_key, (D, HEADS, 3, HS), jnp.float32) * spread, -6.0 * spread, 6.0 * spread)
    return jnp.clip(values, -limit, limit).astype(jnp.bfloat16)


def draw_queries(key, part):
    noise_key = jax.random.fold_in(jax.random.fold_in(key, 3), 0)
    values = jax.random.normal(noise_key, (TOKENS, HEADS, HS), jnp.float32)
    values = jnp.clip(values, -6.0, 6.0)
    return values.astype(jnp.bfloat16)


def draw_nbr_ids(key, part):
    base_key = jax.random.fold_in(key, 7)
    hot_key, owner_key, row_key, step_key = jax.random.split(base_key, 4)
    hot_owner = jax.random.randint(hot_key, (), 0, N_SEQ)
    demand = C_DEV * NBRS
    spare_slots = (hot_owner + 1 + jnp.arange((N_SEQ - 1) * CAP) // CAP) % N_SEQ

    def one_device(device_key):
        first_key, second_key = jax.random.split(device_key)
        picked = jax.random.permutation(first_key, spare_slots)[:demand - CAP]
        owners = jnp.concatenate([jnp.full((CAP,), hot_owner, jnp.int32), picked.astype(jnp.int32)])
        return jax.random.permutation(second_key, owners)
    owners = jax.vmap(one_device)(jax.random.split(owner_key, N_SEQ)).reshape(GROUPS, NBRS)
    first_row = jax.random.randint(row_key, (GROUPS, 1), 0, CORP_DEV)
    row_step = jax.random.randint(step_key, (GROUPS, 1), 1, CORP_DEV)
    row_pick = jnp.concatenate([first_row, (first_row + row_step) % CORP_DEV], axis=1)
    return (owners * CORP_DEV + row_pick).astype(jnp.int32)


def levels(stream_key, dims, cuts, least, top_value):
    factor_of, own = 1.0, jax.random.fold_in(stream_key, 6)
    for axis_at, parts in cuts:
        heights = jnp.exp(jax.random.uniform(jax.random.fold_in(own, axis_at), (parts,), jnp.float32, least / len(cuts), top_value / len(cuts)))
        factor_of = factor_of * jnp.repeat(heights, dims[axis_at] // parts).reshape([-1 if axis == axis_at else 1 for axis in range(len(dims))])
    return factor_of


def gaussian(rng, shape, scale, most, pieces=(), kind=jnp.bfloat16):
    level = levels(rng, shape, pieces, -0.22, 0.18) if pieces else 1.0
    values = jax.random.normal(rng, shape, jnp.float32) * scale * level
    return jnp.minimum(jnp.maximum(values, -most), most).astype(kind)


def setup_inputs(seed: int = 0) -> dict:
    seeds = jax.random.split(jax.random.key(seed), 9)
    return {
        "corpus": draw_corpus(jax.random.fold_in(seeds[8], 71), 0),
        "enc_qkv": draw_enc_qkv(jax.random.fold_in(seeds[8], 71), 0),
        "enc_out": gaussian(seeds[2], (HEADS, HS, D), (2 * HS) ** -0.5, 0.375, ((0, 8),)),
        "cca_kv": gaussian(seeds[3], (D, HEADS, 2, HS), D ** -0.5, 0.09375, ((0, 32), (1, 8))),
        "gain_in": jnp.clip(jnp.exp(jax.random.uniform(seeds[4], (D,), jnp.float32, math.log(0.5), math.log(2.0))), 0.5, 2.0),
        "gain_out": jnp.clip(jnp.exp(jax.random.uniform(seeds[5], (D,), jnp.float32, math.log(0.5), math.log(2.0))), 0.5, 2.0),
        "queries": draw_queries(jax.random.fold_in(seeds[8], 71), 0),
        "nbr_ids": draw_nbr_ids(jax.random.fold_in(seeds[8], 71), 0),
    }


EPS = 1e-06

def rms_scale(values, gain):
    mean_square = lax.optimization_barrier(jnp.mean(values * values, axis=-1, keepdims=True))
    return values * lax.rsqrt(mean_square + EPS) * gain

def to_bf16_and_back(values):
    rounded = lax.optimization_barrier(values.astype(jnp.bfloat16))
    return rounded.astype(jnp.float32)

def encode_row(corpus_row, enc_qkv, enc_out, cca_kv, gain_in, gain_out):
    tokens_f32 = corpus_row.astype(jnp.float32)
    normed_in = rms_scale(tokens_f32, gain_in).astype(jnp.bfloat16)
    projected = jnp.dot(normed_in, enc_qkv.reshape(D, HEADS * 3 * HS), preferred_element_type=jnp.float32).astype(jnp.bfloat16)
    projected = projected.reshape(NLEN, HEADS, 3, HS).astype(jnp.float32)
    scores = jnp.einsum('qhs,khs->hqk', projected[:, :, 0], projected[:, :, 1]) * HS ** (-0.5)
    probs = to_bf16_and_back(jax.nn.softmax(scores, axis=-1))
    attended = jnp.einsum('hqk,khs->qhs', probs, projected[:, :, 2]).astype(jnp.bfloat16)
    enc_sum = jnp.dot(attended.reshape(NLEN, HEADS * HS), enc_out.reshape(HEADS * HS, D), preferred_element_type=jnp.float32)
    normed = rms_scale(tokens_f32 + enc_sum, gain_out).astype(jnp.bfloat16)
    memory = jnp.dot(normed, cca_kv.reshape(D, HEADS * 2 * HS), preferred_element_type=jnp.float32).astype(jnp.bfloat16)
    return memory.reshape(NLEN, HEADS, 2, HS)

def reference(corpus, enc_qkv, enc_out, cca_kv, gain_in, gain_out, queries, nbr_ids):
    table = lax.map(lambda corpus_row: encode_row(corpus_row, enc_qkv, enc_out, cca_kv, gain_in, gain_out), corpus)

    def window(pair):
        block, picks = pair
        window_memory = jnp.take(table, picks.astype(jnp.int32), axis=0).reshape(NBRS * NLEN, HEADS, 2, HS).astype(jnp.float32)
        scores = jnp.einsum('qhs,khs->hqk', block.astype(jnp.float32), window_memory[:, :, 0]) * HS ** (-0.5)
        probs = to_bf16_and_back(jax.nn.softmax(scores, axis=-1))
        return jnp.einsum('hqk,khs->qhs', probs, window_memory[:, :, 1]).astype(jnp.bfloat16)
    lead = GROUP - 1
    blocks = jnp.concatenate([queries[lead:], jnp.zeros((lead, HEADS, HS), queries.dtype)], axis=0)
    blocks = blocks.reshape(GROUPS, GROUP, HEADS, HS)
    outputs = lax.map(window, (blocks, nbr_ids)).reshape(TOKENS, HEADS, HS)
    return jnp.concatenate([jnp.zeros((lead, HEADS, HS), outputs.dtype), outputs[:TOKENS - lead]], axis=0)
```

```python
import functools

import jax
import jax.numpy as jnp
from jax import lax
from jax.experimental import pallas as pl
from jax.experimental.pallas import tpu as pltpu
from jax.sharding import Mesh, PartitionSpec as P

GROUP = 64
EPS = 1e-06
NZ, NX, NY, NC = 8, 4, 4, 2
ROW = 128
HS = 128
CHUNKS = 2
MASKED = -1e30
BF = jnp.bfloat16
F32 = jnp.float32
ANY = pl.BlockSpec(memory_space=pl.ANY)
VMEM_ALL = pl.BlockSpec(memory_space=pltpu.VMEM)


def shifted(value, axis, steps):
    n = lax.axis_size(axis)
    return lax.ppermute(value, axis, [(i, (i + steps) % n) for i in range(n)])


def spread(value, axis):
    n = lax.axis_size(axis)
    copies = jnp.broadcast_to(value[None], (n,) + value.shape)
    return lax.all_to_all(copies, axis, split_axis=0, concat_axis=0, tiled=True)


def encoder_kernel(core_ref, x_ref, w_ref, g_ref, out_ref, wide, wmat, acc, ssq):
    step = pl.program_id(0)
    depth = x_ref.shape[1]

    @pl.when(step == 0)
    def _():
        acc[...] = jnp.zeros_like(acc)
        ssq[...] = jnp.zeros_like(ssq)

    wide[...] = w_ref[...].astype(F32)
    for col in range(6):
        wmat[:, col * HS:(col + 1) * HS] = wide[pl.ds(col, depth, stride=6), :].astype(BF)
    x = x_ref[...].astype(F32)
    ssq[...] += jnp.sum(x * x, axis=1, keepdims=True)
    xg = (x * g_ref[...]).astype(BF)
    acc[...] += jnp.dot(xg, wmat[...], preferred_element_type=F32)

    @pl.when(step == pl.num_programs(0) - 1)
    def _():
        core = core_ref[0]
        total = depth * pl.num_programs(0)
        rinv = lax.rsqrt(ssq[...] / total + EPS)
        rows = x_ref.shape[0] // ROW
        for r in range(rows):
            sl = slice(r * ROW, (r + 1) * ROW)
            scale = rinv[sl]
            parts = []
            for h in range(2):
                q = (acc[sl, h * HS:(h + 1) * HS] * scale).astype(BF)
                k = (acc[sl, (2 + h) * HS:(3 + h) * HS] * scale).astype(BF)
                v = (acc[sl, (4 + h) * HS:(5 + h) * HS] * scale).astype(BF)
                s = lax.dot_general(q, k, (((1,), (1,)), ((), ())), preferred_element_type=F32)
                s = s * (HS ** -0.5)
                m = jnp.max(s, axis=1, keepdims=True)
                p = jnp.exp(s - m)
                p = (p / jnp.sum(p, axis=1, keepdims=True)).astype(BF)
                parts.append(jnp.dot(p, v, preferred_element_type=F32).astype(BF))
            place = (r // 2 + core) % 2
            att = jnp.concatenate(parts, axis=1)
            out_ref[place, r % 2] = att


def encode(corpus_flat, w_rows, gain, core):
    tokens, width = corpus_flat.shape
    steps = 8
    depth = width // steps
    return pl.pallas_call(
        encoder_kernel,
        grid_spec=pltpu.PrefetchScalarGridSpec(
            num_scalar_prefetch=1,
            grid=(steps,),
            in_specs=[
                pl.BlockSpec((tokens, depth), lambda i, c: (0, i)),
                pl.BlockSpec((depth * 6, HS), lambda i, c: (i, 0)),
                pl.BlockSpec((1, depth), lambda i, c: (0, i)),
            ],
            out_specs=pl.BlockSpec((2, 2, ROW, 2 * HS), lambda i, c: (0, 0, 0, 0)),
            scratch_shapes=[
                pltpu.VMEM((depth * 6, HS), F32),
                pltpu.VMEM((depth, 6 * HS), BF),
                pltpu.VMEM((tokens, 6 * HS), F32),
                pltpu.VMEM((tokens, 1), F32),
            ],
        ),
        out_shape=jax.ShapeDtypeStruct((2, 2, ROW, 2 * HS), BF),
        cost_estimate=pl.CostEstimate(
            flops=2 * tokens * width * 6 * HS, bytes_accessed=(tokens + 768) * width * 2, transcendentals=0
        ),
        name="encoder",
    )(core, corpus_flat, w_rows, gain)


def project_kernel(a_ref, b_ref, ea_ref, eb_ref, out_ref):
    total = jnp.dot(a_ref[...], ea_ref[...], preferred_element_type=F32)
    total += jnp.dot(b_ref[...], eb_ref[...], preferred_element_type=F32)
    out_ref[...] = total.astype(BF)


def project(att_own, att_other, e_own, e_other):
    tokens, depth = att_own.shape
    width = e_own.shape[1]
    cols = 1024
    return pl.pallas_call(
        project_kernel,
        grid=(width // cols,),
        in_specs=[
            pl.BlockSpec((tokens, depth), lambda i: (0, 0)),
            pl.BlockSpec((tokens, depth), lambda i: (0, 0)),
            pl.BlockSpec((depth, cols), lambda i: (0, i)),
            pl.BlockSpec((depth, cols), lambda i: (0, i)),
        ],
        out_specs=pl.BlockSpec((tokens, cols), lambda i: (0, i)),
        out_shape=jax.ShapeDtypeStruct((tokens, width), BF),
        cost_estimate=pl.CostEstimate(
            flops=4 * tokens * depth * width, bytes_accessed=4 * depth * width, transcendentals=0
        ),
        name="project",
    )(att_own, att_other, e_own, e_other)


def norm_kernel(block_ref, terms_ref, x_ref, g_ref, out_ref):
    total = x_ref[...].astype(F32)
    for i in range(NY):
        total += terms_ref[i].astype(F32)
    rinv = lax.rsqrt(jnp.mean(total * total, axis=1, keepdims=True) + EPS)
    u = (total * rinv * g_ref[...]).astype(BF)
    for z in range(NZ):
        for x in range(NX):
            src, dst = (z * NX + x) * HS, (x * NZ + z) * HS
            piece = u[:, src:src + HS]
            for i in range(NY):
                out_ref[i, :, dst:dst + HS] = piece


def normalise(terms, corpus_flat, gain, block):
    _, rows, width = terms.shape
    return pl.pallas_call(
        norm_kernel,
        grid_spec=pltpu.PrefetchScalarGridSpec(
            num_scalar_prefetch=1,
            grid=(1,),
            in_specs=[
                pl.BlockSpec((NY, rows, width), lambda i, b: (0, 0, 0)),
                pl.BlockSpec((rows, width), lambda i, b: (b[0], 0)),
                pl.BlockSpec((1, width), lambda i, b: (0, 0)),
            ],
            out_specs=pl.BlockSpec((NY, rows, width), lambda i, b: (0, 0, 0)),
        ),
        out_shape=jax.ShapeDtypeStruct((NY, rows, width), BF),
        cost_estimate=pl.CostEstimate(flops=8 * rows * width, bytes_accessed=18 * rows * width, transcendentals=0),
        name="normalise",
    )(block, terms, corpus_flat, gain)


def memory_kernel(a_ref, b_ref, k_ref, out_ref, acc):
    step = pl.program_id(0)
    half = a_ref.shape[0]

    @pl.when(step == 0)
    def _():
        acc[...] = jnp.zeros_like(acc)

    u = jnp.concatenate([a_ref[...], b_ref[...]], axis=0)
    acc[...] += jnp.dot(u, k_ref[...], preferred_element_type=F32)

    @pl.when(step == pl.num_programs(0) - 1)
    def _():
        out_ref[...] = acc[...].astype(BF)


def memorise(u_own, u_other, weight):
    half, width = u_own.shape
    cols = weight.shape[1]
    steps = 4
    depth = width // steps
    return pl.pallas_call(
        memory_kernel,
        grid=(steps,),
        in_specs=[
            pl.BlockSpec((half, depth), lambda i: (0, i)),
            pl.BlockSpec((half, depth), lambda i: (0, i)),
            pl.BlockSpec((depth, cols), lambda i: (i, 0)),
        ],
        out_specs=pl.BlockSpec((2 * half, cols), lambda i: (0, 0)),
        scratch_shapes=[pltpu.VMEM((2 * half, cols), F32)],
        out_shape=jax.ShapeDtypeStruct((2 * half, cols), BF),
        cost_estimate=pl.CostEstimate(
            flops=4 * half * width * cols, bytes_accessed=2 * width * cols, transcendentals=0
        ),
        name="memorise",
    )(u_own, u_other, weight)


def ring_pieces(block):
    rows = block.shape[0]
    half = rows // 2
    pieces = [(0, 0, rows, block)]
    up = down = block
    for s in range(1, NZ // 2):
        up = shifted(up, "z", 1)
        down = shifted(down, "z", -1)
        pieces += [(s, 0, rows, up), (NZ - s, 0, rows, down)]
    pieces += [
        (NZ // 2, 0, half, shifted(up[:half], "z", 1)),
        (NZ // 2, half, half, shifted(down[half:], "z", -1)),
    ]
    return pieces


PAD = 8


def window_kernel(layout, ids_ref, at_ref, q_ref, *refs):
    pieces = refs[:len(layout)]
    out_ref = refs[len(layout)]
    table, qs, outs, stats, sem = refs[len(layout) + 1:]
    copies = []
    for i, (chunk, distance, first, rows) in enumerate(layout):
        copies.append(
            pltpu.make_async_copy(pieces[i], table.at[distance, chunk, pl.ds(first, rows)], sem.at[i])
        )
    for copy in copies:
        copy.start()
    my_z, my_x, core = at_ref[0], at_ref[1], at_ref[2]
    plane_rows = NX * 1024
    qs[0:PAD, :] = jnp.zeros((PAD, HS), F32)
    qs[PAD + plane_rows:, :] = jnp.zeros((qs.shape[0] - PAD - plane_rows, HS), F32)
    for x in range(NX):
        qs[PAD + x * 1024:PAD + (x + 1) * 1024, :] = q_ref[x, 0:1024].astype(F32)
    for copy in copies:
        copy.wait()

    def place(row):
        row = jnp.maximum(row, 0)
        distance = lax.rem(my_z - row // 16 + NZ, NZ)
        local = lax.rem(row, 4)
        chunk = lax.rem(local, 2)
        half = lax.rem(local // 2 + core, 2)
        return distance, chunk, pl.multiple_of(half * ROW, ROW)

    def held(row):
        return jnp.logical_and(row >= 0, lax.rem(jnp.maximum(row, 0) // 4, NX) == my_x)

    def body(w, carry):
        start = PAD + 2 * (GROUP * w - 1)
        rows = [ids_ref[w, n] for n in range(2)]
        ok = [held(row) for row in rows]
        any_ok = jnp.logical_or(ok[0], ok[1])

        @pl.when(any_ok)
        def _():
            spots = [place(row) for row in rows]
            for h in range(2):
                q = qs[pl.ds(start + h, GROUP, stride=2), :].astype(BF)
                scores = []
                for n in range(2):
                    d, c, first = spots[n]
                    k = table[d, c, pl.ds(first, ROW), h * 256:h * 256 + HS]
                    s = lax.dot_general(q, k, (((1,), (1,)), ((), ())), preferred_element_type=F32)
                    s = s * (HS ** -0.5)
                    scores.append(jnp.where(ok[n], s, MASKED))
                m = jnp.maximum(
                    jnp.max(scores[0], axis=1, keepdims=True), jnp.max(scores[1], axis=1, keepdims=True)
                )
                probs = [jnp.exp(s - m) for s in scores]
                total = jnp.sum(probs[0], axis=1, keepdims=True) + jnp.sum(probs[1], axis=1, keepdims=True)
                inv = 1.0 / total
                out = jnp.zeros((GROUP, HS), F32)
                for n in range(2):
                    d, c, first = spots[n]
                    v = table[d, c, pl.ds(first, ROW), h * 256 + HS:h * 256 + 2 * HS]
                    out += jnp.dot((probs[n] * inv).astype(BF), v, preferred_element_type=F32)
                outs[pl.ds(start + h, GROUP, stride=2), :] = out
                lse = m + jnp.log(total)
                stats[pl.ds(start + h, GROUP, stride=2), :] = jnp.broadcast_to(lse, (GROUP, HS))

        @pl.when(jnp.logical_not(any_ok))
        def _():
            for h in range(2):
                outs[pl.ds(start + h, GROUP, stride=2), :] = jnp.zeros((GROUP, HS), F32)
                stats[pl.ds(start + h, GROUP, stride=2), :] = jnp.full((GROUP, HS), MASKED, F32)

        return carry

    lax.fori_loop(0, ids_ref.shape[0], body, 0)
    eye = lax.broadcasted_iota(jnp.int32, (HS, HS), 0) == lax.broadcasted_iota(jnp.int32, (HS, HS), 1)
    for x in range(NX):
        base = PAD + x * 1024
        out_ref[x, 0:1024] = outs[base:base + 1024, :].astype(BF)
        lines = []
        for b in range(8):
            block = stats[base + b * HS:base + (b + 1) * HS, :]
            lines.append(jnp.sum(jnp.where(eye, block, 0.0), axis=0, keepdims=True))
        lse = jnp.concatenate(lines, axis=0)
        high = lse.astype(BF)
        rest = lse - high.astype(F32)
        middle = rest.astype(BF)
        low = (rest - middle.astype(F32)).astype(BF)
        tail = jnp.concatenate([high.astype(F32), middle.astype(F32), low.astype(F32), jnp.zeros((8, HS), F32)], axis=0)
        out_ref[x, 1024:1056] = tail.astype(BF)


def windows(ids, at, q_plane, pieces):
    layout = tuple((chunk, d, first, rows) for chunk, d, first, rows, _ in pieces)
    total = PAD + NX * 1024 + 2 * GROUP
    return pl.pallas_call(
        functools.partial(window_kernel, layout),
        grid_spec=pltpu.PrefetchScalarGridSpec(
            num_scalar_prefetch=2,
            grid=(1,),
            in_specs=[pl.BlockSpec(q_plane.shape, lambda i, a, b: (0, 0, 0))] + [ANY] * len(pieces),
            out_specs=pl.BlockSpec((NX, 1056, HS), lambda i, a, b: (0, 0, 0)),
            scratch_shapes=[
                pltpu.VMEM((NZ, CHUNKS, 4 * ROW // CHUNKS, 512), BF),
                pltpu.VMEM((total, HS), F32),
                pltpu.VMEM((total, HS), F32),
                pltpu.VMEM((total, HS), F32),
                pltpu.SemaphoreType.DMA((len(pieces),)),
            ],
        ),
        out_shape=jax.ShapeDtypeStruct((NX, 1056, HS), BF),
        cost_estimate=pl.CostEstimate(flops=10**9, bytes_accessed=8 * 2**20, transcendentals=10**6),
        name="windows",
    )(ids, at, q_plane, *[piece[-1] for piece in pieces])


def combine_kernel(parts_ref, out_ref):
    logs = []
    for x in range(NX):
        tail = parts_ref[x, 1024:1056].astype(F32)
        logs.append(tail[0:8] + tail[8:16] + tail[16:24])
    m = functools.reduce(jnp.maximum, logs)
    weights = [jnp.exp(v - m) for v in logs]
    inv = 1.0 / functools.reduce(jnp.add, weights)
    weights = [w * inv for w in weights]
    eye = lax.broadcasted_iota(jnp.int32, (HS, HS), 0) == lax.broadcasted_iota(jnp.int32, (HS, HS), 1)
    for b in range(8):
        total = jnp.zeros((HS, HS), F32)
        for x in range(NX):
            line = jnp.broadcast_to(weights[x][b:b + 1, :], (HS, HS))
            column = jnp.sum(jnp.where(eye, line, 0.0), axis=1, keepdims=True)
            total += column * parts_ref[x, b * HS:(b + 1) * HS].astype(F32)
        out_ref[b * HS:(b + 1) * HS, :] = total.astype(BF)


def combine(parts):
    return pl.pallas_call(
        combine_kernel,
        in_specs=[VMEM_ALL],
        out_specs=VMEM_ALL,
        out_shape=jax.ShapeDtypeStruct((1024, HS), BF),
        cost_estimate=pl.CostEstimate(flops=10**7, bytes_accessed=2 * 2**20, transcendentals=0),
        name="combine",
    )(parts)


def on_device(corpus, enc_qkv, enc_out, cca_kv, gain_in, gain_out, queries, nbr_ids):
    width = corpus.shape[2]
    my_z, my_x, my_y, core = (lax.axis_index(a) for a in ("z", "x", "y", "c"))
    corpus_flat = corpus.reshape(-1, width)
    e_own = enc_out.reshape(2 * HS, width)
    e_other = shifted(e_own, "c", 1)

    kv = lax.optimization_barrier(cca_kv.reshape(cca_kv.shape[0], 512))
    kv = spread(kv, "z").reshape(-1, 512)
    kv = spread(kv, "x").reshape(-1, 512)

    last = lax.ppermute(
        nbr_ids[7:], ("z", "x"), [(i, i + 1) for i in range(NZ * NX - 1)]
    )
    last = jnp.where(jnp.logical_and(my_z == 0, my_x == 0), -1, last)
    ids = jnp.concatenate([last, nbr_ids], axis=0).astype(BF)
    ids = jnp.pad(ids, ((0, 7), (0, HS - 2)))
    q_rows = jnp.concatenate([queries.reshape(1024, HS), ids], axis=0)
    q_plane = spread(q_rows, "x").reshape(NX, 1040, HS)
    got = q_plane[:, 1024:1033, 0:2].astype(jnp.int32)
    plane_ids = jnp.concatenate([got[0], got[1, 1:], got[2, 1:], got[3, 1:]], axis=0)

    w_rows = enc_qkv.transpose(0, 2, 1, 3).reshape(width * 6, HS)
    att = encode(corpus_flat, w_rows, gain_in.reshape(1, width), core.reshape(1).astype(jnp.int32))
    att_own, att_send = att[0], att[1]
    att_other = shifted(att_send, "c", 1)

    pieces = []
    for j in range(CHUNKS):
        own = att_own[j]
        other = att_other[j]
        partial = project(own, other, e_own, e_other).reshape(NY, ROW // NY, width)
        terms = lax.all_to_all(partial, "y", split_axis=0, concat_axis=0, tiled=True)
        block = ((2 * core + j) * NY + my_y).reshape(1).astype(jnp.int32)
        copies = normalise(terms, corpus_flat, gain_out.reshape(1, width), block)
        u = lax.all_to_all(copies, "y", split_axis=0, concat_axis=0, tiled=True)
        u_own = u.reshape(ROW, width)
        u_other = shifted(u_own, "c", 1)
        memory = memorise(u_own, u_other, kv)
        pieces += [(j,) + piece for piece in ring_pieces(memory)]

    at = jnp.stack([my_z, my_x, core]).astype(jnp.int32)
    parts = windows(plane_ids, at, q_plane, pieces)
    parts = lax.all_to_all(parts, "x", split_axis=0, concat_axis=0, tiled=True)
    return combine(parts).reshape(512, 2, HS)


def solution(mesh):
    inner = Mesh(mesh.devices.reshape(NZ, NX, NY, NC), ("z", "x", "y", "c"))
    seq, head = ("z", "x"), ("y", "c")
    placed = (
        P(seq, None, None),
        P(None, head, None, None),
        P(head, None, None),
        P(seq, head, None, None),
        P(),
        P(),
        P(seq, head, None),
        P(seq, None),
    )
    return jax.shard_map(
        on_device, mesh=inner, in_specs=placed, out_specs=P(seq, head, None), check_vma=False
    )
```

```python
import functools

import jax
import jax.numpy as jnp
from jax import lax
from jax.experimental import pallas as pl
from jax.experimental.pallas import tpu as pltpu
from jax.sharding import Mesh, PartitionSpec as P

GROUP = 64
EPS = 1e-06
NZ, NX, NY, NC = 8, 4, 4, 2
ROW = 128
HS = 128
MASKED = -1e30
BF = jnp.bfloat16
F32 = jnp.float32
ANY = pl.BlockSpec(memory_space=pl.ANY)
VMEM_ALL = pl.BlockSpec(memory_space=pltpu.VMEM)


def shifted(value, axis, steps):
    n = lax.axis_size(axis)
    return lax.ppermute(value, axis, [(i, (i + steps) % n) for i in range(n)])


def spread(value, axis):
    n = lax.axis_size(axis)
    copies = jnp.broadcast_to(value[None], (n,) + value.shape)
    return lax.all_to_all(copies, axis, split_axis=0, concat_axis=0, tiled=True)


def encoder_kernel(core_ref, x_ref, w_ref, g_ref, own_ref, send_ref, wide, wmat, acc, ssq):
    step = pl.program_id(0)
    depth = x_ref.shape[1]

    @pl.when(step == 0)
    def _():
        acc[...] = jnp.zeros_like(acc)
        ssq[...] = jnp.zeros_like(ssq)

    wide[...] = w_ref[...].astype(F32)
    for col in range(6):
        wmat[:, col * HS:(col + 1) * HS] = wide[pl.ds(col, depth, stride=6), :].astype(BF)
    x = x_ref[...].astype(F32)
    ssq[...] += jnp.sum(x * x, axis=1, keepdims=True)
    xg = (x * g_ref[...]).astype(BF)
    acc[...] += jnp.dot(xg, wmat[...], preferred_element_type=F32)

    @pl.when(step == pl.num_programs(0) - 1)
    def _():
        core = core_ref[0]
        total = depth * pl.num_programs(0)
        rinv = lax.rsqrt(ssq[...] / total + EPS)
        rows = x_ref.shape[0] // ROW
        for r in range(rows):
            sl = slice(r * ROW, (r + 1) * ROW)
            scale = rinv[sl]
            parts = []
            for h in range(2):
                q = (acc[sl, h * HS:(h + 1) * HS] * scale).astype(BF)
                k = (acc[sl, (2 + h) * HS:(3 + h) * HS] * scale).astype(BF)
                v = (acc[sl, (4 + h) * HS:(5 + h) * HS] * scale).astype(BF)
                s = lax.dot_general(q, k, (((1,), (1,)), ((), ())), preferred_element_type=F32)
                s = s * (HS ** -0.5)
                m = jnp.max(s, axis=1, keepdims=True)
                p = jnp.exp(s - m)
                p = (p / jnp.sum(p, axis=1, keepdims=True)).astype(BF)
                parts.append(jnp.dot(p, v, preferred_element_type=F32).astype(BF))
            att = jnp.concatenate(parts, axis=1)
            spot = slice((r % 2) * ROW, (r % 2 + 1) * ROW)

            @pl.when(core == r // 2)
            def _():
                own_ref[spot, :] = att

            @pl.when(core != r // 2)
            def _():
                send_ref[spot, :] = att


def encode(corpus_flat, w_rows, gain, core):
    tokens, width = corpus_flat.shape
    steps = 8
    depth = width // steps
    return pl.pallas_call(
        encoder_kernel,
        grid_spec=pltpu.PrefetchScalarGridSpec(
            num_scalar_prefetch=1,
            grid=(steps,),
            in_specs=[
                pl.BlockSpec((tokens, depth), lambda i, c: (0, i)),
                pl.BlockSpec((depth * 6, HS), lambda i, c: (i, 0)),
                pl.BlockSpec((1, depth), lambda i, c: (0, i)),
            ],
            out_specs=[pl.BlockSpec((2 * ROW, 2 * HS), lambda i, c: (0, 0))] * 2,
            scratch_shapes=[
                pltpu.VMEM((depth * 6, HS), F32),
                pltpu.VMEM((depth, 6 * HS), BF),
                pltpu.VMEM((tokens, 6 * HS), F32),
                pltpu.VMEM((tokens, 1), F32),
            ],
        ),
        out_shape=[jax.ShapeDtypeStruct((2 * ROW, 2 * HS), BF)] * 2,
        cost_estimate=pl.CostEstimate(
            flops=2 * tokens * width * 6 * HS, bytes_accessed=(tokens + 768) * width * 2, transcendentals=0
        ),
        name="encoder",
    )(core, corpus_flat, w_rows, gain)


def project_kernel(a_ref, b_ref, ea_ref, eb_ref, out_ref):
    total = jnp.dot(a_ref[...], ea_ref[...], preferred_element_type=F32)
    total += jnp.dot(b_ref[...], eb_ref[...], preferred_element_type=F32)
    out_ref[...] = total.astype(BF)


def project(att_own, att_other, e_own, e_other):
    tokens, depth = att_own.shape
    width = e_own.shape[1]
    cols = 1024
    return pl.pallas_call(
        project_kernel,
        grid=(width // cols,),
        in_specs=[
            pl.BlockSpec((tokens, depth), lambda i: (0, 0)),
            pl.BlockSpec((tokens, depth), lambda i: (0, 0)),
            pl.BlockSpec((depth, cols), lambda i: (0, i)),
            pl.BlockSpec((depth, cols), lambda i: (0, i)),
        ],
        out_specs=pl.BlockSpec((tokens, cols), lambda i: (0, i)),
        out_shape=jax.ShapeDtypeStruct((tokens, width), BF),
        cost_estimate=pl.CostEstimate(
            flops=4 * tokens * depth * width, bytes_accessed=4 * depth * width, transcendentals=0
        ),
        name="project",
    )(att_own, att_other, e_own, e_other)


def norm_kernel(block_ref, terms_ref, x_ref, g_ref, out_ref):
    total = x_ref[...].astype(F32)
    for i in range(NY):
        total += terms_ref[i].astype(F32)
    rinv = lax.rsqrt(jnp.mean(total * total, axis=1, keepdims=True) + EPS)
    u = (total * rinv * g_ref[...]).astype(BF)
    for z in range(NZ):
        for x in range(NX):
            src, dst = (z * NX + x) * HS, (x * NZ + z) * HS
            piece = u[:, src:src + HS]
            for i in range(NY):
                out_ref[i, :, dst:dst + HS] = piece


def normalise(terms, corpus_flat, gain, block):
    _, rows, width = terms.shape
    return pl.pallas_call(
        norm_kernel,
        grid_spec=pltpu.PrefetchScalarGridSpec(
            num_scalar_prefetch=1,
            grid=(1,),
            in_specs=[
                VMEM_ALL,
                pl.BlockSpec((rows, width), lambda i, b: (b[0], 0)),
                pl.BlockSpec((1, width), lambda i, b: (0, 0)),
            ],
            out_specs=pl.BlockSpec((NY, rows, width), lambda i, b: (0, 0, 0)),
        ),
        out_shape=jax.ShapeDtypeStruct((NY, rows, width), BF),
        cost_estimate=pl.CostEstimate(flops=8 * rows * width, bytes_accessed=18 * rows * width, transcendentals=0),
        name="normalise",
    )(block, terms, corpus_flat, gain)


ORDER = (0, NX - 1, 1, 2)


def memory_kernel(x_ref, a_ref, b_ref, k0, k1, k2, k3, out_ref, ua, ub, kv, sem):
    depth = NZ * HS
    half = ua.shape[1]
    copies = []
    for i, k_ref in enumerate((k0, k1, k2, k3)):
        first = pl.multiple_of(lax.rem(x_ref[0] + ORDER[i], NX) * depth, depth)
        copies.append((
            pltpu.make_async_copy(k_ref.at[pl.ds(0, depth)], kv.at[i], sem.at[0, i]),
            pltpu.make_async_copy(a_ref.at[:, pl.ds(first, depth)], ua.at[i], sem.at[1, i]),
            pltpu.make_async_copy(b_ref.at[:, pl.ds(first, depth)], ub.at[i], sem.at[2, i]),
        ))
    for group in copies:
        for copy in group:
            copy.start()
    totals = [jnp.zeros((half, out_ref.shape[1]), F32) for _ in range(2)]
    for i, group in enumerate(copies):
        for copy in group:
            copy.wait()
        for part, u in enumerate((ua, ub)):
            totals[part] += jnp.dot(u[i], kv[i], preferred_element_type=F32)
    for part in range(2):
        out_ref[part * half:(part + 1) * half, :] = totals[part].astype(BF)


def memorise(my_x, u_own, u_other, payloads):
    half, width = u_own.shape
    cols = payloads[0].shape[1]
    depth = width // NX
    return pl.pallas_call(
        memory_kernel,
        in_specs=[pl.BlockSpec(memory_space=pltpu.SMEM)] + [ANY] * 6,
        out_specs=VMEM_ALL,
        scratch_shapes=[
            pltpu.VMEM((NX, half, depth), BF),
            pltpu.VMEM((NX, half, depth), BF),
            pltpu.VMEM((NX, depth, cols), BF),
            pltpu.SemaphoreType.DMA((3, NX)),
        ],
        out_shape=jax.ShapeDtypeStruct((2 * half, cols), BF),
        cost_estimate=pl.CostEstimate(
            flops=4 * half * width * cols, bytes_accessed=2 * width * cols, transcendentals=0
        ),
        name="memorise",
    )(my_x, u_own, u_other, *payloads)


def ring_pieces(block):
    rows = block.shape[0]
    half = rows // 2
    pieces = [(0, 0, rows, block)]
    up = down = block
    for s in range(1, NZ // 2):
        up = shifted(up, "z", 1)
        down = shifted(down, "z", -1)
        pieces += [(s, 0, rows, up), (NZ - s, 0, rows, down)]
    pieces += [
        (NZ // 2, 0, half, shifted(up[:half], "z", 1)),
        (NZ // 2, half, half, shifted(down[half:], "z", -1)),
    ]
    return pieces


PAD = 8
Q_FIRST = NZ * HS


def window_kernel(layout, ids_ref, at_ref, *refs):
    payloads = refs[:NX]
    pieces = refs[NX:NX + len(layout)]
    out_ref = refs[NX + len(layout)]
    table, q_in, qs, outs, stats, active, sem, q_sem = refs[NX + len(layout) + 1:]
    my_z, my_x, core = at_ref[0], at_ref[1], at_ref[2]
    count_all = NX * 8 + 1
    plane_rows = NX * 1024
    total_rows = qs.shape[0]
    q_copies = [
        pltpu.make_async_copy(payloads[i].at[pl.ds(Q_FIRST, 256)], q_in.at[i], q_sem.at[i]) for i in range(NX)
    ]
    copies = [
        pltpu.make_async_copy(pieces[i], table.at[distance, pl.ds(first, rows)], sem.at[i])
        for i, (distance, first, rows) in enumerate(layout)
    ]
    for copy in q_copies + copies:
        copy.start()
    outs[...] = jnp.zeros_like(outs)
    stats[...] = jnp.full_like(stats, MASKED)
    qs[0:PAD, :] = jnp.zeros((PAD, HS), F32)
    qs[PAD + plane_rows:, :] = jnp.zeros((total_rows - PAD - plane_rows, HS), F32)
    for i in range(NX):
        base = PAD + lax.rem(my_x + ORDER[i], NX) * 1024
        q_copies[i].wait()
        for b in range(4):
            first = pl.multiple_of(base + b * 256, 8)
            qs[pl.ds(first, 256), :] = q_in[i, :, b * HS:(b + 1) * HS].astype(F32)
    for copy in copies:
        copy.wait()

    def held(row):
        return jnp.logical_and(row >= 0, lax.rem(jnp.maximum(row, 0) // 4, NX) == my_x)

    def wanted(w, n):
        group = jnp.maximum(w - 1, 0)
        step = lax.rem(group // 8 - my_x + NX, NX)
        return ids_ref[step * 18 + jnp.where(w == 0, 0, lax.rem(group, 8) + 1) * 2 + n]

    def note(w, count):
        use = jnp.logical_or(held(wanted(w, 0)), held(wanted(w, 1)))
        active[count] = w
        return count + use.astype(jnp.int32)

    count = lax.fori_loop(0, count_all, note, 0)

    def place(row):
        row = jnp.maximum(row, 0)
        distance = lax.rem(my_z - row // 16 + NZ, NZ)
        local = lax.rem(row, 4)
        half = lax.rem(local // 2 + core, 2)
        return distance, pl.multiple_of(half * 2 * ROW + lax.rem(local, 2) * ROW, ROW)

    def window(w):
        start = PAD + 2 * (GROUP * w - 1)
        rows = [wanted(w, n) for n in range(2)]
        ok = [held(row) for row in rows]
        spots = [place(row) for row in rows]
        results = []
        for h in range(2):
            q = qs[pl.ds(start + h, GROUP, stride=2), :].astype(BF)
            scores = []
            for n in range(2):
                d, first = spots[n]
                k = table[d, pl.ds(first, ROW), h * 256:h * 256 + HS]
                s = lax.dot_general(q, k, (((1,), (1,)), ((), ())), preferred_element_type=F32)
                s = s * (HS ** -0.5)
                scores.append(jnp.where(ok[n], s, MASKED))
            m = jnp.max(jnp.maximum(scores[0], scores[1]), axis=1, keepdims=True)
            probs = [jnp.exp(s - m) for s in scores]
            total = jnp.sum(probs[0] + probs[1], axis=1, keepdims=True)
            inv = 1.0 / total
            out = jnp.zeros((GROUP, HS), F32)
            for n in range(2):
                d, first = spots[n]
                v = table[d, pl.ds(first, ROW), h * 256 + HS:h * 256 + 2 * HS]
                out += jnp.dot((probs[n] * inv).astype(BF), v, preferred_element_type=F32)
            lse = jnp.broadcast_to(m + jnp.log(total), (GROUP, HS))
            results.append((start + h, out, lse))
        return results

    side = 2

    def body(i, carry):
        results = []
        for lane in range(side):
            results += window(active[jnp.minimum(i * side + lane, count - 1)])
        for first, out, lse in results:
            outs[pl.ds(first, GROUP, stride=2), :] = out
            stats[pl.ds(first, GROUP, stride=2), :] = lse
        return carry

    lax.fori_loop(0, (count + side - 1) // side, body, 0)
    eye = lax.broadcasted_iota(jnp.int32, (HS, HS), 0) == lax.broadcasted_iota(jnp.int32, (HS, HS), 1)
    for x in range(NX):
        base = PAD + x * 1024
        out_ref[x, 0:1024] = outs[base:base + 1024, :].astype(BF)
        lines = []
        for b in range(8):
            block = stats[base + b * HS:base + (b + 1) * HS, :]
            lines.append(jnp.sum(jnp.where(eye, block, 0.0), axis=0, keepdims=True))
        lse = jnp.concatenate(lines, axis=0)
        high = lse.astype(BF)
        rest = lse - high.astype(F32)
        middle = rest.astype(BF)
        low = (rest - middle.astype(F32)).astype(BF)
        tail = jnp.concatenate([high.astype(F32), middle.astype(F32), low.astype(F32), jnp.zeros((8, HS), F32)], axis=0)
        out_ref[x, 1024:1056] = tail.astype(BF)


def windows(ids, at, payloads, pieces):
    layout = tuple((d, first, rows) for d, first, rows, _ in pieces)
    total = PAD + NX * 1024 + 2 * GROUP
    smem = pl.BlockSpec(memory_space=pltpu.SMEM)
    return pl.pallas_call(
        functools.partial(window_kernel, layout),
        in_specs=[smem, smem] + [ANY] * (NX + len(pieces)),
        out_specs=VMEM_ALL,
        scratch_shapes=[
            pltpu.VMEM((NZ, 4 * ROW, 512), BF),
            pltpu.VMEM((NX, 256, 512), BF),
            pltpu.VMEM((total, HS), F32),
            pltpu.VMEM((total, HS), F32),
            pltpu.VMEM((total, HS), F32),
            pltpu.SMEM((NX * 8 + 2,), jnp.int32),
            pltpu.SemaphoreType.DMA((len(pieces),)),
            pltpu.SemaphoreType.DMA((NX,)),
        ],
        out_shape=jax.ShapeDtypeStruct((NX, 1056, HS), BF),
        cost_estimate=pl.CostEstimate(flops=10**9, bytes_accessed=8 * 2**20, transcendentals=10**6),
        name="windows",
    )(ids, at, *payloads, *[piece[-1] for piece in pieces])


def combine_kernel(parts_ref, out_ref):
    logs = []
    for x in range(NX):
        tail = parts_ref[x, 1024:1056].astype(F32)
        logs.append(tail[0:8] + tail[8:16] + tail[16:24])
    m = functools.reduce(jnp.maximum, logs)
    weights = [jnp.exp(v - m) for v in logs]
    inv = 1.0 / functools.reduce(jnp.add, weights)
    weights = [w * inv for w in weights]
    eye = lax.broadcasted_iota(jnp.int32, (HS, HS), 0) == lax.broadcasted_iota(jnp.int32, (HS, HS), 1)
    for b in range(8):
        total = jnp.zeros((HS, HS), F32)
        for x in range(NX):
            line = jnp.broadcast_to(weights[x][b:b + 1, :], (HS, HS))
            column = jnp.sum(jnp.where(eye, line, 0.0), axis=1, keepdims=True)
            total += column * parts_ref[x, b * HS:(b + 1) * HS].astype(F32)
        out_ref[b * HS:(b + 1) * HS, :] = total.astype(BF)


def combine(parts):
    return pl.pallas_call(
        combine_kernel,
        in_specs=[VMEM_ALL],
        out_specs=VMEM_ALL,
        out_shape=jax.ShapeDtypeStruct((1024, HS), BF),
        cost_estimate=pl.CostEstimate(flops=10**7, bytes_accessed=2 * 2**20, transcendentals=0),
        name="combine",
    )(parts)


def on_device(corpus, enc_qkv, enc_out, cca_kv, gain_in, gain_out, queries, nbr_ids):
    width = corpus.shape[2]
    my_z, my_x, my_y, core = (lax.axis_index(a) for a in ("z", "x", "y", "c"))
    corpus_flat = corpus.reshape(-1, width)
    e_own = enc_out.reshape(2 * HS, width)
    e_other = shifted(e_own, "c", 1)

    last = lax.ppermute(nbr_ids[7:], ("z", "x"), [(i, i + 1) for i in range(NZ * NX - 1)])
    last = jnp.where(jnp.logical_and(my_z == 0, my_x == 0), -1, last)
    ids = jnp.concatenate([last, nbr_ids], axis=0).astype(BF)

    kv = lax.optimization_barrier(cca_kv.reshape(cca_kv.shape[0], 512))
    kv = spread(kv, "z").reshape(-1, 512)
    q_rows = queries.reshape(4, 256, HS)
    q_wide = jnp.concatenate([q_rows[b] for b in range(4)], axis=1)
    payload = jnp.concatenate([kv, q_wide, jnp.pad(ids, ((0, 7), (0, 510)))], axis=0)
    from_left = shifted(payload, "x", 1)
    from_right = shifted(payload, "x", -1)
    from_far = shifted(payload, "x", 2)

    w_rows = enc_qkv.transpose(0, 2, 1, 3).reshape(width * 6, HS)
    att_own, att_send = encode(
        corpus_flat, w_rows, gain_in.reshape(1, width), core.reshape(1).astype(jnp.int32)
    )
    att_other = shifted(att_send, "c", 1)
    partial = project(att_own, att_other, e_own, e_other).reshape(NY, 2 * ROW // NY, width)
    terms = lax.all_to_all(partial, "y", split_axis=0, concat_axis=0, tiled=True)
    block = (core * NY + my_y).reshape(1).astype(jnp.int32)
    copies = normalise(terms, corpus_flat, gain_out.reshape(1, width), block)
    copies, from_left, from_right = lax.optimization_barrier((copies, from_left, from_right))
    u_own = lax.all_to_all(copies, "y", split_axis=0, concat_axis=0, tiled=True).reshape(2 * ROW, width)
    u_own, from_far = lax.optimization_barrier((u_own, from_far))
    u_other = shifted(u_own, "c", 1)
    payloads = [payload, from_left, from_right, from_far]
    memory = memorise(my_x.reshape(1).astype(jnp.int32), u_own, u_other, payloads)
    pieces = ring_pieces(memory)

    by_step = [payloads[ORDER.index(d)] for d in range(NX)]
    got = jnp.stack([p[Q_FIRST + 256:Q_FIRST + 265, 0:2] for p in by_step]).astype(jnp.int32)
    at = jnp.stack([my_z, my_x, core]).astype(jnp.int32)
    got, at = lax.optimization_barrier((got.reshape(-1), at))
    parts = windows(got, at, payloads, pieces)
    parts = lax.all_to_all(parts, "x", split_axis=0, concat_axis=0, tiled=True)
    return combine(parts).reshape(512, 2, HS)


def solution(mesh):
    inner = Mesh(mesh.devices.reshape(NZ, NX, NY, NC), ("z", "x", "y", "c"))
    seq, head = ("z", "x"), ("y", "c")
    placed = (
        P(seq, None, None),
        P(None, head, None, None),
        P(head, None, None),
        P(seq, head, None, None),
        P(),
        P(),
        P(seq, head, None),
        P(seq, None),
    )
    return jax.shard_map(
        on_device, mesh=inner, in_specs=placed, out_specs=P(seq, head, None), check_vma=False
    )
```

```python
import functools

import jax
import jax.numpy as jnp
from jax import lax
from jax.experimental import pallas as pl
from jax.experimental.pallas import tpu as pltpu
from jax.sharding import Mesh, PartitionSpec as P

GROUP = 64
EPS = 1e-06
MIB = 2**20
NZ, NX, NY, NC = 8, 4, 4, 2
ROW = 128
HS = 128
MASKED = -1e30
BF = jnp.bfloat16
F32 = jnp.float32
ANY = pl.BlockSpec(memory_space=pl.ANY)
VMEM_ALL = pl.BlockSpec(memory_space=pltpu.VMEM)


def shifted(value, axis, steps):
    n = lax.axis_size(axis)
    return lax.ppermute(value, axis, [(i, (i + steps) % n) for i in range(n)])


def spread(value, axis):
    n = lax.axis_size(axis)
    copies = jnp.broadcast_to(value[None], (n,) + value.shape)
    return lax.all_to_all(copies, axis, split_axis=0, concat_axis=0, tiled=True)


def encoder_kernel(core_ref, x_ref, w_ref, g_ref, own_ref, send_ref, wide, wmat, acc, ssq):
    step = pl.program_id(0)
    depth = x_ref.shape[1]

    @pl.when(step == 0)
    def _():
        acc[...] = jnp.zeros_like(acc)
        ssq[...] = jnp.zeros_like(ssq)

    wide[...] = w_ref[...].astype(F32)
    for col in range(6):
        wmat[:, col * HS:(col + 1) * HS] = wide[pl.ds(col, depth, stride=6), :].astype(BF)
    x = x_ref[...].astype(F32)
    ssq[...] += jnp.sum(x * x, axis=1, keepdims=True)
    xg = (x * g_ref[...]).astype(BF)
    acc[...] += jnp.dot(xg, wmat[...], preferred_element_type=F32)

    @pl.when(step == pl.num_programs(0) - 1)
    def _():
        core = core_ref[0]
        total = depth * pl.num_programs(0)
        rinv = lax.rsqrt(ssq[...] / total + EPS)
        rows = x_ref.shape[0] // ROW
        for r in range(rows):
            sl = slice(r * ROW, (r + 1) * ROW)
            scale = rinv[sl]
            parts = []
            for h in range(2):
                q = (acc[sl, h * HS:(h + 1) * HS] * scale).astype(BF)
                k = (acc[sl, (2 + h) * HS:(3 + h) * HS] * scale).astype(BF)
                v = (acc[sl, (4 + h) * HS:(5 + h) * HS] * scale).astype(BF)
                s = lax.dot_general(q, k, (((1,), (1,)), ((), ())), preferred_element_type=F32)
                s = s * (HS ** -0.5)
                m = jnp.max(s, axis=1, keepdims=True)
                p = jnp.exp(s - m)
                p = (p / jnp.sum(p, axis=1, keepdims=True)).astype(BF)
                parts.append(jnp.dot(p, v, preferred_element_type=F32).astype(BF))
            att = jnp.concatenate(parts, axis=1)
            spot = slice((r % 2) * ROW, (r % 2 + 1) * ROW)

            @pl.when(core == r // 2)
            def _():
                own_ref[spot, :] = att

            @pl.when(core != r // 2)
            def _():
                send_ref[spot, :] = att


def encode(corpus_flat, w_rows, gain, core):
    tokens, width = corpus_flat.shape
    steps = 8
    depth = width // steps
    return pl.pallas_call(
        encoder_kernel,
        grid_spec=pltpu.PrefetchScalarGridSpec(
            num_scalar_prefetch=1,
            grid=(steps,),
            in_specs=[
                pl.BlockSpec((tokens, depth), lambda i, c: (0, i)),
                pl.BlockSpec((depth * 6, HS), lambda i, c: (i, 0)),
                pl.BlockSpec((1, depth), lambda i, c: (0, i)),
            ],
            out_specs=[pl.BlockSpec((2 * ROW, 2 * HS), lambda i, c: (0, 0))] * 2,
            scratch_shapes=[
                pltpu.VMEM((depth * 6, HS), F32),
                pltpu.VMEM((depth, 6 * HS), BF),
                pltpu.VMEM((tokens, 6 * HS), F32),
                pltpu.VMEM((tokens, 1), F32),
            ],
        ),
        out_shape=[jax.ShapeDtypeStruct((2 * ROW, 2 * HS), BF)] * 2,
        cost_estimate=pl.CostEstimate(
            flops=2 * tokens * width * 6 * HS, bytes_accessed=(tokens + 768) * width * 2, transcendentals=0
        ),
        compiler_params=pltpu.CompilerParams(vmem_limit_bytes=60 * MIB),
        name="encoder",
    )(core, corpus_flat, w_rows, gain)


def project_kernel(y_ref, a_ref, b_ref, ea_ref, eb_ref, *refs):
    outs, total = refs[:NY], refs[NY]
    rows = total.shape[0] // NY
    value = jnp.dot(a_ref[...], ea_ref[...], preferred_element_type=F32)
    value += jnp.dot(b_ref[...], eb_ref[...], preferred_element_type=F32)
    total[...] = value.astype(BF)
    for k in range(NY):
        first = pl.multiple_of(lax.rem(y_ref[0] + k, NY) * rows, rows)
        outs[k][...] = total[pl.ds(first, rows), :]


def project(my_y, att_own, att_other, e_own, e_other):
    tokens, depth = att_own.shape
    width = e_own.shape[1]
    cols = 1024
    rows = tokens // NY
    return pl.pallas_call(
        project_kernel,
        grid_spec=pltpu.PrefetchScalarGridSpec(
            num_scalar_prefetch=1,
            grid=(width // cols,),
            in_specs=[
                pl.BlockSpec((tokens, depth), lambda i, y: (0, 0)),
                pl.BlockSpec((tokens, depth), lambda i, y: (0, 0)),
                pl.BlockSpec((depth, cols), lambda i, y: (0, i)),
                pl.BlockSpec((depth, cols), lambda i, y: (0, i)),
            ],
            out_specs=[pl.BlockSpec((rows, cols), lambda i, y: (0, i))] * NY,
            scratch_shapes=[pltpu.VMEM((tokens, cols), BF)],
        ),
        out_shape=[jax.ShapeDtypeStruct((rows, width), BF)] * NY,
        cost_estimate=pl.CostEstimate(
            flops=4 * tokens * depth * width, bytes_accessed=4 * depth * width, transcendentals=0
        ),
        compiler_params=pltpu.CompilerParams(vmem_limit_bytes=12 * MIB),
        name="project",
    )(my_y, att_own, att_other, e_own, e_other)


def norm_kernel(block_ref, t0, t1, t2, t3, x_ref, g_ref, out_ref):
    total = x_ref[...].astype(F32)
    for term in (t0, t1, t2, t3):
        total += term[...].astype(F32)
    rinv = lax.rsqrt(jnp.mean(total * total, axis=1, keepdims=True) + EPS)
    u = (total * rinv * g_ref[...]).astype(BF)
    for z in range(NZ):
        for x in range(NX):
            src, dst = (z * NX + x) * HS, (x * NZ + z) * HS
            out_ref[:, dst:dst + HS] = u[:, src:src + HS]


def normalise(terms, corpus_flat, gain, block):
    rows, width = terms[0].shape
    whole = pl.BlockSpec((rows, width), lambda i, b: (0, 0))
    return pl.pallas_call(
        norm_kernel,
        grid_spec=pltpu.PrefetchScalarGridSpec(
            num_scalar_prefetch=1,
            grid=(1,),
            in_specs=[whole] * NY
            + [
                pl.BlockSpec((rows, width), lambda i, b: (b[0], 0)),
                pl.BlockSpec((1, width), lambda i, b: (0, 0)),
            ],
            out_specs=whole,
        ),
        out_shape=jax.ShapeDtypeStruct((rows, width), BF),
        cost_estimate=pl.CostEstimate(flops=8 * rows * width, bytes_accessed=12 * rows * width, transcendentals=0),
        compiler_params=pltpu.CompilerParams(vmem_limit_bytes=60 * MIB),
        name="normalise",
    )(block, *terms, corpus_flat, gain)


ORDER = (0, NX - 1, 1, 2)


def memory_kernel(parts, at_ref, *refs):
    us = refs[:parts]
    k0, k1, k2, k3, k4 = refs[parts:parts + 5]
    out_ref = refs[parts + 5]
    rest = refs[parts + 6:]
    if parts > 1:
        whole, rest = rest[0], rest[1:]
    ua, kv, sem, out_sem = rest
    depth = NZ * HS
    rows = ua.shape[0] // parts
    u_copies = []
    for k in range(parts):
        first = pl.multiple_of(lax.rem(at_ref[1] - k + parts, parts) * rows, rows)
        u_copies.append(pltpu.make_async_copy(us[k], ua.at[pl.ds(first, rows)], sem.at[k]))
    near = [
        pltpu.make_async_copy(k_ref.at[pl.ds(0, depth)], kv.at[i], sem.at[NY + i])
        for i, k_ref in enumerate((k0, k1, k2))
    ]
    top, bottom = k3.shape[0], depth - k3.shape[0]
    far = [
        pltpu.make_async_copy(k3, kv.at[3, pl.ds(0, top)], sem.at[NY + 3]),
        pltpu.make_async_copy(k4.at[pl.ds(0, bottom)], kv.at[3, pl.ds(top, bottom)], sem.at[NY + 4]),
    ]
    for copy in u_copies + near + far:
        copy.start()
    for copy in u_copies:
        copy.wait()
    if parts > 1:
        back = pltpu.make_async_copy(ua, whole, out_sem)
        back.start()
    total = jnp.zeros(out_ref.shape, F32)
    for i in range(NX):
        for copy in (near[i:i + 1] if i < 3 else far):
            copy.wait()
        first = pl.multiple_of(lax.rem(at_ref[0] + ORDER[i], NX) * depth, depth)
        total += jnp.dot(ua[:, pl.ds(first, depth)], kv[i], preferred_element_type=F32)
    out_ref[...] = total.astype(BF)
    if parts > 1:
        back.wait()


def memorise(at, us, payloads):
    width = us[0].shape[1]
    tokens = us[0].shape[0] * len(us)
    cols = payloads[0].shape[1]
    depth = width // NX
    memory = jax.ShapeDtypeStruct((tokens, cols), BF)
    assembled = [jax.ShapeDtypeStruct((tokens, width), BF)] if len(us) > 1 else []
    return pl.pallas_call(
        functools.partial(memory_kernel, len(us)),
        in_specs=[pl.BlockSpec(memory_space=pltpu.SMEM)] + [ANY] * (len(us) + 5),
        out_specs=[VMEM_ALL] + [ANY] * len(assembled),
        scratch_shapes=[
            pltpu.VMEM((tokens, width), BF),
            pltpu.VMEM((NX, depth, cols), BF),
            pltpu.SemaphoreType.DMA((NY + 5,)),
            pltpu.SemaphoreType.DMA,
        ],
        out_shape=[memory] + assembled,
        cost_estimate=pl.CostEstimate(
            flops=2 * tokens * width * cols, bytes_accessed=2 * width * cols, transcendentals=0
        ),
        compiler_params=pltpu.CompilerParams(vmem_limit_bytes=12 * MIB),
        name="memorise",
    )(at, *us, *payloads)


def ring_pieces(block, base):
    rows = block.shape[0]
    half = rows // 2
    pieces = [(0, base, rows, block)]
    up = down = block
    for s in range(1, NZ // 2):
        up = shifted(up, "z", 1)
        down = shifted(down, "z", -1)
        pieces += [(s, base, rows, up), (NZ - s, base, rows, down)]
    pieces += [
        (NZ // 2, base, half, shifted(up[:half], "z", 1)),
        (NZ // 2, base + half, half, shifted(down[half:], "z", -1)),
    ]
    return pieces


PAD = 8
Q_FIRST = NZ * HS
PAYLOAD_TOP = 640


def window_kernel(layout, ids_ref, at_ref, *refs):
    payloads = refs[:NX]
    pieces = refs[NX:NX + len(layout)]
    out_ref = refs[NX + len(layout)]
    table, q_in, qs, outs, stats, active, sem, q_sem = refs[NX + len(layout) + 1:]
    q_first = (Q_FIRST, Q_FIRST, Q_FIRST, Q_FIRST - PAYLOAD_TOP)
    my_z, my_x, core = at_ref[0], at_ref[1], at_ref[2]
    count_all = NX * 8 + 1
    plane_rows = NX * 1024
    total_rows = qs.shape[0]
    q_copies = [
        pltpu.make_async_copy(payloads[i].at[pl.ds(q_first[i], 256)], q_in.at[i], q_sem.at[i]) for i in range(NX)
    ]
    copies = [
        pltpu.make_async_copy(pieces[i], table.at[distance, pl.ds(first, rows)], sem.at[i])
        for i, (distance, first, rows) in enumerate(layout)
    ]
    for copy in q_copies + copies:
        copy.start()
    outs[...] = jnp.zeros_like(outs)
    stats[...] = jnp.full_like(stats, MASKED)
    qs[0:PAD, :] = jnp.zeros((PAD, HS), F32)
    qs[PAD + plane_rows:, :] = jnp.zeros((total_rows - PAD - plane_rows, HS), F32)
    for i in range(NX):
        base = PAD + lax.rem(my_x + ORDER[i], NX) * 1024
        q_copies[i].wait()
        for b in range(4):
            first = pl.multiple_of(base + b * 256, 8)
            qs[pl.ds(first, 256), :] = q_in[i, :, b * HS:(b + 1) * HS].astype(F32)
    for copy in copies:
        copy.wait()

    def held(row):
        return jnp.logical_and(row >= 0, lax.rem(jnp.maximum(row, 0) // 4, NX) == my_x)

    def wanted(w, n):
        group = jnp.maximum(w - 1, 0)
        step = lax.rem(group // 8 - my_x + NX, NX)
        return ids_ref[step * 18 + jnp.where(w == 0, 0, lax.rem(group, 8) + 1) * 2 + n]

    def note(w, count):
        use = jnp.logical_or(held(wanted(w, 0)), held(wanted(w, 1)))
        active[count] = w
        return count + use.astype(jnp.int32)

    count = lax.fori_loop(0, count_all, note, 0)

    def place(row):
        row = jnp.maximum(row, 0)
        distance = lax.rem(my_z - row // 16 + NZ, NZ)
        local = lax.rem(row, 4)
        half = lax.rem(local // 2 + core, 2)
        return distance, pl.multiple_of(half * 2 * ROW + lax.rem(local, 2) * ROW, ROW)

    def window(w):
        start = PAD + 2 * (GROUP * w - 1)
        rows = [wanted(w, n) for n in range(2)]
        ok = [held(row) for row in rows]
        spots = [place(row) for row in rows]
        results = []
        for h in range(2):
            q = qs[pl.ds(start + h, GROUP, stride=2), :].astype(BF)
            scores = []
            for n in range(2):
                d, first = spots[n]
                k = table[d, pl.ds(first, ROW), h * 256:h * 256 + HS]
                s = lax.dot_general(q, k, (((1,), (1,)), ((), ())), preferred_element_type=F32)
                s = s * (HS ** -0.5)
                scores.append(jnp.where(ok[n], s, MASKED))
            m = jnp.max(jnp.maximum(scores[0], scores[1]), axis=1, keepdims=True)
            probs = [jnp.exp(s - m) for s in scores]
            total = jnp.sum(probs[0] + probs[1], axis=1, keepdims=True)
            inv = 1.0 / total
            out = jnp.zeros((GROUP, HS), F32)
            for n in range(2):
                d, first = spots[n]
                v = table[d, pl.ds(first, ROW), h * 256 + HS:h * 256 + 2 * HS]
                out += jnp.dot((probs[n] * inv).astype(BF), v, preferred_element_type=F32)
            lse = jnp.broadcast_to(m + jnp.log(total), (GROUP, HS))
            results.append((start + h, out, lse))
        return results

    side = 2

    def body(i, carry):
        results = []
        for lane in range(side):
            results += window(active[jnp.minimum(i * side + lane, count - 1)])
        for first, out, lse in results:
            outs[pl.ds(first, GROUP, stride=2), :] = out
            stats[pl.ds(first, GROUP, stride=2), :] = lse
        return carry

    lax.fori_loop(0, (count + side - 1) // side, body, 0)
    eye = lax.broadcasted_iota(jnp.int32, (HS, HS), 0) == lax.broadcasted_iota(jnp.int32, (HS, HS), 1)
    for x in range(NX):
        base = PAD + x * 1024
        out_ref[x, 0:1024] = outs[base:base + 1024, :].astype(BF)
        lines = []
        for b in range(8):
            block = stats[base + b * HS:base + (b + 1) * HS, :]
            lines.append(jnp.sum(jnp.where(eye, block, 0.0), axis=0, keepdims=True))
        lse = jnp.concatenate(lines, axis=0)
        high = lse.astype(BF)
        rest = lse - high.astype(F32)
        middle = rest.astype(BF)
        low = (rest - middle.astype(F32)).astype(BF)
        tail = jnp.concatenate([high.astype(F32), middle.astype(F32), low.astype(F32), jnp.zeros((8, HS), F32)], axis=0)
        out_ref[x, 1024:1056] = tail.astype(BF)


def windows(ids, at, payloads, pieces):
    layout = tuple((d, first, rows) for d, first, rows, _ in pieces)
    total = PAD + NX * 1024 + 2 * GROUP
    smem = pl.BlockSpec(memory_space=pltpu.SMEM)
    return pl.pallas_call(
        functools.partial(window_kernel, layout),
        in_specs=[smem, smem] + [ANY] * (NX + len(pieces)),
        out_specs=VMEM_ALL,
        scratch_shapes=[
            pltpu.VMEM((NZ, 4 * ROW, 512), BF),
            pltpu.VMEM((NX, 256, 512), BF),
            pltpu.VMEM((total, HS), F32),
            pltpu.VMEM((total, HS), F32),
            pltpu.VMEM((total, HS), F32),
            pltpu.SMEM((NX * 8 + 2,), jnp.int32),
            pltpu.SemaphoreType.DMA((len(pieces),)),
            pltpu.SemaphoreType.DMA((NX,)),
        ],
        out_shape=jax.ShapeDtypeStruct((NX, 1056, HS), BF),
        cost_estimate=pl.CostEstimate(flops=10**9, bytes_accessed=8 * 2**20, transcendentals=10**6),
        compiler_params=pltpu.CompilerParams(vmem_limit_bytes=58 * MIB),
        name="windows",
    )(ids, at, *payloads, *[piece[-1] for piece in pieces])


def combine_kernel(parts_ref, out_ref):
    logs = []
    for x in range(NX):
        tail = parts_ref[x, 1024:1056].astype(F32)
        logs.append(tail[0:8] + tail[8:16] + tail[16:24])
    m = functools.reduce(jnp.maximum, logs)
    weights = [jnp.exp(v - m) for v in logs]
    inv = 1.0 / functools.reduce(jnp.add, weights)
    weights = [w * inv for w in weights]
    eye = lax.broadcasted_iota(jnp.int32, (HS, HS), 0) == lax.broadcasted_iota(jnp.int32, (HS, HS), 1)
    for b in range(8):
        total = jnp.zeros((HS, HS), F32)
        for x in range(NX):
            line = jnp.broadcast_to(weights[x][b:b + 1, :], (HS, HS))
            column = jnp.sum(jnp.where(eye, line, 0.0), axis=1, keepdims=True)
            total += column * parts_ref[x, b * HS:(b + 1) * HS].astype(F32)
        out_ref[b * HS:(b + 1) * HS, :] = total.astype(BF)


def combine(parts):
    return pl.pallas_call(
        combine_kernel,
        in_specs=[VMEM_ALL],
        out_specs=VMEM_ALL,
        out_shape=jax.ShapeDtypeStruct((1024, HS), BF),
        cost_estimate=pl.CostEstimate(flops=10**7, bytes_accessed=2 * 2**20, transcendentals=0),
        compiler_params=pltpu.CompilerParams(vmem_limit_bytes=8 * MIB),
        name="combine",
    )(parts)


def as_index(*values):
    return jnp.stack(values).astype(jnp.int32)


def on_device(corpus, enc_qkv, enc_out, cca_kv, gain_in, gain_out, queries, nbr_ids):
    width = corpus.shape[2]
    my_z, my_x, my_y, core = (lax.axis_index(a) for a in ("z", "x", "y", "c"))
    corpus_flat = corpus.reshape(-1, width)
    e_own = enc_out.reshape(2 * HS, width)
    e_other = shifted(e_own, "c", 1)

    kv = lax.optimization_barrier(cca_kv.reshape(cca_kv.shape[0], 512))
    kv = spread(kv, "z").reshape(-1, 512)

    w_rows = enc_qkv.transpose(0, 2, 1, 3).reshape(width * 6, HS)
    att_own, att_send = encode(corpus_flat, w_rows, gain_in.reshape(1, width), as_index(core))
    nbr_ids, queries, att_send = lax.optimization_barrier((nbr_ids, queries, att_send))
    att_other = shifted(att_send, "c", 1)

    last = lax.ppermute(nbr_ids[7:], ("z", "x"), [(i, i + 1) for i in range(NZ * NX - 1)])
    last = jnp.where(jnp.logical_and(my_z == 0, my_x == 0), -1, last)
    ids = jnp.concatenate([last, nbr_ids], axis=0).astype(BF)
    terms = project(as_index(my_y), att_own, att_other, e_own, e_other)

    kv, terms = lax.optimization_barrier((kv, terms))
    q_rows = queries.reshape(4, 256, HS)
    q_wide = jnp.concatenate([q_rows[b] for b in range(4)], axis=1)
    payload = jnp.concatenate([kv, q_wide, jnp.pad(ids, ((0, 7), (0, 510)))], axis=0)
    from_left = shifted(payload, "x", 1)
    from_right = shifted(payload, "x", -1)

    terms = [terms[0]] + [shifted(terms[k], "y", k) for k in range(1, NY)]
    u = normalise(terms, corpus_flat, gain_out.reshape(1, width), as_index(core * NY + my_y))
    u, from_left, from_right = lax.optimization_barrier((u, from_left, from_right))
    far_top = shifted(from_left[:PAYLOAD_TOP], "x", 1)
    far_bottom = shifted(from_right[PAYLOAD_TOP:], "x", -1)
    payloads = [payload, from_left, from_right, far_top, far_bottom]
    us = [u] + [shifted(u, "y", k) for k in range(1, NY)]
    at = as_index(my_x, my_y)
    memory_own, u_own = memorise(at, us, payloads)
    u_other = shifted(u_own, "c", 1)
    pieces = ring_pieces(memory_own, 0)
    (memory_other,) = memorise(at, [u_other], payloads)
    pieces += ring_pieces(memory_other, 2 * ROW)

    ids_first = Q_FIRST + 256
    near = [p[ids_first:ids_first + 9, 0:2] for p in payloads[:3]]
    far = far_bottom[ids_first - PAYLOAD_TOP:ids_first - PAYLOAD_TOP + 9, 0:2]
    got = jnp.stack([near[0], near[2], far, near[1]]).astype(jnp.int32)
    got, at = lax.optimization_barrier((got.reshape(-1), as_index(my_z, my_x, core)))
    payloads = payloads[:3] + [far_bottom]
    parts = windows(got, at, payloads, pieces)
    parts = lax.all_to_all(parts, "x", split_axis=0, concat_axis=0, tiled=True)
    return combine(parts).reshape(512, 2, HS)


def solution(mesh):
    inner = Mesh(mesh.devices.reshape(NZ, NX, NY, NC), ("z", "x", "y", "c"))
    seq, head = ("z", "x"), ("y", "c")
    placed = (
        P(seq, None, None),
        P(None, head, None, None),
        P(head, None, None),
        P(seq, head, None, None),
        P(),
        P(),
        P(seq, head, None),
        P(seq, None),
    )
    return jax.shard_map(
        on_device, mesh=inner, in_specs=placed, out_specs=P(seq, head, None), check_vma=False
    )
```

```python
import functools

import jax
import jax.numpy as jnp
from jax import lax
from jax.experimental import pallas as pl
from jax.experimental.pallas import tpu as pltpu
from jax.sharding import Mesh, PartitionSpec as P

GROUP = 64
EPS = 1e-06
MIB = 2**20
NZ, NX, NY, NC = 8, 4, 4, 2
ROW = 128
HS = 128
MASKED = -1e30
LOG_SCALE = HS ** -0.5 * 1.4426950408889634
BF = jnp.bfloat16
F32 = jnp.float32
ANY = pl.BlockSpec(memory_space=pl.ANY)
VMEM_ALL = pl.BlockSpec(memory_space=pltpu.VMEM)


def shifted(value, axis, steps):
    n = lax.axis_size(axis)
    return lax.ppermute(value, axis, [(i, (i + steps) % n) for i in range(n)])


def spread(value, axis):
    n = lax.axis_size(axis)
    copies = jnp.broadcast_to(value[None], (n,) + value.shape)
    return lax.all_to_all(copies, axis, split_axis=0, concat_axis=0, tiled=True)


def encoder_kernel(at_ref, x_ref, w_ref, g_ref, out_ref, wide, wmat, acc, ssq):
    step = pl.program_id(0)
    depth = x_ref.shape[1]

    @pl.when(step == 0)
    def _():
        acc[...] = jnp.zeros_like(acc)
        ssq[...] = jnp.zeros_like(ssq)

    wide[...] = w_ref[...].astype(F32)
    for col in range(6):
        wmat[:, col * HS:(col + 1) * HS] = wide[pl.ds(col, depth, stride=6), :].astype(BF)
    x = x_ref[...].astype(F32)
    ssq[...] += jnp.sum(x * x, axis=1, keepdims=True)
    xg = (x * g_ref[...]).astype(BF)
    acc[...] += jnp.dot(xg, wmat[...], preferred_element_type=F32)

    @pl.when(step == pl.num_programs(0) - 1)
    def _():
        core, my_y = at_ref[0], at_ref[1]
        total = depth * pl.num_programs(0)
        scale = lax.rsqrt(ssq[...] / total + EPS)
        rows = x_ref.shape[0] // ROW
        for pair in range(rows // 2):
            spots = [(r, h) for r in (2 * pair, 2 * pair + 1) for h in range(2)]

            def part(r, col):
                sl = slice(r * ROW, (r + 1) * ROW)
                return (acc[sl, col * HS:(col + 1) * HS] * scale[sl]).astype(BF)

            scores = [
                lax.dot_general(
                    part(r, h), part(r, 2 + h), (((1,), (1,)), ((), ())), preferred_element_type=F32
                ) * LOG_SCALE
                for r, h in spots
            ]
            tops = [jnp.max(s, axis=1, keepdims=True) for s in scores]
            probs = [jnp.exp2(s - m) for s, m in zip(scores, tops)]
            sums = [jnp.sum(p, axis=1, keepdims=True) for p in probs]
            atts = [
                (jnp.dot(p.astype(BF), part(r, 4 + h), preferred_element_type=F32) * (1.0 / total_p)).astype(BF)
                for (r, h), p, total_p in zip(spots, probs, sums)
            ]
            side = lax.rem(pair + core, 2)
            for i in range(2):
                att = jnp.concatenate(atts[2 * i:2 * i + 2], axis=1)
                for half in range(2):
                    k = lax.rem(2 * i + half - my_y + NY, NY)
                    out_ref[side, pl.ds(pl.multiple_of(k * 64, 64), 64), :] = att[half * 64:(half + 1) * 64]


def encode(corpus_flat, w_rows, gain, at):
    tokens, width = corpus_flat.shape
    steps = 4
    depth = width // steps
    return pl.pallas_call(
        encoder_kernel,
        grid_spec=pltpu.PrefetchScalarGridSpec(
            num_scalar_prefetch=1,
            grid=(steps,),
            in_specs=[
                pl.BlockSpec((tokens, depth), lambda i, c: (0, i)),
                pl.BlockSpec((depth * 6, HS), lambda i, c: (i, 0)),
                pl.BlockSpec((1, depth), lambda i, c: (0, i)),
            ],
            out_specs=pl.BlockSpec((2, 2 * ROW, 2 * HS), lambda i, c: (0, 0, 0)),
            scratch_shapes=[
                pltpu.VMEM((depth * 6, HS), F32),
                pltpu.VMEM((depth, 6 * HS), BF),
                pltpu.VMEM((tokens, 6 * HS), F32),
                pltpu.VMEM((tokens, 1), F32),
            ],
        ),
        out_shape=jax.ShapeDtypeStruct((2, 2 * ROW, 2 * HS), BF),
        cost_estimate=pl.CostEstimate(
            flops=2 * tokens * width * 6 * HS, bytes_accessed=(tokens + 768) * width * 2, transcendentals=0
        ),
        compiler_params=pltpu.CompilerParams(vmem_limit_bytes=60 * MIB),
        name="encoder",
    )(at, corpus_flat, w_rows, gain)


def project_kernel(a_ref, b_ref, ea_ref, eb_ref, *outs):
    rows = a_ref.shape[1] // NY
    value = jnp.dot(a_ref[0], ea_ref[...], preferred_element_type=F32)
    value += jnp.dot(b_ref[...], eb_ref[...], preferred_element_type=F32)
    for k in range(NY):
        outs[k][...] = value[k * rows:(k + 1) * rows].astype(BF)


def project(att, att_other, e_own, e_other):
    tokens, depth = att_other.shape
    width = e_own.shape[1]
    cols = 1024
    rows = tokens // NY
    return pl.pallas_call(
        project_kernel,
        grid=(width // cols,),
        in_specs=[
            pl.BlockSpec((1, tokens, depth), lambda i: (0, 0, 0)),
            pl.BlockSpec((tokens, depth), lambda i: (0, 0)),
            pl.BlockSpec((depth, cols), lambda i: (0, i)),
            pl.BlockSpec((depth, cols), lambda i: (0, i)),
        ],
        out_specs=[pl.BlockSpec((rows, cols), lambda i: (0, i))] * NY,
        out_shape=[jax.ShapeDtypeStruct((rows, width), BF)] * NY,
        cost_estimate=pl.CostEstimate(
            flops=4 * tokens * depth * width, bytes_accessed=4 * depth * width, transcendentals=0
        ),
        compiler_params=pltpu.CompilerParams(vmem_limit_bytes=12 * MIB),
        name="project",
    )(att, att_other, e_own, e_other)


def norm_kernel(block_ref, t0, t1, t2, t3, x_ref, g_ref, out_ref):
    total = x_ref[...].astype(F32)
    for term in (t0, t1, t2, t3):
        total += term[...].astype(F32)
    rinv = lax.rsqrt(jnp.mean(total * total, axis=1, keepdims=True) + EPS)
    u = (total * rinv * g_ref[...]).astype(BF)
    for z in range(NZ):
        for x in range(NX):
            src, dst = (z * NX + x) * HS, (x * NZ + z) * HS
            out_ref[:, dst:dst + HS] = u[:, src:src + HS]


def normalise(terms, corpus_flat, gain, block):
    rows, width = terms[0].shape
    whole = pl.BlockSpec((rows, width), lambda i, b: (0, 0))
    return pl.pallas_call(
        norm_kernel,
        grid_spec=pltpu.PrefetchScalarGridSpec(
            num_scalar_prefetch=1,
            grid=(1,),
            in_specs=[whole] * NY
            + [
                pl.BlockSpec((rows, width), lambda i, b: (b[0], 0)),
                pl.BlockSpec((1, width), lambda i, b: (0, 0)),
            ],
            out_specs=whole,
        ),
        out_shape=jax.ShapeDtypeStruct((rows, width), BF),
        cost_estimate=pl.CostEstimate(flops=8 * rows * width, bytes_accessed=12 * rows * width, transcendentals=0),
        compiler_params=pltpu.CompilerParams(vmem_limit_bytes=60 * MIB),
        name="normalise",
    )(block, *terms, corpus_flat, gain)


ORDER = (0, NX - 1, 1, 2)


def memory_kernel(parts, at_ref, *refs):
    us = refs[:parts]
    k0, k1, k2, k3, k4 = refs[parts:parts + 5]
    out_ref = refs[parts + 5]
    rest = refs[parts + 6:]
    if parts > 1:
        whole, rest = rest[0], rest[1:]
    ua, kv, sem, out_sem = rest
    depth = NZ * HS
    rows = ua.shape[0] // parts
    u_copies = []
    for k in range(parts):
        first = pl.multiple_of(lax.rem(at_ref[1] - k + parts, parts) * rows, rows)
        u_copies.append(pltpu.make_async_copy(us[k], ua.at[pl.ds(first, rows)], sem.at[k]))
    near = [
        pltpu.make_async_copy(k_ref.at[pl.ds(0, depth)], kv.at[i], sem.at[NY + i])
        for i, k_ref in enumerate((k0, k1, k2))
    ]
    top, bottom = k3.shape[0], depth - k3.shape[0]
    far = [
        pltpu.make_async_copy(k3, kv.at[3, pl.ds(0, top)], sem.at[NY + 3]),
        pltpu.make_async_copy(k4.at[pl.ds(0, bottom)], kv.at[3, pl.ds(top, bottom)], sem.at[NY + 4]),
    ]
    for copy in u_copies + near + far:
        copy.start()
    for copy in u_copies:
        copy.wait()
    if parts > 1:
        back = pltpu.make_async_copy(ua, whole, out_sem)
        back.start()
    total = jnp.zeros(out_ref.shape, F32)
    for i in range(NX):
        for copy in (near[i:i + 1] if i < 3 else far):
            copy.wait()
        first = pl.multiple_of(lax.rem(at_ref[0] + ORDER[i], NX) * depth, depth)
        total += jnp.dot(ua[:, pl.ds(first, depth)], kv[i], preferred_element_type=F32)
    out_ref[...] = total.astype(BF)
    if parts > 1:
        back.wait()


def memorise(at, us, payloads):
    width = us[0].shape[1]
    tokens = us[0].shape[0] * len(us)
    cols = payloads[0].shape[1]
    depth = width // NX
    memory = jax.ShapeDtypeStruct((tokens, cols), BF)
    assembled = [jax.ShapeDtypeStruct((tokens, width), BF)] if len(us) > 1 else []
    return pl.pallas_call(
        functools.partial(memory_kernel, len(us)),
        in_specs=[pl.BlockSpec(memory_space=pltpu.SMEM)] + [ANY] * (len(us) + 5),
        out_specs=[VMEM_ALL] + [ANY] * len(assembled),
        scratch_shapes=[
            pltpu.VMEM((tokens, width), BF),
            pltpu.VMEM((NX, depth, cols), BF),
            pltpu.SemaphoreType.DMA((NY + 5,)),
            pltpu.SemaphoreType.DMA,
        ],
        out_shape=[memory] + assembled,
        cost_estimate=pl.CostEstimate(
            flops=2 * tokens * width * cols, bytes_accessed=2 * width * cols, transcendentals=0
        ),
        compiler_params=pltpu.CompilerParams(vmem_limit_bytes=12 * MIB),
        name="memorise",
    )(at, *us, *payloads)


def ring_pieces(block, base):
    rows = block.shape[0]
    half = rows // 2
    pieces = [(0, base, rows, block)]
    up = down = block
    for s in range(1, NZ // 2):
        up = shifted(up, "z", 1)
        down = shifted(down, "z", -1)
        pieces += [(s, base, rows, up), (NZ - s, base, rows, down)]
    pieces += [
        (NZ // 2, base, half, shifted(up[:half], "z", 1)),
        (NZ // 2, base + half, half, shifted(down[half:], "z", -1)),
    ]
    return pieces


PAD = 8
Q_FIRST = NZ * HS
PAYLOAD_TOP = 640


def window_kernel(layout, ids_ref, at_ref, *refs):
    payloads = refs[:NX]
    pieces = refs[NX:NX + len(layout)]
    out_ref = refs[NX + len(layout)]
    table, q_in, qs, outs, stats, one_list, two_list, sem, q_sem = refs[NX + len(layout) + 1:]
    q_first = (Q_FIRST, Q_FIRST, Q_FIRST, Q_FIRST - PAYLOAD_TOP)
    my_z, my_x, core = at_ref[0], at_ref[1], at_ref[2]
    count_all = NX * 8 + 1
    plane_rows = NX * 1024
    total_rows = qs.shape[0]
    q_copies = [
        pltpu.make_async_copy(payloads[i].at[pl.ds(q_first[i], 256)], q_in.at[i], q_sem.at[i]) for i in range(NX)
    ]
    copies = [
        pltpu.make_async_copy(pieces[i], table.at[pl.ds(distance * 512 + first, rows)], sem.at[i])
        for i, (distance, first, rows) in enumerate(layout)
    ]
    for copy in q_copies + copies:
        copy.start()
    outs[...] = jnp.zeros_like(outs)
    stats[...] = jnp.full_like(stats, MASKED)
    qs[0:PAD, :] = jnp.zeros((PAD, HS), F32)
    qs[PAD + plane_rows:, :] = jnp.zeros((total_rows - PAD - plane_rows, HS), F32)
    for i in range(NX):
        base = PAD + lax.rem(my_x + ORDER[i], NX) * 1024
        q_copies[i].wait()
        for b in range(4):
            first = pl.multiple_of(base + b * 256, 8)
            qs[pl.ds(first, 256), :] = q_in[i, :, b * HS:(b + 1) * HS].astype(F32)
    def held(row):
        return jnp.logical_and(row >= 0, jnp.bitwise_and(jnp.right_shift(row, 2), NX - 1) == my_x)

    def wanted(w, n):
        group = jnp.maximum(w - 1, 0)
        step = jnp.bitwise_and(jnp.right_shift(group, 3) - my_x, NX - 1)
        return ids_ref[step * 18 + jnp.where(w == 0, 0, jnp.bitwise_and(group, 7) + 1) * 2 + n]

    def place(row):
        distance = jnp.bitwise_and(my_z - jnp.right_shift(row, 4), NZ - 1)
        local = jnp.bitwise_and(row, 3)
        half = jnp.bitwise_and(jnp.right_shift(local, 1) + core, 1)
        return distance * 512 + half * 256 + jnp.bitwise_and(local, 1) * 128

    def note(w, counts):
        ones, twos = counts
        rows = [wanted(w, n) for n in range(2)]
        ok = [held(row).astype(jnp.int32) for row in rows]
        single, both = ok[0] + ok[1] == 1, ok[0] + ok[1] == 2
        spot = place(jnp.where(ok[0] == 1, rows[0], rows[1]))
        one_list[2 * ones] = w
        one_list[2 * ones + 1] = spot
        two_list[3 * twos] = w
        two_list[3 * twos + 1] = spot
        two_list[3 * twos + 2] = place(jnp.maximum(rows[1], 0))
        return ones + single.astype(jnp.int32), twos + both.astype(jnp.int32)

    ones, twos = lax.fori_loop(0, count_all, note, (0, 0))
    for copy in copies:
        copy.wait()

    def attend(items):
        jobs = []
        for start, spots in items:
            for h in range(2):
                q = qs[pl.ds(start + h, GROUP, stride=2), :].astype(BF)
                k = [table[pl.ds(pl.multiple_of(f, ROW), ROW), h * 256:h * 256 + HS] for f in spots]
                k = k[0] if len(k) == 1 else jnp.concatenate(k, axis=0)
                s = lax.dot_general(q, k, (((1,), (1,)), ((), ())), preferred_element_type=F32)
                jobs.append([start + h, h, spots, s])
        for job in jobs:
            job[3] = job[3] * LOG_SCALE
            job.append(jnp.max(job[3], axis=1, keepdims=True))
        for job in jobs:
            job[3] = jnp.exp2(job[3] - job[4])
            job.append(jnp.sum(job[3], axis=1, keepdims=True))
        for first, h, spots, p, m, total in jobs:
            v = [table[pl.ds(pl.multiple_of(f, ROW), ROW), h * 256 + HS:h * 256 + 2 * HS] for f in spots]
            v = v[0] if len(v) == 1 else jnp.concatenate(v, axis=0)
            out = jnp.dot(p.astype(BF), v, preferred_element_type=F32) * (1.0 / total)
            outs[pl.ds(first, GROUP, stride=2), :] = out
            stats[pl.ds(first, GROUP, stride=2), :] = jnp.broadcast_to(m + jnp.log2(total), (GROUP, HS))

    def query_row(w):
        return PAD + 2 * (GROUP * w - 1)

    def one_pair(i, carry):
        items = []
        for lane in range(2):
            at = jnp.minimum(2 * i + lane, ones - 1)
            items.append((query_row(one_list[2 * at]), [one_list[2 * at + 1]]))
        attend(items)
        return carry

    def two(i, carry):
        attend([(query_row(two_list[3 * i]), [two_list[3 * i + 1], two_list[3 * i + 2]])])
        return carry

    lax.fori_loop(0, (ones + 1) // 2, one_pair, 0)
    lax.fori_loop(0, twos, two, 0)
    eye = lax.broadcasted_iota(jnp.int32, (HS, HS), 0) == lax.broadcasted_iota(jnp.int32, (HS, HS), 1)
    for x in range(NX):
        base = PAD + x * 1024
        out_ref[x, 0:1024] = outs[base:base + 1024, :].astype(BF)
        lines = []
        for b in range(8):
            block = stats[base + b * HS:base + (b + 1) * HS, :]
            lines.append(jnp.sum(jnp.where(eye, block, 0.0), axis=0, keepdims=True))
        lse = jnp.concatenate(lines, axis=0)
        high = lse.astype(BF)
        rest = lse - high.astype(F32)
        middle = rest.astype(BF)
        low = (rest - middle.astype(F32)).astype(BF)
        tail = jnp.concatenate([high.astype(F32), middle.astype(F32), low.astype(F32), jnp.zeros((8, HS), F32)], axis=0)
        out_ref[x, 1024:1056] = tail.astype(BF)


def windows(ids, at, payloads, pieces):
    layout = tuple((d, first, rows) for d, first, rows, _ in pieces)
    total = PAD + NX * 1024 + 2 * GROUP
    smem = pl.BlockSpec(memory_space=pltpu.SMEM)
    return pl.pallas_call(
        functools.partial(window_kernel, layout),
        in_specs=[smem, smem] + [ANY] * (NX + len(pieces)),
        out_specs=VMEM_ALL,
        scratch_shapes=[
            pltpu.VMEM((NZ * 4 * ROW, 512), BF),
            pltpu.VMEM((NX, 256, 512), BF),
            pltpu.VMEM((total, HS), F32),
            pltpu.VMEM((total, HS), F32),
            pltpu.VMEM((total, HS), F32),
            pltpu.SMEM((128,), jnp.int32),
            pltpu.SMEM((128,), jnp.int32),
            pltpu.SemaphoreType.DMA((len(pieces),)),
            pltpu.SemaphoreType.DMA((NX,)),
        ],
        out_shape=jax.ShapeDtypeStruct((NX, 1056, HS), BF),
        cost_estimate=pl.CostEstimate(flops=10**9, bytes_accessed=8 * 2**20, transcendentals=10**6),
        compiler_params=pltpu.CompilerParams(vmem_limit_bytes=58 * MIB),
        name="windows",
    )(ids, at, *payloads, *[piece[-1] for piece in pieces])


def combine_kernel(parts_ref, out_ref):
    logs = []
    for x in range(NX):
        tail = parts_ref[x, 1024:1056].astype(F32)
        logs.append(tail[0:8] + tail[8:16] + tail[16:24])
    m = functools.reduce(jnp.maximum, logs)
    weights = [jnp.exp2(v - m) for v in logs]
    inv = 1.0 / functools.reduce(jnp.add, weights)
    weights = [w * inv for w in weights]
    eye = lax.broadcasted_iota(jnp.int32, (HS, HS), 0) == lax.broadcasted_iota(jnp.int32, (HS, HS), 1)
    for b in range(8):
        total = jnp.zeros((HS, HS), F32)
        for x in range(NX):
            line = jnp.broadcast_to(weights[x][b:b + 1, :], (HS, HS))
            column = jnp.sum(jnp.where(eye, line, 0.0), axis=1, keepdims=True)
            total += column * parts_ref[x, b * HS:(b + 1) * HS].astype(F32)
        out_ref[b * HS:(b + 1) * HS, :] = total.astype(BF)


def combine(parts):
    return pl.pallas_call(
        combine_kernel,
        in_specs=[VMEM_ALL],
        out_specs=VMEM_ALL,
        out_shape=jax.ShapeDtypeStruct((1024, HS), BF),
        cost_estimate=pl.CostEstimate(flops=10**7, bytes_accessed=2 * 2**20, transcendentals=0),
        compiler_params=pltpu.CompilerParams(vmem_limit_bytes=8 * MIB),
        name="combine",
    )(parts)


def as_index(*values):
    return jnp.stack(values).astype(jnp.int32)


def on_device(corpus, enc_qkv, enc_out, cca_kv, gain_in, gain_out, queries, nbr_ids):
    width = corpus.shape[2]
    my_z, my_x, my_y, core = (lax.axis_index(a) for a in ("z", "x", "y", "c"))
    corpus_flat = corpus.reshape(-1, width)
    e_own = enc_out.reshape(2 * HS, width)
    e_other = shifted(e_own, "c", 1)

    kv = lax.optimization_barrier(cca_kv.reshape(cca_kv.shape[0], 512))
    kv = spread(kv, "z").reshape(-1, 512)

    w_rows = enc_qkv.transpose(0, 2, 1, 3).reshape(width * 6, HS)
    att = encode(corpus_flat, w_rows, gain_in.reshape(1, width), as_index(core, my_y))
    nbr_ids, queries, att = lax.optimization_barrier((nbr_ids, queries, att))
    att_other = shifted(att[1], "c", 1)

    last = lax.ppermute(nbr_ids[7:], ("z", "x"), [(i, i + 1) for i in range(NZ * NX - 1)])
    last = jnp.where(jnp.logical_and(my_z == 0, my_x == 0), -1, last)
    ids = jnp.concatenate([last, nbr_ids], axis=0).astype(BF)
    terms = project(att, att_other, e_own, e_other)

    terms = [terms[0]] + [shifted(terms[k], "y", k) for k in range(1, NY)]
    kv, terms[1], terms[3] = lax.optimization_barrier((kv, terms[1], terms[3]))
    q_rows = queries.reshape(4, 256, HS)
    q_wide = jnp.concatenate([q_rows[b] for b in range(4)], axis=1)
    payload = jnp.concatenate([kv, q_wide, jnp.pad(ids, ((0, 7), (0, 510)))], axis=0)
    from_left = shifted(payload, "x", 1)
    from_right = shifted(payload, "x", -1)

    u = normalise(terms, corpus_flat, gain_out.reshape(1, width), as_index(core * NY + my_y))
    us = [u] + [shifted(u, "y", k) for k in range(1, NY)]
    us[1], us[3], from_left, from_right = lax.optimization_barrier((us[1], us[3], from_left, from_right))
    far_top = shifted(from_left[:PAYLOAD_TOP], "x", 1)
    far_bottom = shifted(from_right[PAYLOAD_TOP:], "x", -1)
    payloads = [payload, from_left, from_right, far_top, far_bottom]
    at = as_index(my_x, my_y)
    memory_own, u_own = memorise(at, us, payloads)
    u_other = shifted(u_own, "c", 1)
    pieces = ring_pieces(memory_own, 0)
    (memory_other,) = memorise(at, [u_other], payloads)
    pieces += ring_pieces(memory_other, 2 * ROW)

    ids_first = Q_FIRST + 256
    near = [p[ids_first:ids_first + 9, 0:2] for p in payloads[:3]]
    far = far_bottom[ids_first - PAYLOAD_TOP:ids_first - PAYLOAD_TOP + 9, 0:2]
    got = jnp.stack([near[0], near[2], far, near[1]]).astype(jnp.int32)
    got, at = lax.optimization_barrier((got.reshape(-1), as_index(my_z, my_x, core)))
    payloads = payloads[:3] + [far_bottom]
    parts = windows(got, at, payloads, pieces)
    parts = lax.all_to_all(parts, "x", split_axis=0, concat_axis=0, tiled=True)
    return combine(parts).reshape(512, 2, HS)


def solution(mesh):
    inner = Mesh(mesh.devices.reshape(NZ, NX, NY, NC), ("z", "x", "y", "c"))
    seq, head = ("z", "x"), ("y", "c")
    placed = (
        P(seq, None, None),
        P(None, head, None, None),
        P(head, None, None),
        P(seq, head, None, None),
        P(),
        P(),
        P(seq, head, None),
        P(seq, None),
    )
    return jax.shard_map(
        on_device, mesh=inner, in_specs=placed, out_specs=P(seq, head, None), check_vma=False
    )
```

```python
import functools

import jax
import jax.numpy as jnp
from jax import lax
from jax.experimental import pallas as pl
from jax.experimental.pallas import tpu as pltpu
from jax.sharding import Mesh, PartitionSpec as P

GROUP = 64
EPS = 1e-06
MIB = 2**20
NZ, NX, NY, NC = 8, 4, 4, 2
ROW = 128
HS = 128
MASKED = -1e30
LOG_SCALE = HS ** -0.5 * 1.4426950408889634
BF = jnp.bfloat16
F32 = jnp.float32
ANY = pl.BlockSpec(memory_space=pl.ANY)
VMEM_ALL = pl.BlockSpec(memory_space=pltpu.VMEM)


def shifted(value, axis, steps):
    n = lax.axis_size(axis)
    return lax.ppermute(value, axis, [(i, (i + steps) % n) for i in range(n)])


def spread(value, axis):
    n = lax.axis_size(axis)
    copies = jnp.broadcast_to(value[None], (n,) + value.shape)
    return lax.all_to_all(copies, axis, split_axis=0, concat_axis=0, tiled=True)


def encoder_kernel(core_ref, y_ref, x_ref, w_ref, g_ref, own_ref, send_ref, wide, wmat, acc, ssq):
    step = pl.program_id(0)
    depth = x_ref.shape[1]

    @pl.when(step == 0)
    def _():
        acc[...] = jnp.zeros_like(acc)
        ssq[...] = jnp.zeros_like(ssq)

    wide[...] = w_ref[...].astype(F32)
    for col in range(6):
        wmat[:, col * HS:(col + 1) * HS] = wide[pl.ds(col, depth, stride=6), :].astype(BF)
    x = x_ref[...].astype(F32)
    ssq[...] += jnp.sum(x * x, axis=1, keepdims=True)
    xg = (x * g_ref[...]).astype(BF)
    acc[...] += jnp.dot(xg, wmat[...], preferred_element_type=F32)

    @pl.when(step == pl.num_programs(0) - 1)
    def _():
        core, my_y = core_ref[0], y_ref[0]
        done = []
        total = depth * pl.num_programs(0)
        scale = lax.rsqrt(ssq[...] / total + EPS)
        rows = x_ref.shape[0] // ROW
        for pair in range(rows // 2):
            spots = [(r, h) for r in (2 * pair, 2 * pair + 1) for h in range(2)]

            def part(r, col):
                sl = slice(r * ROW, (r + 1) * ROW)
                return (acc[sl, col * HS:(col + 1) * HS] * scale[sl]).astype(BF)

            scores = [
                lax.dot_general(
                    part(r, h), part(r, 2 + h), (((1,), (1,)), ((), ())), preferred_element_type=F32
                ) * LOG_SCALE
                for r, h in spots
            ]
            tops = [jnp.max(s, axis=1, keepdims=True) for s in scores]
            probs = [jnp.exp2(s - m) for s, m in zip(scores, tops)]
            sums = [jnp.sum(p, axis=1, keepdims=True) for p in probs]
            atts = [
                (jnp.dot(p.astype(BF), part(r, 4 + h), preferred_element_type=F32) * (1.0 / total_p)).astype(BF)
                for (r, h), p, total_p in zip(spots, probs, sums)
            ]
            done.append([jnp.concatenate(atts[2 * i:2 * i + 2], axis=1) for i in range(2)])
        for i in range(2):
            own = jnp.where(core == 0, done[0][i], done[1][i])
            send = jnp.where(core == 0, done[1][i], done[0][i])
            for half in range(2):
                k = jnp.bitwise_and(2 * i + half - my_y, NY - 1)
                spot = pl.ds(pl.multiple_of(k * 64, 64), 64)
                own_ref[spot, :] = own[half * 64:(half + 1) * 64]
                send_ref[spot, :] = send[half * 64:(half + 1) * 64]


def encode(corpus_flat, w_rows, gain, core, my_y):
    tokens, width = corpus_flat.shape
    steps = 4
    depth = width // steps
    return pl.pallas_call(
        encoder_kernel,
        grid_spec=pltpu.PrefetchScalarGridSpec(
            num_scalar_prefetch=2,
            grid=(steps,),
            in_specs=[
                pl.BlockSpec((tokens, depth), lambda i, c, y: (0, i)),
                pl.BlockSpec((depth * 6, HS), lambda i, c, y: (i, 0)),
                pl.BlockSpec((1, depth), lambda i, c, y: (0, i)),
            ],
            out_specs=[pl.BlockSpec((2 * ROW, 2 * HS), lambda i, c, y: (0, 0))] * 2,
            scratch_shapes=[
                pltpu.VMEM((depth * 6, HS), F32),
                pltpu.VMEM((depth, 6 * HS), BF),
                pltpu.VMEM((tokens, 6 * HS), F32),
                pltpu.VMEM((tokens, 1), F32),
            ],
        ),
        out_shape=[jax.ShapeDtypeStruct((2 * ROW, 2 * HS), BF)] * 2,
        cost_estimate=pl.CostEstimate(
            flops=2 * tokens * width * 6 * HS, bytes_accessed=(tokens + 768) * width * 2, transcendentals=0
        ),
        compiler_params=pltpu.CompilerParams(vmem_limit_bytes=60 * MIB),
        name="encoder",
    )(core, my_y, corpus_flat, w_rows, gain)


def project_kernel(a_ref, b_ref, ea_ref, eb_ref, *outs):
    rows = a_ref.shape[0] // NY
    value = jnp.dot(a_ref[...], ea_ref[...], preferred_element_type=F32)
    value += jnp.dot(b_ref[...], eb_ref[...], preferred_element_type=F32)
    for k in range(NY):
        outs[k][...] = value[k * rows:(k + 1) * rows].astype(BF)


def project(att, att_other, e_own, e_other):
    tokens, depth = att_other.shape
    width = e_own.shape[1]
    cols = 1024
    rows = tokens // NY
    return pl.pallas_call(
        project_kernel,
        grid=(width // cols,),
        in_specs=[
            pl.BlockSpec((tokens, depth), lambda i: (0, 0)),
            pl.BlockSpec((tokens, depth), lambda i: (0, 0)),
            pl.BlockSpec((depth, cols), lambda i: (0, i)),
            pl.BlockSpec((depth, cols), lambda i: (0, i)),
        ],
        out_specs=[pl.BlockSpec((rows, cols), lambda i: (0, i))] * NY,
        out_shape=[jax.ShapeDtypeStruct((rows, width), BF)] * NY,
        cost_estimate=pl.CostEstimate(
            flops=4 * tokens * depth * width, bytes_accessed=4 * depth * width, transcendentals=0
        ),
        compiler_params=pltpu.CompilerParams(vmem_limit_bytes=60 * MIB),
        name="project",
    )(att, att_other, e_own, e_other)


def norm_kernel(block_ref, t0, t1, t2, t3, x_ref, g_ref, out_ref):
    total = x_ref[...].astype(F32)
    for term in (t0, t1, t2, t3):
        total += term[...].astype(F32)
    rinv = lax.rsqrt(jnp.mean(total * total, axis=1, keepdims=True) + EPS)
    u = (total * rinv * g_ref[...]).astype(BF)
    for z in range(NZ):
        for x in range(NX):
            src, dst = (z * NX + x) * HS, (x * NZ + z) * HS
            out_ref[:, dst:dst + HS] = u[:, src:src + HS]


def normalise(terms, corpus_flat, gain, block):
    rows, width = terms[0].shape
    whole = pl.BlockSpec((rows, width), lambda i, b: (0, 0))
    return pl.pallas_call(
        norm_kernel,
        grid_spec=pltpu.PrefetchScalarGridSpec(
            num_scalar_prefetch=1,
            grid=(1,),
            in_specs=[whole] * NY
            + [
                pl.BlockSpec((rows, width), lambda i, b: (b[0], 0)),
                pl.BlockSpec((1, width), lambda i, b: (0, 0)),
            ],
            out_specs=whole,
        ),
        out_shape=jax.ShapeDtypeStruct((rows, width), BF),
        cost_estimate=pl.CostEstimate(flops=8 * rows * width, bytes_accessed=12 * rows * width, transcendentals=0),
        compiler_params=pltpu.CompilerParams(vmem_limit_bytes=60 * MIB),
        name="normalise",
    )(block, *terms, corpus_flat, gain)


ORDER = (0, NX - 1, 1, 2)


def memory_kernel(parts, at_ref, *refs):
    us = refs[:parts]
    k0, k1, k2, k3, k4 = refs[parts:parts + 5]
    out_ref = refs[parts + 5]
    rest = refs[parts + 6:]
    if parts > 1:
        whole, rest = rest[0], rest[1:]
    ua, kv, sem, out_sem = rest
    depth = NZ * HS
    rows = ua.shape[0] // parts
    u_copies = []
    for k in range(parts):
        first = pl.multiple_of(lax.rem(at_ref[1] - k + parts, parts) * rows, rows)
        u_copies.append(pltpu.make_async_copy(us[k], ua.at[pl.ds(first, rows)], sem.at[k]))
    near = [
        pltpu.make_async_copy(k_ref.at[pl.ds(0, depth)], kv.at[i], sem.at[NY + i])
        for i, k_ref in enumerate((k0, k1, k2))
    ]
    top, bottom = k3.shape[0], depth - k3.shape[0]
    far = [
        pltpu.make_async_copy(k3, kv.at[3, pl.ds(0, top)], sem.at[NY + 3]),
        pltpu.make_async_copy(k4.at[pl.ds(0, bottom)], kv.at[3, pl.ds(top, bottom)], sem.at[NY + 4]),
    ]
    for copy in u_copies + near + far:
        copy.start()
    for copy in u_copies:
        copy.wait()
    if parts > 1:
        back = pltpu.make_async_copy(ua, whole, out_sem)
        back.start()
    total = jnp.zeros(out_ref.shape, F32)
    for i in range(NX):
        for copy in (near[i:i + 1] if i < 3 else far):
            copy.wait()
        first = pl.multiple_of(lax.rem(at_ref[0] + ORDER[i], NX) * depth, depth)
        total += jnp.dot(ua[:, pl.ds(first, depth)], kv[i], preferred_element_type=F32)
    out_ref[...] = total.astype(BF)
    if parts > 1:
        back.wait()


def memorise(at, us, payloads):
    width = us[0].shape[1]
    tokens = us[0].shape[0] * len(us)
    cols = payloads[0].shape[1]
    depth = width // NX
    memory = jax.ShapeDtypeStruct((tokens, cols), BF)
    assembled = [jax.ShapeDtypeStruct((tokens, width), BF)] if len(us) > 1 else []
    return pl.pallas_call(
        functools.partial(memory_kernel, len(us)),
        in_specs=[pl.BlockSpec(memory_space=pltpu.SMEM)] + [ANY] * (len(us) + 5),
        out_specs=[VMEM_ALL] + [ANY] * len(assembled),
        scratch_shapes=[
            pltpu.VMEM((tokens, width), BF),
            pltpu.VMEM((NX, depth, cols), BF),
            pltpu.SemaphoreType.DMA((NY + 5,)),
            pltpu.SemaphoreType.DMA,
        ],
        out_shape=[memory] + assembled,
        cost_estimate=pl.CostEstimate(
            flops=2 * tokens * width * cols, bytes_accessed=2 * width * cols, transcendentals=0
        ),
        compiler_params=pltpu.CompilerParams(vmem_limit_bytes=12 * MIB),
        name="memorise",
    )(at, *us, *payloads)


def ring_pieces(block, base):
    rows = block.shape[0]
    half = rows // 2
    pieces = [(0, base, rows, block)]
    up = down = block
    for s in range(1, NZ // 2):
        up = shifted(up, "z", 1)
        down = shifted(down, "z", -1)
        pieces += [(s, base, rows, up), (NZ - s, base, rows, down)]
    pieces += [
        (NZ // 2, base, half, shifted(up[:half], "z", 1)),
        (NZ // 2, base + half, half, shifted(down[half:], "z", -1)),
    ]
    return pieces


PAD = 8


def plan_kernel(ids_ref, z_ref, x_ref, core_ref, one_list, two_list, counts_ref):
    my_z, my_x, core = z_ref[0], x_ref[0], core_ref[0]

    def held(row):
        return jnp.logical_and(row >= 0, jnp.bitwise_and(jnp.right_shift(row, 2), NX - 1) == my_x)

    def wanted(w, n):
        group = jnp.maximum(w - 1, 0)
        step = jnp.bitwise_and(jnp.right_shift(group, 3) - my_x, NX - 1)
        here = step * 16 + jnp.bitwise_and(group, 7) * 2
        under = NX * 16 + jnp.bitwise_and(NX - 1 - my_x, NX - 1) * 16 + 14
        row = ids_ref[jnp.where(w == 0, under, here) + n]
        return jnp.where(jnp.logical_and(w == 0, my_z == 0), -1, row)

    def place(row):
        distance = jnp.bitwise_and(my_z - jnp.right_shift(row, 4), NZ - 1)
        local = jnp.bitwise_and(row, 3)
        half = jnp.bitwise_and(jnp.right_shift(local, 1) + core, 1)
        return distance * 512 + half * 256 + jnp.bitwise_and(local, 1) * 128

    def note(w, counts):
        ones, twos = counts
        rows = [wanted(w, n) for n in range(2)]
        ok = [held(row).astype(jnp.int32) for row in rows]
        single, both = ok[0] + ok[1] == 1, ok[0] + ok[1] == 2
        spot = place(jnp.maximum(jnp.where(ok[0] == 1, rows[0], rows[1]), 0))
        one_list[2 * ones] = w
        one_list[2 * ones + 1] = spot
        two_list[3 * twos] = w
        two_list[3 * twos + 1] = spot
        two_list[3 * twos + 2] = place(jnp.maximum(rows[1], 0))
        return ones + single.astype(jnp.int32), twos + both.astype(jnp.int32)

    ones, twos = lax.fori_loop(0, NX * 8 + 1, note, (0, 0))
    counts_ref[0] = ones
    counts_ref[1] = twos


def plan(ids, my_z, my_x, core):
    smem = pl.BlockSpec(memory_space=pltpu.SMEM)
    return pl.pallas_call(
        plan_kernel,
        in_specs=[smem] * 4,
        out_specs=[smem] * 3,
        out_shape=[
            jax.ShapeDtypeStruct((128,), jnp.int32),
            jax.ShapeDtypeStruct((128,), jnp.int32),
            jax.ShapeDtypeStruct((2,), jnp.int32),
        ],
        name="plan",
    )(ids, my_z, my_x, core)


def window_kernel(layout, one_list, two_list, counts_ref, x_ref, *refs):
    q_refs, refs = refs[:NX], refs[NX:]
    pieces = refs[:len(layout)]
    out_ref = refs[len(layout)]
    table, q_in, qs, outs, stats, sem, q_sem = refs[len(layout) + 1:]
    ones, twos = counts_ref[0], counts_ref[1]
    plane_rows = NX * 1024
    total_rows = qs.shape[0]
    q_copies = [pltpu.make_async_copy(q_refs[d].at[pl.ds(0, 1024)], q_in.at[d], q_sem.at[d]) for d in range(NX)]
    copies = [
        pltpu.make_async_copy(pieces[i], table.at[pl.ds(distance * 512 + first, rows)], sem.at[i])
        for i, (distance, first, rows) in enumerate(layout)
    ]
    for copy in q_copies + copies:
        copy.start()
    outs[...] = jnp.zeros_like(outs)
    stats[...] = jnp.full_like(stats, MASKED)
    qs[0:PAD, :] = jnp.zeros((PAD, HS), F32)
    qs[PAD + plane_rows:, :] = jnp.zeros((total_rows - PAD - plane_rows, HS), F32)
    for d in range(NX):
        q_copies[d].wait()
        first = pl.multiple_of(PAD + jnp.bitwise_and(x_ref[0] + d, NX - 1) * 1024, 8)
        qs[pl.ds(first, 1024), :] = q_in[d].astype(F32)
    for copy in copies:
        copy.wait()

    def attend(items):
        jobs = []
        for start, spots in items:
            for h in range(2):
                q = qs[pl.ds(start + h, GROUP, stride=2), :].astype(BF)
                k = [table[pl.ds(pl.multiple_of(f, ROW), ROW), h * 256:h * 256 + HS] for f in spots]
                k = k[0] if len(k) == 1 else jnp.concatenate(k, axis=0)
                s = lax.dot_general(q, k, (((1,), (1,)), ((), ())), preferred_element_type=F32)
                jobs.append([start + h, h, spots, s])
        for job in jobs:
            job[3] = job[3] * LOG_SCALE
            job.append(jnp.max(job[3], axis=1, keepdims=True))
        for job in jobs:
            job[3] = jnp.exp2(job[3] - job[4])
            job.append(jnp.sum(job[3], axis=1, keepdims=True))
        for first, h, spots, p, m, total in jobs:
            v = [table[pl.ds(pl.multiple_of(f, ROW), ROW), h * 256 + HS:h * 256 + 2 * HS] for f in spots]
            v = v[0] if len(v) == 1 else jnp.concatenate(v, axis=0)
            out = jnp.dot(p.astype(BF), v, preferred_element_type=F32) * (1.0 / total)
            outs[pl.ds(first, GROUP, stride=2), :] = out
            stats[pl.ds(first, GROUP, stride=2), :] = jnp.broadcast_to(m + jnp.log2(total), (GROUP, HS))

    def query_row(w):
        return PAD + 2 * (GROUP * w - 1)

    def one_pair(i, carry):
        items = []
        for lane in range(2):
            at = jnp.minimum(2 * i + lane, ones - 1)
            items.append((query_row(one_list[2 * at]), [one_list[2 * at + 1]]))
        attend(items)
        return carry

    def two(i, carry):
        attend([(query_row(two_list[3 * i]), [two_list[3 * i + 1], two_list[3 * i + 2]])])
        return carry

    lax.fori_loop(0, (ones + 1) // 2, one_pair, 0)
    lax.fori_loop(0, twos, two, 0)
    eye = lax.broadcasted_iota(jnp.int32, (HS, HS), 0) == lax.broadcasted_iota(jnp.int32, (HS, HS), 1)
    for x in range(NX):
        base = PAD + x * 1024
        out_ref[x, 0:1024] = outs[base:base + 1024, :].astype(BF)
        lines = []
        for b in range(8):
            block = stats[base + b * HS:base + (b + 1) * HS, :]
            lines.append(jnp.sum(jnp.where(eye, block, 0.0), axis=0, keepdims=True))
        lse = jnp.concatenate(lines, axis=0)
        high = lse.astype(BF)
        rest = lse - high.astype(F32)
        middle = rest.astype(BF)
        low = (rest - middle.astype(F32)).astype(BF)
        tail = jnp.concatenate([high.astype(F32), middle.astype(F32), low.astype(F32), jnp.zeros((8, HS), F32)], axis=0)
        out_ref[x, 1024:1056] = tail.astype(BF)


def windows(lists, my_x, queries, pieces):
    layout = tuple((d, first, rows) for d, first, rows, _ in pieces)
    total = PAD + NX * 1024 + 2 * GROUP
    smem = pl.BlockSpec(memory_space=pltpu.SMEM)
    return pl.pallas_call(
        functools.partial(window_kernel, layout),
        in_specs=[smem] * 4 + [ANY] * (NX + len(pieces)),
        out_specs=VMEM_ALL,
        scratch_shapes=[
            pltpu.VMEM((NZ * 4 * ROW, 512), BF),
            pltpu.VMEM((NX, 1024, HS), BF),
            pltpu.VMEM((total, HS), F32),
            pltpu.VMEM((total, HS), F32),
            pltpu.VMEM((total, HS), F32),
            pltpu.SemaphoreType.DMA((len(pieces),)),
            pltpu.SemaphoreType.DMA((NX,)),
        ],
        out_shape=jax.ShapeDtypeStruct((NX, 1056, HS), BF),
        cost_estimate=pl.CostEstimate(flops=10**9, bytes_accessed=8 * 2**20, transcendentals=10**6),
        compiler_params=pltpu.CompilerParams(vmem_limit_bytes=58 * MIB),
        name="windows",
    )(*lists, my_x, *queries, *[piece[-1] for piece in pieces])


def combine_kernel(parts_ref, out_ref):
    logs = []
    for x in range(NX):
        tail = parts_ref[x, 1024:1056].astype(F32)
        logs.append(tail[0:8] + tail[8:16] + tail[16:24])
    m = functools.reduce(jnp.maximum, logs)
    weights = [jnp.exp2(v - m) for v in logs]
    inv = 1.0 / functools.reduce(jnp.add, weights)
    weights = [w * inv for w in weights]
    eye = lax.broadcasted_iota(jnp.int32, (HS, HS), 0) == lax.broadcasted_iota(jnp.int32, (HS, HS), 1)
    for b in range(8):
        total = jnp.zeros((HS, HS), F32)
        for x in range(NX):
            line = jnp.broadcast_to(weights[x][b:b + 1, :], (HS, HS))
            column = jnp.sum(jnp.where(eye, line, 0.0), axis=1, keepdims=True)
            total += column * parts_ref[x, b * HS:(b + 1) * HS].astype(F32)
        out_ref[b * HS:(b + 1) * HS, :] = total.astype(BF)


def combine(parts):
    return pl.pallas_call(
        combine_kernel,
        in_specs=[VMEM_ALL],
        out_specs=VMEM_ALL,
        out_shape=jax.ShapeDtypeStruct((1024, HS), BF),
        cost_estimate=pl.CostEstimate(flops=10**7, bytes_accessed=2 * 2**20, transcendentals=0),
        compiler_params=pltpu.CompilerParams(vmem_limit_bytes=8 * MIB),
        name="combine",
    )(parts)


def as_index(*values):
    return jnp.stack(values).astype(jnp.int32)


def on_device(corpus, enc_qkv, enc_out, cca_kv, gain_in, gain_out, queries, nbr_ids):
    width = corpus.shape[2]
    my_z, my_x, my_y, core = (lax.axis_index(a) for a in ("z", "x", "y", "c"))
    corpus_flat = corpus.reshape(-1, width)
    e_own = enc_out.reshape(2 * HS, width)
    e_other = shifted(e_own, "c", 1)

    kv = lax.optimization_barrier(cca_kv.reshape(cca_kv.shape[0], 512))
    kv = spread(kv, "z").reshape(-1, 512)

    w_rows = enc_qkv.transpose(0, 2, 1, 3).reshape(width * 6, HS)
    att_own, att_send = encode(corpus_flat, w_rows, gain_in.reshape(1, width), as_index(core), as_index(my_y))
    nbr_ids, queries, att_send = lax.optimization_barrier((nbr_ids, queries, att_send))
    att_other = shifted(att_send, "c", 1)

    id_rows = jnp.pad(nbr_ids.astype(BF), ((0, 8), (0, HS - 2)))
    q_rows = jnp.concatenate([queries.reshape(1024, HS), id_rows], axis=0)
    qs = [q_rows] + [shifted(q_rows, "x", -d) for d in range(1, NX)]
    terms = project(att_own, att_other, e_own, e_other)

    terms = [terms[0]] + [shifted(terms[k], "y", k) for k in range(1, NY)]
    kv, terms[1], terms[3], qs = lax.optimization_barrier((kv, terms[1], terms[3], qs))
    got = jnp.stack([q[1024:1032, 0:2] for q in qs]).astype(jnp.int32).reshape(-1)
    below = shifted(got, "z", 1)
    from_left = shifted(kv, "x", 1)
    from_right = shifted(kv, "x", -1)

    u = normalise(terms, corpus_flat, gain_out.reshape(1, width), as_index(core * NY + my_y))
    us = [u] + [shifted(u, "y", k) for k in range(1, NY)]
    us[1], us[3], from_left, from_right, below = lax.optimization_barrier(
        (us[1], us[3], from_left, from_right, below)
    )
    ids = jnp.concatenate([got, below])
    half = kv.shape[0] // 2
    far_top = shifted(from_left[:half], "x", 1)
    far_bottom = shifted(from_right[half:], "x", -1)
    weights = [kv, from_left, from_right, far_top, far_bottom]
    at = as_index(my_x, my_y)
    memory_own, u_own = memorise(at, us, weights)
    u_other = shifted(u_own, "c", 1)
    pieces = ring_pieces(memory_own, 0)
    (memory_other,) = memorise(at, [u_other], weights)
    pieces += ring_pieces(memory_other, 2 * ROW)

    lists = plan(ids, as_index(my_z), as_index(my_x), as_index(core))
    parts = windows(lists, as_index(my_x), qs, pieces)
    parts = lax.all_to_all(parts, "x", split_axis=0, concat_axis=0, tiled=True)
    return combine(parts).reshape(512, 2, HS)


def solution(mesh):
    inner = Mesh(mesh.devices.reshape(NZ, NX, NY, NC), ("z", "x", "y", "c"))
    seq, head = ("z", "x"), ("y", "c")
    placed = (
        P(seq, None, None),
        P(None, head, None, None),
        P(head, None, None),
        P(seq, head, None, None),
        P(),
        P(),
        P(seq, head, None),
        P(seq, None),
    )
    return jax.shard_map(
        on_device, mesh=inner, in_specs=placed, out_specs=P(seq, head, None), check_vma=False
    )
```

```python
import functools

import jax
import jax.numpy as jnp
from jax import lax
from jax.experimental import pallas as pl
from jax.experimental.pallas import tpu as pltpu
from jax.sharding import Mesh, PartitionSpec as P

GROUP = 64
EPS = 1e-06
MIB = 2**20
NZ, NX, NY, NC = 8, 4, 4, 2
ROW = 128
HS = 128
MASKED = -1e30
LOG_SCALE = HS ** -0.5 * 1.4426950408889634
BF = jnp.bfloat16
F32 = jnp.float32
ANY = pl.BlockSpec(memory_space=pl.ANY)
VMEM_ALL = pl.BlockSpec(memory_space=pltpu.VMEM)


def shifted(value, axis, steps):
    n = lax.axis_size(axis)
    return lax.ppermute(value, axis, [(i, (i + steps) % n) for i in range(n)])


def spread(value, axis):
    n = lax.axis_size(axis)
    copies = jnp.broadcast_to(value[None], (n,) + value.shape)
    return lax.all_to_all(copies, axis, split_axis=0, concat_axis=0, tiled=True)


def encoder_kernel(core_ref, y_ref, x_ref, w_ref, g_ref, own_ref, send_ref, wide, wmat, acc, ssq):
    step = pl.program_id(0)
    depth = x_ref.shape[1]

    @pl.when(step == 0)
    def _():
        acc[...] = jnp.zeros_like(acc)
        ssq[...] = jnp.zeros_like(ssq)

    wide[...] = w_ref[...].astype(F32)
    for col in range(6):
        wmat[:, col * HS:(col + 1) * HS] = wide[pl.ds(col, depth, stride=6), :].astype(BF)
    x = x_ref[...].astype(F32)
    ssq[...] += jnp.sum(x * x, axis=1, keepdims=True)
    xg = (x * g_ref[...]).astype(BF)
    acc[...] += jnp.dot(xg, wmat[...], preferred_element_type=F32)

    @pl.when(step == pl.num_programs(0) - 1)
    def _():
        core, my_y = core_ref[0], y_ref[0]
        done = []
        total = depth * pl.num_programs(0)
        scale = lax.rsqrt(ssq[...] / total + EPS)
        rows = x_ref.shape[0] // ROW
        for pair in range(rows // 2):
            spots = [(r, h) for r in (2 * pair, 2 * pair + 1) for h in range(2)]

            def part(r, col):
                sl = slice(r * ROW, (r + 1) * ROW)
                return (acc[sl, col * HS:(col + 1) * HS] * scale[sl]).astype(BF)

            scores = [
                lax.dot_general(
                    part(r, h), part(r, 2 + h), (((1,), (1,)), ((), ())), preferred_element_type=F32
                ) * LOG_SCALE
                for r, h in spots
            ]
            tops = [jnp.max(s, axis=1, keepdims=True) for s in scores]
            probs = [jnp.exp2(s - m) for s, m in zip(scores, tops)]
            sums = [jnp.sum(p, axis=1, keepdims=True) for p in probs]
            atts = [
                (jnp.dot(p.astype(BF), part(r, 4 + h), preferred_element_type=F32) * (1.0 / total_p)).astype(BF)
                for (r, h), p, total_p in zip(spots, probs, sums)
            ]
            done.append([jnp.concatenate(atts[2 * i:2 * i + 2], axis=1) for i in range(2)])
        for i in range(2):
            own = jnp.where(core == 0, done[0][i], done[1][i])
            send = jnp.where(core == 0, done[1][i], done[0][i])
            for half in range(2):
                k = jnp.bitwise_and(2 * i + half - my_y, NY - 1)
                spot = pl.ds(pl.multiple_of(k * 64, 64), 64)
                own_ref[spot, :] = own[half * 64:(half + 1) * 64]
                send_ref[spot, :] = send[half * 64:(half + 1) * 64]


def encode(corpus_flat, w_rows, gain, core, my_y):
    tokens, width = corpus_flat.shape
    steps = 4
    depth = width // steps
    return pl.pallas_call(
        encoder_kernel,
        grid_spec=pltpu.PrefetchScalarGridSpec(
            num_scalar_prefetch=2,
            grid=(steps,),
            in_specs=[
                pl.BlockSpec((tokens, depth), lambda i, c, y: (0, i)),
                pl.BlockSpec((depth * 6, HS), lambda i, c, y: (i, 0)),
                pl.BlockSpec((1, depth), lambda i, c, y: (0, i)),
            ],
            out_specs=[pl.BlockSpec((2 * ROW, 2 * HS), lambda i, c, y: (0, 0))] * 2,
            scratch_shapes=[
                pltpu.VMEM((depth * 6, HS), F32),
                pltpu.VMEM((depth, 6 * HS), BF),
                pltpu.VMEM((tokens, 6 * HS), F32),
                pltpu.VMEM((tokens, 1), F32),
            ],
        ),
        out_shape=[jax.ShapeDtypeStruct((2 * ROW, 2 * HS), BF)] * 2,
        cost_estimate=pl.CostEstimate(
            flops=2 * tokens * width * 6 * HS, bytes_accessed=(tokens + 768) * width * 2, transcendentals=0
        ),
        compiler_params=pltpu.CompilerParams(vmem_limit_bytes=60 * MIB),
        name="encoder",
    )(core, my_y, corpus_flat, w_rows, gain)


def project_kernel(a_ref, b_ref, ea_ref, eb_ref, *outs):
    rows = a_ref.shape[0] // NY
    value = jnp.dot(a_ref[...], ea_ref[...], preferred_element_type=F32)
    value += jnp.dot(b_ref[...], eb_ref[...], preferred_element_type=F32)
    for k in range(NY):
        outs[k][...] = value[k * rows:(k + 1) * rows].astype(BF)


def project(att, att_other, e_own, e_other):
    tokens, depth = att_other.shape
    width = e_own.shape[1]
    cols = 1024
    rows = tokens // NY
    return pl.pallas_call(
        project_kernel,
        grid=(width // cols,),
        in_specs=[
            pl.BlockSpec((tokens, depth), lambda i: (0, 0)),
            pl.BlockSpec((tokens, depth), lambda i: (0, 0)),
            pl.BlockSpec((depth, cols), lambda i: (0, i)),
            pl.BlockSpec((depth, cols), lambda i: (0, i)),
        ],
        out_specs=[pl.BlockSpec((rows, cols), lambda i: (0, i))] * NY,
        out_shape=[jax.ShapeDtypeStruct((rows, width), BF)] * NY,
        cost_estimate=pl.CostEstimate(
            flops=4 * tokens * depth * width, bytes_accessed=4 * depth * width, transcendentals=0
        ),
        compiler_params=pltpu.CompilerParams(vmem_limit_bytes=60 * MIB),
        name="project",
    )(att, att_other, e_own, e_other)


def norm_kernel(block_ref, t0, t1, t2, t3, x_ref, g_ref, out_ref):
    total = x_ref[...].astype(F32)
    for term in (t0, t1, t2, t3):
        total += term[...].astype(F32)
    rinv = lax.rsqrt(jnp.mean(total * total, axis=1, keepdims=True) + EPS)
    u = (total * rinv * g_ref[...]).astype(BF)
    for z in range(NZ):
        for x in range(NX):
            src, dst = (z * NX + x) * HS, (x * NZ + z) * HS
            out_ref[:, dst:dst + HS] = u[:, src:src + HS]


def normalise(terms, corpus_flat, gain, block):
    rows, width = terms[0].shape
    whole = pl.BlockSpec((rows, width), lambda i, b: (0, 0))
    return pl.pallas_call(
        norm_kernel,
        grid_spec=pltpu.PrefetchScalarGridSpec(
            num_scalar_prefetch=1,
            grid=(1,),
            in_specs=[whole] * NY
            + [
                pl.BlockSpec((rows, width), lambda i, b: (b[0], 0)),
                pl.BlockSpec((1, width), lambda i, b: (0, 0)),
            ],
            out_specs=whole,
        ),
        out_shape=jax.ShapeDtypeStruct((rows, width), BF),
        cost_estimate=pl.CostEstimate(flops=8 * rows * width, bytes_accessed=12 * rows * width, transcendentals=0),
        compiler_params=pltpu.CompilerParams(vmem_limit_bytes=60 * MIB),
        name="normalise",
    )(block, *terms, corpus_flat, gain)


ORDER = (0, NX - 1, 1, 2)


def memory_kernel(parts, at_ref, *refs):
    us = refs[:parts]
    k_refs = refs[parts:parts + NX]
    out_ref = refs[parts + NX]
    rest = refs[parts + NX + 1:]
    if parts > 1:
        whole, rest = rest[0], rest[1:]
    ua, kv, sem, out_sem = rest
    depth = NZ * HS
    rows = ua.shape[0] // parts
    u_copies = []
    for k in range(parts):
        first = pl.multiple_of(lax.rem(at_ref[1] - k + parts, parts) * rows, rows)
        u_copies.append(pltpu.make_async_copy(us[k], ua.at[pl.ds(first, rows)], sem.at[k]))
    k_copies = [pltpu.make_async_copy(k_ref, kv.at[i], sem.at[NY + i]) for i, k_ref in enumerate(k_refs)]
    for copy in u_copies + k_copies:
        copy.start()
    for copy in u_copies:
        copy.wait()
    if parts > 1:
        back = pltpu.make_async_copy(ua, whole, out_sem)
        back.start()
    total = jnp.zeros(out_ref.shape, F32)
    for i in range(NX):
        k_copies[i].wait()
        first = pl.multiple_of(lax.rem(at_ref[0] + ORDER[i], NX) * depth, depth)
        total += jnp.dot(ua[:, pl.ds(first, depth)], kv[i], preferred_element_type=F32)
    out_ref[...] = total.astype(BF)
    if parts > 1:
        back.wait()


def memorise(at, us, payloads):
    width = us[0].shape[1]
    tokens = us[0].shape[0] * len(us)
    cols = payloads[0].shape[1]
    depth = width // NX
    memory = jax.ShapeDtypeStruct((tokens, cols), BF)
    assembled = [jax.ShapeDtypeStruct((tokens, width), BF)] if len(us) > 1 else []
    return pl.pallas_call(
        functools.partial(memory_kernel, len(us)),
        in_specs=[pl.BlockSpec(memory_space=pltpu.SMEM)] + [ANY] * (len(us) + NX),
        out_specs=[VMEM_ALL] + [ANY] * len(assembled),
        scratch_shapes=[
            pltpu.VMEM((tokens, width), BF),
            pltpu.VMEM((NX, depth, cols), BF),
            pltpu.SemaphoreType.DMA((NY + NX,)),
            pltpu.SemaphoreType.DMA,
        ],
        out_shape=[memory] + assembled,
        cost_estimate=pl.CostEstimate(
            flops=2 * tokens * width * cols, bytes_accessed=2 * width * cols, transcendentals=0
        ),
        compiler_params=pltpu.CompilerParams(vmem_limit_bytes=12 * MIB),
        name="memorise",
    )(at, *us, *payloads)


def ring_pieces(block, base):
    rows = block.shape[0]
    half = rows // 2
    pieces = [(0, base, rows, block)]
    up = down = block
    for s in range(1, NZ // 2):
        up = shifted(up, "z", 1)
        down = shifted(down, "z", -1)
        pieces += [(s, base, rows, up), (NZ - s, base, rows, down)]
    pieces += [
        (NZ // 2, base, half, shifted(up[:half], "z", 1)),
        (NZ // 2, base + half, half, shifted(down[half:], "z", -1)),
    ]
    return pieces


PAD = 8


def plan_kernel(ids_ref, z_ref, x_ref, core_ref, one_list, two_list, counts_ref):
    my_z, my_x, core = z_ref[0], x_ref[0], core_ref[0]

    def held(row):
        return jnp.logical_and(row >= 0, jnp.bitwise_and(jnp.right_shift(row, 2), NX - 1) == my_x)

    def wanted(w, n):
        group = jnp.maximum(w - 1, 0)
        step = jnp.bitwise_and(jnp.right_shift(group, 3) - my_x, NX - 1)
        here = step * 16 + jnp.bitwise_and(group, 7) * 2
        under = NX * 16 + jnp.bitwise_and(NX - 1 - my_x, NX - 1) * 16 + 14
        row = ids_ref[jnp.where(w == 0, under, here) + n]
        return jnp.where(jnp.logical_and(w == 0, my_z == 0), -1, row)

    def place(row):
        distance = jnp.bitwise_and(my_z - jnp.right_shift(row, 4), NZ - 1)
        local = jnp.bitwise_and(row, 3)
        half = jnp.bitwise_and(jnp.right_shift(local, 1) + core, 1)
        return distance * 512 + half * 256 + jnp.bitwise_and(local, 1) * 128

    def note(w, counts):
        ones, twos = counts
        rows = [wanted(w, n) for n in range(2)]
        ok = [held(row).astype(jnp.int32) for row in rows]
        single, both = ok[0] + ok[1] == 1, ok[0] + ok[1] == 2
        spot = place(jnp.maximum(jnp.where(ok[0] == 1, rows[0], rows[1]), 0))
        one_list[2 * ones] = w
        one_list[2 * ones + 1] = spot
        two_list[3 * twos] = w
        two_list[3 * twos + 1] = spot
        two_list[3 * twos + 2] = place(jnp.maximum(rows[1], 0))
        return ones + single.astype(jnp.int32), twos + both.astype(jnp.int32)

    ones, twos = lax.fori_loop(0, NX * 8 + 1, note, (0, 0))
    counts_ref[0] = ones
    counts_ref[1] = twos


def plan(ids, my_z, my_x, core):
    smem = pl.BlockSpec(memory_space=pltpu.SMEM)
    return pl.pallas_call(
        plan_kernel,
        in_specs=[smem] * 4,
        out_specs=[smem] * 3,
        out_shape=[
            jax.ShapeDtypeStruct((128,), jnp.int32),
            jax.ShapeDtypeStruct((128,), jnp.int32),
            jax.ShapeDtypeStruct((2,), jnp.int32),
        ],
        name="plan",
    )(ids, my_z, my_x, core)


def window_kernel(layout, one_list, two_list, counts_ref, x_ref, *refs):
    q_refs, refs = refs[:NX], refs[NX:]
    pieces = refs[:len(layout)]
    out_ref = refs[len(layout)]
    table, q_in, qs, outs, stats, sem, q_sem = refs[len(layout) + 1:]
    ones, twos = counts_ref[0], counts_ref[1]
    plane_rows = NX * 1024
    total_rows = qs.shape[0]
    q_copies = [pltpu.make_async_copy(q_refs[d].at[pl.ds(0, 1024)], q_in.at[d], q_sem.at[d]) for d in range(NX)]
    copies = [
        pltpu.make_async_copy(pieces[i], table.at[pl.ds(distance * 512 + first, rows)], sem.at[i])
        for i, (distance, first, rows) in enumerate(layout)
    ]
    for copy in q_copies + copies:
        copy.start()
    outs[...] = jnp.zeros_like(outs)
    stats[...] = jnp.full_like(stats, MASKED)
    qs[0:PAD, :] = jnp.zeros((PAD, HS), F32)
    qs[PAD + plane_rows:, :] = jnp.zeros((total_rows - PAD - plane_rows, HS), F32)
    for d in range(NX):
        q_copies[d].wait()
        first = pl.multiple_of(PAD + jnp.bitwise_and(x_ref[0] + d, NX - 1) * 1024, 8)
        qs[pl.ds(first, 1024), :] = q_in[d].astype(F32)
    for copy in copies:
        copy.wait()

    def attend(items):
        jobs = []
        for start, spots in items:
            for h in range(2):
                q = qs[pl.ds(start + h, GROUP, stride=2), :].astype(BF)
                k = [table[pl.ds(pl.multiple_of(f, ROW), ROW), h * 256:h * 256 + HS] for f in spots]
                k = k[0] if len(k) == 1 else jnp.concatenate(k, axis=0)
                s = lax.dot_general(q, k, (((1,), (1,)), ((), ())), preferred_element_type=F32)
                jobs.append([start + h, h, spots, s])
        for job in jobs:
            job[3] = job[3] * LOG_SCALE
            job.append(jnp.max(job[3], axis=1, keepdims=True))
        for job in jobs:
            job[3] = jnp.exp2(job[3] - job[4])
            job.append(jnp.sum(job[3], axis=1, keepdims=True))
        for first, h, spots, p, m, total in jobs:
            v = [table[pl.ds(pl.multiple_of(f, ROW), ROW), h * 256 + HS:h * 256 + 2 * HS] for f in spots]
            v = v[0] if len(v) == 1 else jnp.concatenate(v, axis=0)
            out = jnp.dot(p.astype(BF), v, preferred_element_type=F32) * (1.0 / total)
            outs[pl.ds(first, GROUP, stride=2), :] = out
            stats[pl.ds(first, GROUP, stride=2), :] = jnp.broadcast_to(m + jnp.log2(total), (GROUP, HS))

    def query_row(w):
        return PAD + 2 * (GROUP * w - 1)

    def one_pair(i, carry):
        items = []
        for lane in range(2):
            at = jnp.minimum(2 * i + lane, ones - 1)
            items.append((query_row(one_list[2 * at]), [one_list[2 * at + 1]]))
        attend(items)
        return carry

    def two(i, carry):
        attend([(query_row(two_list[3 * i]), [two_list[3 * i + 1], two_list[3 * i + 2]])])
        return carry

    lax.fori_loop(0, (ones + 1) // 2, one_pair, 0)
    lax.fori_loop(0, twos, two, 0)
    eye = lax.broadcasted_iota(jnp.int32, (HS, HS), 0) == lax.broadcasted_iota(jnp.int32, (HS, HS), 1)
    for x in range(NX):
        base = PAD + x * 1024
        out_ref[x, 0:1024] = outs[base:base + 1024, :].astype(BF)
        lines = []
        for b in range(8):
            block = stats[base + b * HS:base + (b + 1) * HS, :]
            lines.append(jnp.sum(jnp.where(eye, block, 0.0), axis=0, keepdims=True))
        lse = jnp.concatenate(lines, axis=0)
        high = lse.astype(BF)
        rest = lse - high.astype(F32)
        middle = rest.astype(BF)
        low = (rest - middle.astype(F32)).astype(BF)
        tail = jnp.concatenate([high.astype(F32), middle.astype(F32), low.astype(F32), jnp.zeros((8, HS), F32)], axis=0)
        out_ref[x, 1024:1056] = tail.astype(BF)


def windows(lists, my_x, queries, pieces):
    layout = tuple((d, first, rows) for d, first, rows, _ in pieces)
    total = PAD + NX * 1024 + 2 * GROUP
    smem = pl.BlockSpec(memory_space=pltpu.SMEM)
    return pl.pallas_call(
        functools.partial(window_kernel, layout),
        in_specs=[smem] * 4 + [ANY] * (NX + len(pieces)),
        out_specs=VMEM_ALL,
        scratch_shapes=[
            pltpu.VMEM((NZ * 4 * ROW, 512), BF),
            pltpu.VMEM((NX, 1024, HS), BF),
            pltpu.VMEM((total, HS), F32),
            pltpu.VMEM((total, HS), F32),
            pltpu.VMEM((total, HS), F32),
            pltpu.SemaphoreType.DMA((len(pieces),)),
            pltpu.SemaphoreType.DMA((NX,)),
        ],
        out_shape=jax.ShapeDtypeStruct((NX, 1056, HS), BF),
        cost_estimate=pl.CostEstimate(flops=10**9, bytes_accessed=8 * 2**20, transcendentals=10**6),
        compiler_params=pltpu.CompilerParams(vmem_limit_bytes=58 * MIB),
        name="windows",
    )(*lists, my_x, *queries, *[piece[-1] for piece in pieces])


def combine_kernel(parts_ref, out_ref):
    logs = []
    for x in range(NX):
        tail = parts_ref[x, 1024:1056].astype(F32)
        logs.append(tail[0:8] + tail[8:16] + tail[16:24])
    m = functools.reduce(jnp.maximum, logs)
    weights = [jnp.exp2(v - m) for v in logs]
    inv = 1.0 / functools.reduce(jnp.add, weights)
    weights = [w * inv for w in weights]
    eye = lax.broadcasted_iota(jnp.int32, (HS, HS), 0) == lax.broadcasted_iota(jnp.int32, (HS, HS), 1)
    for b in range(8):
        total = jnp.zeros((HS, HS), F32)
        for x in range(NX):
            line = jnp.broadcast_to(weights[x][b:b + 1, :], (HS, HS))
            column = jnp.sum(jnp.where(eye, line, 0.0), axis=1, keepdims=True)
            total += column * parts_ref[x, b * HS:(b + 1) * HS].astype(F32)
        out_ref[b * HS:(b + 1) * HS, :] = total.astype(BF)


def combine(parts):
    return pl.pallas_call(
        combine_kernel,
        in_specs=[VMEM_ALL],
        out_specs=VMEM_ALL,
        out_shape=jax.ShapeDtypeStruct((1024, HS), BF),
        cost_estimate=pl.CostEstimate(flops=10**7, bytes_accessed=2 * 2**20, transcendentals=0),
        compiler_params=pltpu.CompilerParams(vmem_limit_bytes=8 * MIB),
        name="combine",
    )(parts)


def as_index(*values):
    return jnp.stack(values).astype(jnp.int32)


def on_device(corpus, enc_qkv, enc_out, cca_kv, gain_in, gain_out, queries, nbr_ids):
    width = corpus.shape[2]
    my_z, my_x, my_y, core = (lax.axis_index(a) for a in ("z", "x", "y", "c"))
    corpus_flat = corpus.reshape(-1, width)
    e_own = enc_out.reshape(2 * HS, width)
    e_other = shifted(e_own, "c", 1)

    kv = lax.optimization_barrier(cca_kv.reshape(cca_kv.shape[0], 512))
    kv = spread(kv, "z").reshape(-1, 512)

    w_rows = enc_qkv.transpose(0, 2, 1, 3).reshape(width * 6, HS)
    att_own, att_send = encode(corpus_flat, w_rows, gain_in.reshape(1, width), as_index(core), as_index(my_y))
    nbr_ids, queries, att_send = lax.optimization_barrier((nbr_ids, queries, att_send))
    att_other = shifted(att_send, "c", 1)

    id_rows = jnp.pad(nbr_ids.astype(BF), ((0, 8), (0, HS - 2)))
    q_rows = jnp.concatenate([queries.reshape(1024, HS), id_rows], axis=0)
    qs = [q_rows] + [shifted(q_rows, "x", -d) for d in range(1, NX)]
    terms = project(att_own, att_other, e_own, e_other)

    terms = [terms[0]] + [shifted(terms[k], "y", k) for k in range(1, NY)]
    kv, terms[1], terms[3] = lax.optimization_barrier((kv, terms[1], terms[3]))
    terms[2], qs = lax.optimization_barrier((terms[2], qs))
    got = jnp.stack([q[1024:1032, 0:2] for q in qs]).astype(jnp.int32).reshape(-1)
    below = shifted(got, "z", 1)
    from_left = shifted(kv, "x", 1)
    from_right = shifted(kv, "x", -1)
    from_far = shifted(kv, "x", 2)

    u = normalise(terms, corpus_flat, gain_out.reshape(1, width), as_index(core * NY + my_y))
    us = [u] + [shifted(u, "y", k) for k in range(1, NY)]
    lists = plan(jnp.concatenate([got, below]), as_index(my_z), as_index(my_x), as_index(core))
    weights = [kv, from_left, from_right, from_far]
    us[1], us[3], lists, weights = lax.optimization_barrier((us[1], us[3], lists, weights))
    at = as_index(my_x, my_y)
    memory_own, u_own = memorise(at, us, weights)
    u_other = shifted(u_own, "c", 1)
    pieces = ring_pieces(memory_own, 0)
    (memory_other,) = memorise(at, [u_other], weights)
    pieces += ring_pieces(memory_other, 2 * ROW)

    parts = windows(lists, as_index(my_x), qs, pieces)
    parts = lax.all_to_all(parts, "x", split_axis=0, concat_axis=0, tiled=True)
    return combine(parts).reshape(512, 2, HS)


def solution(mesh):
    inner = Mesh(mesh.devices.reshape(NZ, NX, NY, NC), ("z", "x", "y", "c"))
    seq, head = ("z", "x"), ("y", "c")
    placed = (
        P(seq, None, None),
        P(None, head, None, None),
        P(head, None, None),
        P(seq, head, None, None),
        P(),
        P(),
        P(seq, head, None),
        P(seq, None),
    )
    return jax.shard_map(
        on_device, mesh=inner, in_specs=placed, out_specs=P(seq, head, None), check_vma=False
    )
```

```python
import functools

import jax
import jax.numpy as jnp
from jax import lax
from jax.experimental import pallas as pl
from jax.experimental.pallas import tpu as pltpu
from jax.sharding import Mesh, PartitionSpec as P

GROUP = 64
EPS = 1e-06
MIB = 2**20
NZ, NX, NY, NC = 8, 4, 4, 2
ROW = 128
HS = 128
MASKED = -1e30
LOG_SCALE = HS ** -0.5 * 1.4426950408889634
BF = jnp.bfloat16
F32 = jnp.float32
ANY = pl.BlockSpec(memory_space=pl.ANY)
VMEM_ALL = pl.BlockSpec(memory_space=pltpu.VMEM)


def shifted(value, axis, steps):
    n = lax.axis_size(axis)
    return lax.ppermute(value, axis, [(i, (i + steps) % n) for i in range(n)])


def spread(value, axis):
    n = lax.axis_size(axis)
    copies = jnp.broadcast_to(value[None], (n,) + value.shape)
    return lax.all_to_all(copies, axis, split_axis=0, concat_axis=0, tiled=True)


def encoder_kernel(core_ref, y_ref, x_ref, w_ref, g_ref, own_ref, send_ref, wide, wmat, acc, ssq):
    step = pl.program_id(0)
    depth = x_ref.shape[1]

    @pl.when(step == 0)
    def _():
        acc[...] = jnp.zeros_like(acc)
        ssq[...] = jnp.zeros_like(ssq)

    wide[...] = w_ref[...].astype(F32)
    for col in range(6):
        wmat[:, col * HS:(col + 1) * HS] = wide[pl.ds(col, depth, stride=6), :].astype(BF)
    x = x_ref[...].astype(F32)
    ssq[...] += jnp.sum(x * x, axis=1, keepdims=True)
    xg = (x * g_ref[...]).astype(BF)
    acc[...] += jnp.dot(xg, wmat[...], preferred_element_type=F32)

    @pl.when(step == pl.num_programs(0) - 1)
    def _():
        core, my_y = core_ref[0], y_ref[0]
        done = []
        total = depth * pl.num_programs(0)
        scale = lax.rsqrt(ssq[...] / total + EPS)
        rows = x_ref.shape[0] // ROW
        for pair in range(rows // 2):
            spots = [(r, h) for r in (2 * pair, 2 * pair + 1) for h in range(2)]

            def part(r, col):
                sl = slice(r * ROW, (r + 1) * ROW)
                return (acc[sl, col * HS:(col + 1) * HS] * scale[sl]).astype(BF)

            scores = [
                lax.dot_general(
                    part(r, h), part(r, 2 + h), (((1,), (1,)), ((), ())), preferred_element_type=F32
                ) * LOG_SCALE
                for r, h in spots
            ]
            tops = [jnp.max(s, axis=1, keepdims=True) for s in scores]
            probs = [jnp.exp2(s - m) for s, m in zip(scores, tops)]
            sums = [jnp.sum(p, axis=1, keepdims=True) for p in probs]
            atts = [
                (jnp.dot(p.astype(BF), part(r, 4 + h), preferred_element_type=F32) * (1.0 / total_p)).astype(BF)
                for (r, h), p, total_p in zip(spots, probs, sums)
            ]
            done.append([jnp.concatenate(atts[2 * i:2 * i + 2], axis=1) for i in range(2)])
        for i in range(2):
            own = jnp.where(core == 0, done[0][i], done[1][i])
            send = jnp.where(core == 0, done[1][i], done[0][i])
            for half in range(2):
                k = jnp.bitwise_and(2 * i + half - my_y, NY - 1)
                spot = pl.ds(pl.multiple_of(k * 64, 64), 64)
                own_ref[spot, :] = own[half * 64:(half + 1) * 64]
                send_ref[spot, :] = send[half * 64:(half + 1) * 64]


def encode(corpus_flat, w_rows, gain, core, my_y):
    tokens, width = corpus_flat.shape
    steps = 4
    depth = width // steps
    return pl.pallas_call(
        encoder_kernel,
        grid_spec=pltpu.PrefetchScalarGridSpec(
            num_scalar_prefetch=2,
            grid=(steps,),
            in_specs=[
                pl.BlockSpec((tokens, depth), lambda i, c, y: (0, i)),
                pl.BlockSpec((depth * 6, HS), lambda i, c, y: (i, 0)),
                pl.BlockSpec((1, depth), lambda i, c, y: (0, i)),
            ],
            out_specs=[pl.BlockSpec((2 * ROW, 2 * HS), lambda i, c, y: (0, 0))] * 2,
            scratch_shapes=[
                pltpu.VMEM((depth * 6, HS), F32),
                pltpu.VMEM((depth, 6 * HS), BF),
                pltpu.VMEM((tokens, 6 * HS), F32),
                pltpu.VMEM((tokens, 1), F32),
            ],
        ),
        out_shape=[jax.ShapeDtypeStruct((2 * ROW, 2 * HS), BF)] * 2,
        cost_estimate=pl.CostEstimate(
            flops=2 * tokens * width * 6 * HS, bytes_accessed=(tokens + 768) * width * 2, transcendentals=0
        ),
        compiler_params=pltpu.CompilerParams(vmem_limit_bytes=60 * MIB),
        name="encoder",
    )(core, my_y, corpus_flat, w_rows, gain)


def project_kernel(a_ref, b_ref, ea_ref, eb_ref, *outs):
    rows = a_ref.shape[0] // NY
    value = jnp.dot(a_ref[...], ea_ref[...], preferred_element_type=F32)
    value += jnp.dot(b_ref[...], eb_ref[...], preferred_element_type=F32)
    for k in range(NY):
        outs[k][...] = value[k * rows:(k + 1) * rows].astype(BF)


def project(att, att_other, e_own, e_other):
    tokens, depth = att_other.shape
    width = e_own.shape[1]
    cols = 1024
    rows = tokens // NY
    return pl.pallas_call(
        project_kernel,
        grid=(width // cols,),
        in_specs=[
            pl.BlockSpec((tokens, depth), lambda i: (0, 0)),
            pl.BlockSpec((tokens, depth), lambda i: (0, 0)),
            pl.BlockSpec((depth, cols), lambda i: (0, i)),
            pl.BlockSpec((depth, cols), lambda i: (0, i)),
        ],
        out_specs=[pl.BlockSpec((rows, cols), lambda i: (0, i))] * NY,
        out_shape=[jax.ShapeDtypeStruct((rows, width), BF)] * NY,
        cost_estimate=pl.CostEstimate(
            flops=4 * tokens * depth * width, bytes_accessed=4 * depth * width, transcendentals=0
        ),
        compiler_params=pltpu.CompilerParams(vmem_limit_bytes=60 * MIB),
        name="project",
    )(att, att_other, e_own, e_other)


def norm_kernel(block_ref, t0, t1, t2, t3, x_ref, g_ref, out_ref):
    total = x_ref[...].astype(F32)
    for term in (t0, t1, t2, t3):
        total += term[...].astype(F32)
    rinv = lax.rsqrt(jnp.mean(total * total, axis=1, keepdims=True) + EPS)
    u = (total * rinv * g_ref[...]).astype(BF)
    for z in range(NZ):
        for x in range(NX):
            src, dst = (z * NX + x) * HS, (x * NZ + z) * HS
            out_ref[:, dst:dst + HS] = u[:, src:src + HS]


def normalise(terms, corpus_flat, gain, block):
    rows, width = terms[0].shape
    whole = pl.BlockSpec((rows, width), lambda i, b: (0, 0))
    return pl.pallas_call(
        norm_kernel,
        grid_spec=pltpu.PrefetchScalarGridSpec(
            num_scalar_prefetch=1,
            grid=(1,),
            in_specs=[whole] * NY
            + [
                pl.BlockSpec((rows, width), lambda i, b: (b[0], 0)),
                pl.BlockSpec((1, width), lambda i, b: (0, 0)),
            ],
            out_specs=whole,
        ),
        out_shape=jax.ShapeDtypeStruct((rows, width), BF),
        cost_estimate=pl.CostEstimate(flops=8 * rows * width, bytes_accessed=12 * rows * width, transcendentals=0),
        compiler_params=pltpu.CompilerParams(vmem_limit_bytes=60 * MIB),
        name="normalise",
    )(block, *terms, corpus_flat, gain)


ORDER = (0, NX - 1, 1, 2)


def memory_kernel(parts, at_ref, *refs):
    us = refs[:parts]
    k_refs = refs[parts:parts + NX]
    out_ref = refs[parts + NX]
    rest = refs[parts + NX + 1:]
    if parts > 1:
        whole, rest = rest[0], rest[1:]
    ua, kv, sem, out_sem = rest
    depth = NZ * HS
    rows = ua.shape[0] // parts
    u_copies = []
    for k in range(parts):
        first = pl.multiple_of(lax.rem(at_ref[1] - k + parts, parts) * rows, rows)
        u_copies.append(pltpu.make_async_copy(us[k], ua.at[pl.ds(first, rows)], sem.at[k]))
    k_copies = [pltpu.make_async_copy(k_ref, kv.at[i], sem.at[NY + i]) for i, k_ref in enumerate(k_refs)]
    for copy in u_copies + k_copies:
        copy.start()
    for copy in u_copies:
        copy.wait()
    if parts > 1:
        back = pltpu.make_async_copy(ua, whole, out_sem)
        back.start()
    total = jnp.zeros(out_ref.shape, F32)
    for i in range(NX):
        k_copies[i].wait()
        first = pl.multiple_of(lax.rem(at_ref[0] + ORDER[i], NX) * depth, depth)
        total += jnp.dot(ua[:, pl.ds(first, depth)], kv[i], preferred_element_type=F32)
    out_ref[...] = total.astype(BF)
    if parts > 1:
        back.wait()


def memorise(at, us, payloads):
    width = us[0].shape[1]
    tokens = us[0].shape[0] * len(us)
    cols = payloads[0].shape[1]
    depth = width // NX
    memory = jax.ShapeDtypeStruct((tokens, cols), BF)
    assembled = [jax.ShapeDtypeStruct((tokens, width), BF)] if len(us) > 1 else []
    return pl.pallas_call(
        functools.partial(memory_kernel, len(us)),
        in_specs=[pl.BlockSpec(memory_space=pltpu.SMEM)] + [ANY] * (len(us) + NX),
        out_specs=[VMEM_ALL] + [ANY] * len(assembled),
        scratch_shapes=[
            pltpu.VMEM((tokens, width), BF),
            pltpu.VMEM((NX, depth, cols), BF),
            pltpu.SemaphoreType.DMA((NY + NX,)),
            pltpu.SemaphoreType.DMA,
        ],
        out_shape=[memory] + assembled,
        cost_estimate=pl.CostEstimate(
            flops=2 * tokens * width * cols, bytes_accessed=2 * width * cols, transcendentals=0
        ),
        compiler_params=pltpu.CompilerParams(vmem_limit_bytes=12 * MIB),
        name="memorise",
    )(at, *us, *payloads)


def ring_pieces(block, base):
    rows = block.shape[0]
    half = rows // 2
    pieces = [(0, base, rows, block)]
    up = down = block
    for s in range(1, NZ // 2):
        up = shifted(up, "z", 1)
        down = shifted(down, "z", -1)
        pieces += [(s, base, rows, up), (NZ - s, base, rows, down)]
    pieces += [
        (NZ // 2, base, half, shifted(up[:half], "z", 1)),
        (NZ // 2, base + half, half, shifted(down[half:], "z", -1)),
    ]
    return pieces


PAD = 8


def plan_kernel(ids_ref, z_ref, x_ref, core_ref, one_list, two_list, counts_ref):
    my_z, my_x, core = z_ref[0], x_ref[0], core_ref[0]

    def held(row):
        return jnp.logical_and(row >= 0, jnp.bitwise_and(jnp.right_shift(row, 2), NX - 1) == my_x)

    def wanted(w, n):
        group = jnp.maximum(w - 1, 0)
        step = jnp.bitwise_and(jnp.right_shift(group, 3) - my_x, NX - 1)
        here = step * 16 + jnp.bitwise_and(group, 7) * 2
        under = NX * 16 + jnp.bitwise_and(NX - 1 - my_x, NX - 1) * 16 + 14
        row = ids_ref[jnp.where(w == 0, under, here) + n]
        return jnp.where(jnp.logical_and(w == 0, my_z == 0), -1, row)

    def place(row):
        distance = jnp.bitwise_and(my_z - jnp.right_shift(row, 4), NZ - 1)
        local = jnp.bitwise_and(row, 3)
        half = jnp.bitwise_and(jnp.right_shift(local, 1) + core, 1)
        return distance * 512 + half * 256 + jnp.bitwise_and(local, 1) * 128

    def note(w, counts):
        ones, twos = counts
        rows = [wanted(w, n) for n in range(2)]
        ok = [held(row).astype(jnp.int32) for row in rows]
        single, both = ok[0] + ok[1] == 1, ok[0] + ok[1] == 2
        spot = place(jnp.maximum(jnp.where(ok[0] == 1, rows[0], rows[1]), 0))
        one_list[2 * ones] = w
        one_list[2 * ones + 1] = spot
        two_list[3 * twos] = w
        two_list[3 * twos + 1] = spot
        two_list[3 * twos + 2] = place(jnp.maximum(rows[1], 0))
        return ones + single.astype(jnp.int32), twos + both.astype(jnp.int32)

    ones, twos = lax.fori_loop(0, NX * 8 + 1, note, (0, 0))
    counts_ref[0] = ones
    counts_ref[1] = twos


def plan(ids, my_z, my_x, core):
    smem = pl.BlockSpec(memory_space=pltpu.SMEM)
    return pl.pallas_call(
        plan_kernel,
        in_specs=[smem] * 4,
        out_specs=[smem] * 3,
        out_shape=[
            jax.ShapeDtypeStruct((128,), jnp.int32),
            jax.ShapeDtypeStruct((128,), jnp.int32),
            jax.ShapeDtypeStruct((2,), jnp.int32),
        ],
        name="plan",
    )(ids, my_z, my_x, core)


def window_kernel(layout, one_list, two_list, counts_ref, x_ref, *refs):
    q_refs, refs = refs[:NX], refs[NX:]
    pieces = refs[:len(layout)]
    out_ref = refs[len(layout)]
    table, q_in, qs, outs, stats, sem, q_sem = refs[len(layout) + 1:]
    ones, twos = counts_ref[0], counts_ref[1]
    plane_rows = NX * 1024
    total_rows = qs.shape[0]
    q_copies = [pltpu.make_async_copy(q_refs[d].at[pl.ds(0, 1024)], q_in.at[d], q_sem.at[d]) for d in range(NX)]
    copies = [
        pltpu.make_async_copy(pieces[i], table.at[pl.ds(distance * 512 + first, rows)], sem.at[i])
        for i, (distance, first, rows) in enumerate(layout)
    ]
    for copy in q_copies + copies:
        copy.start()
    outs[...] = jnp.zeros_like(outs)
    stats[...] = jnp.full_like(stats, MASKED)
    qs[0:PAD, :] = jnp.zeros((PAD, HS), F32)
    qs[PAD + plane_rows:, :] = jnp.zeros((total_rows - PAD - plane_rows, HS), F32)
    for d in range(NX):
        q_copies[d].wait()
        first = pl.multiple_of(PAD + jnp.bitwise_and(x_ref[0] + d, NX - 1) * 1024, 8)
        qs[pl.ds(first, 1024), :] = q_in[d].astype(F32)
    for copy in copies:
        copy.wait()

    def attend(items):
        jobs = []
        for start, spots in items:
            for h in range(2):
                q = qs[pl.ds(start + h, GROUP, stride=2), :].astype(BF)
                k = [table[pl.ds(pl.multiple_of(f, ROW), ROW), h * 256:h * 256 + HS] for f in spots]
                k = k[0] if len(k) == 1 else jnp.concatenate(k, axis=0)
                s = lax.dot_general(q, k, (((1,), (1,)), ((), ())), preferred_element_type=F32)
                jobs.append([start + h, h, spots, s])
        for job in jobs:
            job[3] = job[3] * LOG_SCALE
            job.append(jnp.max(job[3], axis=1, keepdims=True))
        for job in jobs:
            job[3] = jnp.exp2(job[3] - job[4])
            job.append(jnp.sum(job[3], axis=1, keepdims=True))
        for first, h, spots, p, m, total in jobs:
            v = [table[pl.ds(pl.multiple_of(f, ROW), ROW), h * 256 + HS:h * 256 + 2 * HS] for f in spots]
            v = v[0] if len(v) == 1 else jnp.concatenate(v, axis=0)
            out = jnp.dot(p.astype(BF), v, preferred_element_type=F32) * (1.0 / total)
            outs[pl.ds(first, GROUP, stride=2), :] = out
            stats[pl.ds(first, GROUP, stride=2), :] = jnp.broadcast_to(m + jnp.log2(total), (GROUP, HS))

    def query_row(w):
        return PAD + 2 * (GROUP * w - 1)

    def one_pair(i, carry):
        items = []
        for lane in range(2):
            at = jnp.minimum(2 * i + lane, ones - 1)
            items.append((query_row(one_list[2 * at]), [one_list[2 * at + 1]]))
        attend(items)
        return carry

    def two(i, carry):
        attend([(query_row(two_list[3 * i]), [two_list[3 * i + 1], two_list[3 * i + 2]])])
        return carry

    lax.fori_loop(0, (ones + 1) // 2, one_pair, 0)
    lax.fori_loop(0, twos, two, 0)
    eye = lax.broadcasted_iota(jnp.int32, (HS, HS), 0) == lax.broadcasted_iota(jnp.int32, (HS, HS), 1)
    for x in range(NX):
        base = PAD + x * 1024
        out_ref[x, 0:1024] = outs[base:base + 1024, :].astype(BF)
        lines = []
        for b in range(8):
            block = stats[base + b * HS:base + (b + 1) * HS, :]
            lines.append(jnp.sum(jnp.where(eye, block, 0.0), axis=0, keepdims=True))
        lse = jnp.concatenate(lines, axis=0)
        high = lse.astype(BF)
        rest = lse - high.astype(F32)
        middle = rest.astype(BF)
        low = (rest - middle.astype(F32)).astype(BF)
        tail = jnp.concatenate([high.astype(F32), middle.astype(F32), low.astype(F32), jnp.zeros((8, HS), F32)], axis=0)
        out_ref[x, 1024:1056] = tail.astype(BF)


def windows(lists, my_x, queries, pieces):
    layout = tuple((d, first, rows) for d, first, rows, _ in pieces)
    total = PAD + NX * 1024 + 2 * GROUP
    smem = pl.BlockSpec(memory_space=pltpu.SMEM)
    return pl.pallas_call(
        functools.partial(window_kernel, layout),
        in_specs=[smem] * 4 + [ANY] * (NX + len(pieces)),
        out_specs=VMEM_ALL,
        scratch_shapes=[
            pltpu.VMEM((NZ * 4 * ROW, 512), BF),
            pltpu.VMEM((NX, 1024, HS), BF),
            pltpu.VMEM((total, HS), F32),
            pltpu.VMEM((total, HS), F32),
            pltpu.VMEM((total, HS), F32),
            pltpu.SemaphoreType.DMA((len(pieces),)),
            pltpu.SemaphoreType.DMA((NX,)),
        ],
        out_shape=jax.ShapeDtypeStruct((NX, 1056, HS), BF),
        cost_estimate=pl.CostEstimate(flops=10**9, bytes_accessed=8 * 2**20, transcendentals=10**6),
        compiler_params=pltpu.CompilerParams(vmem_limit_bytes=58 * MIB),
        name="windows",
    )(*lists, my_x, *queries, *[piece[-1] for piece in pieces])


def combine_kernel(parts_ref, out_ref):
    logs = []
    for x in range(NX):
        tail = parts_ref[x, 1024:1056].astype(F32)
        logs.append(tail[0:8] + tail[8:16] + tail[16:24])
    m = functools.reduce(jnp.maximum, logs)
    weights = [jnp.exp2(v - m) for v in logs]
    inv = 1.0 / functools.reduce(jnp.add, weights)
    weights = [w * inv for w in weights]
    eye = lax.broadcasted_iota(jnp.int32, (HS, HS), 0) == lax.broadcasted_iota(jnp.int32, (HS, HS), 1)
    for b in range(8):
        total = jnp.zeros((HS, HS), F32)
        for x in range(NX):
            line = jnp.broadcast_to(weights[x][b:b + 1, :], (HS, HS))
            column = jnp.sum(jnp.where(eye, line, 0.0), axis=1, keepdims=True)
            total += column * parts_ref[x, b * HS:(b + 1) * HS].astype(F32)
        out_ref[b * HS:(b + 1) * HS, :] = total.astype(BF)


def combine(parts):
    return pl.pallas_call(
        combine_kernel,
        in_specs=[VMEM_ALL],
        out_specs=VMEM_ALL,
        out_shape=jax.ShapeDtypeStruct((1024, HS), BF),
        cost_estimate=pl.CostEstimate(flops=10**7, bytes_accessed=2 * 2**20, transcendentals=0),
        compiler_params=pltpu.CompilerParams(vmem_limit_bytes=8 * MIB),
        name="combine",
    )(parts)


def as_index(*values):
    return jnp.stack(values).astype(jnp.int32)


def on_device(corpus, enc_qkv, enc_out, cca_kv, gain_in, gain_out, queries, nbr_ids):
    width = corpus.shape[2]
    my_z, my_x, my_y, core = (lax.axis_index(a) for a in ("z", "x", "y", "c"))
    corpus_flat = corpus.reshape(-1, width)
    e_own = enc_out.reshape(2 * HS, width)
    e_other = shifted(e_own, "c", 1)

    kv = lax.optimization_barrier(cca_kv.reshape(cca_kv.shape[0], 512))
    kv = spread(kv, "z").reshape(-1, 512)

    w_rows = enc_qkv.transpose(0, 2, 1, 3).reshape(width * 6, HS)
    att_own, att_send = encode(corpus_flat, w_rows, gain_in.reshape(1, width), as_index(core), as_index(my_y))
    nbr_ids, queries, att_send = lax.optimization_barrier((nbr_ids, queries, att_send))
    att_other = shifted(att_send, "c", 1)

    id_rows = jnp.pad(nbr_ids.astype(BF), ((0, 8), (0, HS - 2)))
    q_rows = jnp.concatenate([queries.reshape(1024, HS), id_rows], axis=0)
    qs = [q_rows] + [shifted(q_rows, "x", -d) for d in range(1, NX)]
    terms = project(att_own, att_other, e_own, e_other)

    terms = [terms[0]] + [shifted(terms[k], "y", k) for k in range(1, NY)]
    kv, terms[1] = lax.optimization_barrier((kv, terms[1]))
    terms[2], terms[3], qs = lax.optimization_barrier((terms[2], terms[3], qs))
    got = jnp.stack([q[1024:1032, 0:2] for q in qs]).astype(jnp.int32).reshape(-1)
    below = shifted(got, "z", 1)
    from_left = shifted(kv, "x", 1)
    from_right = shifted(kv, "x", -1)
    from_far = shifted(kv, "x", 2)

    u = normalise(terms, corpus_flat, gain_out.reshape(1, width), as_index(core * NY + my_y))
    us = [u] + [shifted(u, "y", k) for k in range(1, NY)]
    lists = plan(jnp.concatenate([got, below]), as_index(my_z), as_index(my_x), as_index(core))
    weights = [kv, from_left, from_right, from_far]
    us[1], us[3], lists, weights = lax.optimization_barrier((us[1], us[3], lists, weights))
    at = as_index(my_x, my_y)
    memory_own, u_own = memorise(at, us, weights)
    u_other = shifted(u_own, "c", 1)
    pieces = ring_pieces(memory_own, 0)
    (memory_other,) = memorise(at, [u_other], weights)
    pieces += ring_pieces(memory_other, 2 * ROW)

    parts = windows(lists, as_index(my_x), qs, pieces)
    parts = lax.all_to_all(parts, "x", split_axis=0, concat_axis=0, tiled=True)
    return combine(parts).reshape(512, 2, HS)


def solution(mesh):
    inner = Mesh(mesh.devices.reshape(NZ, NX, NY, NC), ("z", "x", "y", "c"))
    seq, head = ("z", "x"), ("y", "c")
    placed = (
        P(seq, None, None),
        P(None, head, None, None),
        P(head, None, None),
        P(seq, head, None, None),
        P(),
        P(),
        P(seq, head, None),
        P(seq, None),
    )
    return jax.shard_map(
        on_device, mesh=inner, in_specs=placed, out_specs=P(seq, head, None), check_vma=False
    )
```

```python
import functools

import jax
import jax.numpy as jnp
from jax import lax
from jax.experimental import pallas as pl
from jax.experimental.pallas import tpu as pltpu
from jax.sharding import Mesh, PartitionSpec as P

GROUP = 64
EPS = 1e-06
MIB = 2**20
NZ, NX, NY, NC = 8, 4, 4, 2
ROW = 128
HS = 128
MASKED = -1e30
LOG_SCALE = HS ** -0.5 * 1.4426950408889634
BF = jnp.bfloat16
F32 = jnp.float32
ANY = pl.BlockSpec(memory_space=pl.ANY)
VMEM_ALL = pl.BlockSpec(memory_space=pltpu.VMEM)


def shifted(value, axis, steps):
    n = lax.axis_size(axis)
    return lax.ppermute(value, axis, [(i, (i + steps) % n) for i in range(n)])


def spread(value, axis):
    n = lax.axis_size(axis)
    copies = jnp.broadcast_to(value[None], (n,) + value.shape)
    return lax.all_to_all(copies, axis, split_axis=0, concat_axis=0, tiled=True)


def encoder_kernel(core_ref, y_ref, x_ref, w_ref, g_ref, own_ref, send_ref, wide, wmat, acc, ssq):
    step = pl.program_id(0)
    depth = x_ref.shape[1]

    @pl.when(step == 0)
    def _():
        acc[...] = jnp.zeros_like(acc)
        ssq[...] = jnp.zeros_like(ssq)

    wide[...] = w_ref[...].astype(F32)
    for col in range(6):
        wmat[:, col * HS:(col + 1) * HS] = wide[pl.ds(col, depth, stride=6), :].astype(BF)
    x = x_ref[...].astype(F32)
    ssq[...] += jnp.sum(x * x, axis=1, keepdims=True)
    xg = (x * g_ref[...]).astype(BF)
    acc[...] += jnp.dot(xg, wmat[...], preferred_element_type=F32)

    @pl.when(step == pl.num_programs(0) - 1)
    def _():
        core, my_y = core_ref[0], y_ref[0]
        done = []
        total = depth * pl.num_programs(0)
        scale = lax.rsqrt(ssq[...] / total + EPS)
        rows = x_ref.shape[0] // ROW
        for pair in range(rows // 2):
            spots = [(r, h) for r in (2 * pair, 2 * pair + 1) for h in range(2)]

            def part(r, col):
                sl = slice(r * ROW, (r + 1) * ROW)
                return (acc[sl, col * HS:(col + 1) * HS] * scale[sl]).astype(BF)

            scores = [
                lax.dot_general(
                    part(r, h), part(r, 2 + h), (((1,), (1,)), ((), ())), preferred_element_type=F32
                ) * LOG_SCALE
                for r, h in spots
            ]
            tops = [jnp.max(s, axis=1, keepdims=True) for s in scores]
            probs = [jnp.exp2(s - m) for s, m in zip(scores, tops)]
            sums = [jnp.sum(p, axis=1, keepdims=True) for p in probs]
            atts = [
                (jnp.dot(p.astype(BF), part(r, 4 + h), preferred_element_type=F32) * (1.0 / total_p)).astype(BF)
                for (r, h), p, total_p in zip(spots, probs, sums)
            ]
            done.append([jnp.concatenate(atts[2 * i:2 * i + 2], axis=1) for i in range(2)])
        for i in range(2):
            own = jnp.where(core == 0, done[0][i], done[1][i])
            send = jnp.where(core == 0, done[1][i], done[0][i])
            for half in range(2):
                k = jnp.bitwise_and(2 * i + half - my_y, NY - 1)
                spot = pl.ds(pl.multiple_of(k * 64, 64), 64)
                own_ref[spot, :] = own[half * 64:(half + 1) * 64]
                send_ref[spot, :] = send[half * 64:(half + 1) * 64]


def encode(corpus_flat, w_rows, gain, core, my_y):
    tokens, width = corpus_flat.shape
    steps = 4
    depth = width // steps
    return pl.pallas_call(
        encoder_kernel,
        grid_spec=pltpu.PrefetchScalarGridSpec(
            num_scalar_prefetch=2,
            grid=(steps,),
            in_specs=[
                pl.BlockSpec((tokens, depth), lambda i, c, y: (0, i)),
                pl.BlockSpec((depth * 6, HS), lambda i, c, y: (i, 0)),
                pl.BlockSpec((1, depth), lambda i, c, y: (0, i)),
            ],
            out_specs=[pl.BlockSpec((2 * ROW, 2 * HS), lambda i, c, y: (0, 0))] * 2,
            scratch_shapes=[
                pltpu.VMEM((depth * 6, HS), F32),
                pltpu.VMEM((depth, 6 * HS), BF),
                pltpu.VMEM((tokens, 6 * HS), F32),
                pltpu.VMEM((tokens, 1), F32),
            ],
        ),
        out_shape=[jax.ShapeDtypeStruct((2 * ROW, 2 * HS), BF)] * 2,
        cost_estimate=pl.CostEstimate(
            flops=2 * tokens * width * 6 * HS, bytes_accessed=(tokens + 768) * width * 2, transcendentals=0
        ),
        compiler_params=pltpu.CompilerParams(vmem_limit_bytes=60 * MIB),
        name="encoder",
    )(core, my_y, corpus_flat, w_rows, gain)


def project_kernel(a_ref, b_ref, ea_ref, eb_ref, *outs):
    rows = a_ref.shape[0] // NY
    value = jnp.dot(a_ref[...], ea_ref[...], preferred_element_type=F32)
    value += jnp.dot(b_ref[...], eb_ref[...], preferred_element_type=F32)
    for k in range(NY):
        outs[k][...] = value[k * rows:(k + 1) * rows].astype(BF)


def project(att, att_other, e_own, e_other):
    tokens, depth = att_other.shape
    width = e_own.shape[1]
    cols = 1024
    rows = tokens // NY
    return pl.pallas_call(
        project_kernel,
        grid=(width // cols,),
        in_specs=[
            pl.BlockSpec((tokens, depth), lambda i: (0, 0)),
            pl.BlockSpec((tokens, depth), lambda i: (0, 0)),
            pl.BlockSpec((depth, cols), lambda i: (0, i)),
            pl.BlockSpec((depth, cols), lambda i: (0, i)),
        ],
        out_specs=[pl.BlockSpec((rows, cols), lambda i: (0, i))] * NY,
        out_shape=[jax.ShapeDtypeStruct((rows, width), BF)] * NY,
        cost_estimate=pl.CostEstimate(
            flops=4 * tokens * depth * width, bytes_accessed=4 * depth * width, transcendentals=0
        ),
        compiler_params=pltpu.CompilerParams(vmem_limit_bytes=60 * MIB),
        name="project",
    )(att, att_other, e_own, e_other)


def norm_kernel(block_ref, t0, t1, t2, t3, x_ref, g_ref, out_ref):
    total = x_ref[...].astype(F32)
    for term in (t0, t1, t2, t3):
        total += term[...].astype(F32)
    rinv = lax.rsqrt(jnp.mean(total * total, axis=1, keepdims=True) + EPS)
    u = (total * rinv * g_ref[...]).astype(BF)
    for z in range(NZ):
        for x in range(NX):
            src, dst = (z * NX + x) * HS, (x * NZ + z) * HS
            out_ref[:, dst:dst + HS] = u[:, src:src + HS]


def normalise(terms, corpus_flat, gain, block):
    rows, width = terms[0].shape
    whole = pl.BlockSpec((rows, width), lambda i, b: (0, 0))
    return pl.pallas_call(
        norm_kernel,
        grid_spec=pltpu.PrefetchScalarGridSpec(
            num_scalar_prefetch=1,
            grid=(1,),
            in_specs=[whole] * NY
            + [
                pl.BlockSpec((rows, width), lambda i, b: (b[0], 0)),
                pl.BlockSpec((1, width), lambda i, b: (0, 0)),
            ],
            out_specs=whole,
        ),
        out_shape=jax.ShapeDtypeStruct((rows, width), BF),
        cost_estimate=pl.CostEstimate(flops=8 * rows * width, bytes_accessed=12 * rows * width, transcendentals=0),
        compiler_params=pltpu.CompilerParams(vmem_limit_bytes=60 * MIB),
        name="normalise",
    )(block, *terms, corpus_flat, gain)


ORDER = (0, NX - 1, 1, 2)


def memory_kernel(parts, at_ref, *refs):
    us = refs[:parts]
    k0, k1, k2, k3, k4 = refs[parts:parts + 5]
    out_ref = refs[parts + 5]
    rest = refs[parts + 6:]
    if parts > 1:
        whole, rest = rest[0], rest[1:]
    ua, kv, sem, out_sem = rest
    depth = NZ * HS
    rows = ua.shape[0] // parts
    u_copies = []
    for k in range(parts):
        first = pl.multiple_of(lax.rem(at_ref[1] - k + parts, parts) * rows, rows)
        u_copies.append(pltpu.make_async_copy(us[k], ua.at[pl.ds(first, rows)], sem.at[k]))
    near = [
        pltpu.make_async_copy(k_ref.at[pl.ds(0, depth)], kv.at[i], sem.at[NY + i])
        for i, k_ref in enumerate((k0, k1, k2))
    ]
    top, bottom = k3.shape[0], depth - k3.shape[0]
    far = [
        pltpu.make_async_copy(k3, kv.at[3, pl.ds(0, top)], sem.at[NY + 3]),
        pltpu.make_async_copy(k4.at[pl.ds(0, bottom)], kv.at[3, pl.ds(top, bottom)], sem.at[NY + 4]),
    ]
    for copy in u_copies + near + far:
        copy.start()
    for copy in u_copies:
        copy.wait()
    if parts > 1:
        back = pltpu.make_async_copy(ua, whole, out_sem)
        back.start()
    total = jnp.zeros(out_ref.shape, F32)
    for i in range(NX):
        for copy in (near[i:i + 1] if i < 3 else far):
            copy.wait()
        first = pl.multiple_of(lax.rem(at_ref[0] + ORDER[i], NX) * depth, depth)
        total += jnp.dot(ua[:, pl.ds(first, depth)], kv[i], preferred_element_type=F32)
    out_ref[...] = total.astype(BF)
    if parts > 1:
        back.wait()


def memorise(at, us, payloads):
    width = us[0].shape[1]
    tokens = us[0].shape[0] * len(us)
    cols = payloads[0].shape[1]
    depth = width // NX
    memory = jax.ShapeDtypeStruct((tokens, cols), BF)
    assembled = [jax.ShapeDtypeStruct((tokens, width), BF)] if len(us) > 1 else []
    return pl.pallas_call(
        functools.partial(memory_kernel, len(us)),
        in_specs=[pl.BlockSpec(memory_space=pltpu.SMEM)] + [ANY] * (len(us) + 5),
        out_specs=[VMEM_ALL] + [ANY] * len(assembled),
        scratch_shapes=[
            pltpu.VMEM((tokens, width), BF),
            pltpu.VMEM((NX, depth, cols), BF),
            pltpu.SemaphoreType.DMA((NY + 5,)),
            pltpu.SemaphoreType.DMA,
        ],
        out_shape=[memory] + assembled,
        cost_estimate=pl.CostEstimate(
            flops=2 * tokens * width * cols, bytes_accessed=2 * width * cols, transcendentals=0
        ),
        compiler_params=pltpu.CompilerParams(vmem_limit_bytes=12 * MIB),
        name="memorise",
    )(at, *us, *payloads)


def ring_pieces(block, base):
    rows = block.shape[0]
    half = rows // 2
    pieces = [(0, base, rows, block)]
    up = down = block
    for s in range(1, NZ // 2):
        up = shifted(up, "z", 1)
        down = shifted(down, "z", -1)
        pieces += [(s, base, rows, up), (NZ - s, base, rows, down)]
    pieces += [
        (NZ // 2, base, half, shifted(up[:half], "z", 1)),
        (NZ // 2, base + half, half, shifted(down[half:], "z", -1)),
    ]
    return pieces


PAD = 8


def plan_kernel(ids_ref, z_ref, x_ref, core_ref, one_list, two_list, counts_ref):
    my_z, my_x, core = z_ref[0], x_ref[0], core_ref[0]

    def held(row):
        return jnp.logical_and(row >= 0, jnp.bitwise_and(jnp.right_shift(row, 2), NX - 1) == my_x)

    def wanted(w, n):
        group = jnp.maximum(w - 1, 0)
        step = jnp.bitwise_and(jnp.right_shift(group, 3) - my_x, NX - 1)
        here = step * 16 + jnp.bitwise_and(group, 7) * 2
        under = NX * 16 + jnp.bitwise_and(NX - 1 - my_x, NX - 1) * 16 + 14
        row = ids_ref[jnp.where(w == 0, under, here) + n]
        return jnp.where(jnp.logical_and(w == 0, my_z == 0), -1, row)

    def place(row):
        distance = jnp.bitwise_and(my_z - jnp.right_shift(row, 4), NZ - 1)
        local = jnp.bitwise_and(row, 3)
        half = jnp.bitwise_and(jnp.right_shift(local, 1) + core, 1)
        return distance * 512 + half * 256 + jnp.bitwise_and(local, 1) * 128

    def note(w, counts):
        ones, twos = counts
        rows = [wanted(w, n) for n in range(2)]
        ok = [held(row).astype(jnp.int32) for row in rows]
        single, both = ok[0] + ok[1] == 1, ok[0] + ok[1] == 2
        spot = place(jnp.maximum(jnp.where(ok[0] == 1, rows[0], rows[1]), 0))
        one_list[2 * ones] = w
        one_list[2 * ones + 1] = spot
        two_list[3 * twos] = w
        two_list[3 * twos + 1] = spot
        two_list[3 * twos + 2] = place(jnp.maximum(rows[1], 0))
        return ones + single.astype(jnp.int32), twos + both.astype(jnp.int32)

    ones, twos = lax.fori_loop(0, NX * 8 + 1, note, (0, 0))
    counts_ref[0] = ones
    counts_ref[1] = twos


def plan(ids, my_z, my_x, core):
    smem = pl.BlockSpec(memory_space=pltpu.SMEM)
    return pl.pallas_call(
        plan_kernel,
        in_specs=[smem] * 4,
        out_specs=[smem] * 3,
        out_shape=[
            jax.ShapeDtypeStruct((128,), jnp.int32),
            jax.ShapeDtypeStruct((128,), jnp.int32),
            jax.ShapeDtypeStruct((2,), jnp.int32),
        ],
        name="plan",
    )(ids, my_z, my_x, core)


def window_kernel(layout, one_list, two_list, counts_ref, x_ref, *refs):
    q_refs, refs = refs[:NX], refs[NX:]
    pieces = refs[:len(layout)]
    out_ref = refs[len(layout)]
    table, q_in, qs, outs, stats, sem, q_sem = refs[len(layout) + 1:]
    ones, twos = counts_ref[0], counts_ref[1]
    plane_rows = NX * 1024
    total_rows = qs.shape[0]
    q_copies = [pltpu.make_async_copy(q_refs[d].at[pl.ds(0, 1024)], q_in.at[d], q_sem.at[d]) for d in range(NX)]
    copies = [
        pltpu.make_async_copy(pieces[i], table.at[pl.ds(distance * 512 + first, rows)], sem.at[i])
        for i, (distance, first, rows) in enumerate(layout)
    ]
    for copy in q_copies + copies:
        copy.start()
    outs[...] = jnp.zeros_like(outs)
    stats[...] = jnp.full_like(stats, MASKED)
    qs[0:PAD, :] = jnp.zeros((PAD, HS), F32)
    qs[PAD + plane_rows:, :] = jnp.zeros((total_rows - PAD - plane_rows, HS), F32)
    for d in range(NX):
        q_copies[d].wait()
        first = pl.multiple_of(PAD + jnp.bitwise_and(x_ref[0] + d, NX - 1) * 1024, 8)
        qs[pl.ds(first, 1024), :] = q_in[d].astype(F32)
    for copy in copies:
        copy.wait()

    def attend(items):
        jobs = []
        for start, spots in items:
            for h in range(2):
                q = qs[pl.ds(start + h, GROUP, stride=2), :].astype(BF)
                k = [table[pl.ds(pl.multiple_of(f, ROW), ROW), h * 256:h * 256 + HS] for f in spots]
                k = k[0] if len(k) == 1 else jnp.concatenate(k, axis=0)
                s = lax.dot_general(q, k, (((1,), (1,)), ((), ())), preferred_element_type=F32)
                jobs.append([start + h, h, spots, s])
        for job in jobs:
            job[3] = job[3] * LOG_SCALE
            job.append(jnp.max(job[3], axis=1, keepdims=True))
        for job in jobs:
            job[3] = jnp.exp2(job[3] - job[4])
            job.append(jnp.sum(job[3], axis=1, keepdims=True))
        for first, h, spots, p, m, total in jobs:
            v = [table[pl.ds(pl.multiple_of(f, ROW), ROW), h * 256 + HS:h * 256 + 2 * HS] for f in spots]
            v = v[0] if len(v) == 1 else jnp.concatenate(v, axis=0)
            out = jnp.dot(p.astype(BF), v, preferred_element_type=F32) * (1.0 / total)
            outs[pl.ds(first, GROUP, stride=2), :] = out
            stats[pl.ds(first, GROUP, stride=2), :] = jnp.broadcast_to(m + jnp.log2(total), (GROUP, HS))

    def query_row(w):
        return PAD + 2 * (GROUP * w - 1)

    def one_pair(i, carry):
        items = []
        for lane in range(2):
            at = jnp.minimum(2 * i + lane, ones - 1)
            items.append((query_row(one_list[2 * at]), [one_list[2 * at + 1]]))
        attend(items)
        return carry

    def two(i, carry):
        attend([(query_row(two_list[3 * i]), [two_list[3 * i + 1], two_list[3 * i + 2]])])
        return carry

    lax.fori_loop(0, (ones + 1) // 2, one_pair, 0)
    lax.fori_loop(0, twos, two, 0)
    eye = lax.broadcasted_iota(jnp.int32, (HS, HS), 0) == lax.broadcasted_iota(jnp.int32, (HS, HS), 1)
    for x in range(NX):
        base = PAD + x * 1024
        out_ref[x, 0:1024] = outs[base:base + 1024, :].astype(BF)
        lines = []
        for b in range(8):
            block = stats[base + b * HS:base + (b + 1) * HS, :]
            lines.append(jnp.sum(jnp.where(eye, block, 0.0), axis=0, keepdims=True))
        lse = jnp.concatenate(lines, axis=0)
        high = lse.astype(BF)
        rest = lse - high.astype(F32)
        middle = rest.astype(BF)
        low = (rest - middle.astype(F32)).astype(BF)
        tail = jnp.concatenate([high.astype(F32), middle.astype(F32), low.astype(F32), jnp.zeros((8, HS), F32)], axis=0)
        out_ref[x, 1024:1056] = tail.astype(BF)


def windows(lists, my_x, queries, pieces):
    layout = tuple((d, first, rows) for d, first, rows, _ in pieces)
    total = PAD + NX * 1024 + 2 * GROUP
    smem = pl.BlockSpec(memory_space=pltpu.SMEM)
    return pl.pallas_call(
        functools.partial(window_kernel, layout),
        in_specs=[smem] * 4 + [ANY] * (NX + len(pieces)),
        out_specs=VMEM_ALL,
        scratch_shapes=[
            pltpu.VMEM((NZ * 4 * ROW, 512), BF),
            pltpu.VMEM((NX, 1024, HS), BF),
            pltpu.VMEM((total, HS), F32),
            pltpu.VMEM((total, HS), F32),
            pltpu.VMEM((total, HS), F32),
            pltpu.SemaphoreType.DMA((len(pieces),)),
            pltpu.SemaphoreType.DMA((NX,)),
        ],
        out_shape=jax.ShapeDtypeStruct((NX, 1056, HS), BF),
        cost_estimate=pl.CostEstimate(flops=10**9, bytes_accessed=8 * 2**20, transcendentals=10**6),
        compiler_params=pltpu.CompilerParams(vmem_limit_bytes=58 * MIB),
        name="windows",
    )(*lists, my_x, *queries, *[piece[-1] for piece in pieces])


def combine_kernel(parts_ref, out_ref):
    logs = []
    for x in range(NX):
        tail = parts_ref[x, 1024:1056].astype(F32)
        logs.append(tail[0:8] + tail[8:16] + tail[16:24])
    m = functools.reduce(jnp.maximum, logs)
    weights = [jnp.exp2(v - m) for v in logs]
    inv = 1.0 / functools.reduce(jnp.add, weights)
    weights = [w * inv for w in weights]
    eye = lax.broadcasted_iota(jnp.int32, (HS, HS), 0) == lax.broadcasted_iota(jnp.int32, (HS, HS), 1)
    for b in range(8):
        total = jnp.zeros((HS, HS), F32)
        for x in range(NX):
            line = jnp.broadcast_to(weights[x][b:b + 1, :], (HS, HS))
            column = jnp.sum(jnp.where(eye, line, 0.0), axis=1, keepdims=True)
            total += column * parts_ref[x, b * HS:(b + 1) * HS].astype(F32)
        out_ref[b * HS:(b + 1) * HS, :] = total.astype(BF)


def combine(parts):
    return pl.pallas_call(
        combine_kernel,
        in_specs=[VMEM_ALL],
        out_specs=VMEM_ALL,
        out_shape=jax.ShapeDtypeStruct((1024, HS), BF),
        cost_estimate=pl.CostEstimate(flops=10**7, bytes_accessed=2 * 2**20, transcendentals=0),
        compiler_params=pltpu.CompilerParams(vmem_limit_bytes=8 * MIB),
        name="combine",
    )(parts)


def as_index(*values):
    return jnp.stack(values).astype(jnp.int32)


def on_device(corpus, enc_qkv, enc_out, cca_kv, gain_in, gain_out, queries, nbr_ids):
    width = corpus.shape[2]
    my_z, my_x, my_y, core = (lax.axis_index(a) for a in ("z", "x", "y", "c"))
    corpus_flat = corpus.reshape(-1, width)
    e_own = enc_out.reshape(2 * HS, width)
    e_other = shifted(e_own, "c", 1)

    kv = lax.optimization_barrier(cca_kv.reshape(cca_kv.shape[0], 512))
    kv = spread(kv, "z").reshape(-1, 512)

    w_rows = enc_qkv.transpose(0, 2, 1, 3).reshape(width * 6, HS)
    att_own, att_send = encode(corpus_flat, w_rows, gain_in.reshape(1, width), as_index(core), as_index(my_y))
    nbr_ids, queries, att_send = lax.optimization_barrier((nbr_ids, queries, att_send))
    att_other = shifted(att_send, "c", 1)

    id_rows = jnp.pad(nbr_ids.astype(BF), ((0, 8), (0, HS - 2)))
    q_rows = jnp.concatenate([queries.reshape(1024, HS), id_rows], axis=0)
    qs = [q_rows] + [shifted(q_rows, "x", -d) for d in range(1, NX)]
    terms = project(att_own, att_other, e_own, e_other)

    terms = [terms[0]] + [shifted(terms[k], "y", k) for k in range(1, NY)]
    kv, terms[1], terms[3], qs = lax.optimization_barrier((kv, terms[1], terms[3], qs))
    got = jnp.stack([q[1024:1032, 0:2] for q in qs]).astype(jnp.int32).reshape(-1)
    below = shifted(got, "z", 1)
    from_left = shifted(kv, "x", 1)
    from_right = shifted(kv, "x", -1)

    u = normalise(terms, corpus_flat, gain_out.reshape(1, width), as_index(core * NY + my_y))
    us = [u] + [shifted(u, "y", k) for k in range(1, NY)]
    lists = plan(jnp.concatenate([got, below]), as_index(my_z), as_index(my_x), as_index(core))
    us[1], from_left, from_right = lax.optimization_barrier((us[1], from_left, from_right))
    half = kv.shape[0] // 2
    far_top = shifted(from_left[:half], "x", 1)
    far_bottom = shifted(from_right[half:], "x", -1)
    weights = [kv, from_left, from_right, far_top, far_bottom]
    us[1], us[3], lists, weights = lax.optimization_barrier((us[1], us[3], lists, weights))
    at = as_index(my_x, my_y)
    memory_own, u_own = memorise(at, us, weights)
    u_other = shifted(u_own, "c", 1)
    pieces = ring_pieces(memory_own, 0)
    (memory_other,) = memorise(at, [u_other], weights)
    pieces += ring_pieces(memory_other, 2 * ROW)

    parts = windows(lists, as_index(my_x), qs, pieces)
    parts = lax.all_to_all(parts, "x", split_axis=0, concat_axis=0, tiled=True)
    return combine(parts).reshape(512, 2, HS)


def solution(mesh):
    inner = Mesh(mesh.devices.reshape(NZ, NX, NY, NC), ("z", "x", "y", "c"))
    seq, head = ("z", "x"), ("y", "c")
    placed = (
        P(seq, None, None),
        P(None, head, None, None),
        P(head, None, None),
        P(seq, head, None, None),
        P(),
        P(),
        P(seq, head, None),
        P(seq, None),
    )
    return jax.shard_map(
        on_device, mesh=inner, in_specs=placed, out_specs=P(seq, head, None), check_vma=False
    )
```

```python
import functools

import jax
import jax.numpy as jnp
from jax import lax
from jax.experimental import pallas as pl
from jax.experimental.pallas import tpu as pltpu
from jax.sharding import Mesh, PartitionSpec as P

GROUP = 64
EPS = 1e-06
MIB = 2**20
NZ, NX, NY, NC = 8, 4, 4, 2
ROW = 128
HS = 128
MASKED = -1e30
LOG_SCALE = HS ** -0.5 * 1.4426950408889634
BF = jnp.bfloat16
F32 = jnp.float32
ANY = pl.BlockSpec(memory_space=pl.ANY)
VMEM_ALL = pl.BlockSpec(memory_space=pltpu.VMEM)


def shifted(value, axis, steps):
    n = lax.axis_size(axis)
    return lax.ppermute(value, axis, [(i, (i + steps) % n) for i in range(n)])


def spread(value, axis):
    n = lax.axis_size(axis)
    copies = jnp.broadcast_to(value[None], (n,) + value.shape)
    return lax.all_to_all(copies, axis, split_axis=0, concat_axis=0, tiled=True)


def encoder_kernel(core_ref, y_ref, x_ref, w_ref, g_ref, own_ref, send_ref, wide, wmat, acc, ssq):
    step = pl.program_id(0)
    depth = x_ref.shape[1]

    @pl.when(step == 0)
    def _():
        acc[...] = jnp.zeros_like(acc)
        ssq[...] = jnp.zeros_like(ssq)

    wide[...] = w_ref[...].astype(F32)
    for col in range(6):
        wmat[:, col * HS:(col + 1) * HS] = wide[pl.ds(col, depth, stride=6), :].astype(BF)
    x = x_ref[...].astype(F32)
    ssq[...] += jnp.sum(x * x, axis=1, keepdims=True)
    xg = (x * g_ref[...]).astype(BF)
    acc[...] += jnp.dot(xg, wmat[...], preferred_element_type=F32)

    @pl.when(step == pl.num_programs(0) - 1)
    def _():
        core, my_y = core_ref[0], y_ref[0]
        done = []
        total = depth * pl.num_programs(0)
        scale = lax.rsqrt(ssq[...] / total + EPS)
        rows = x_ref.shape[0] // ROW
        for pair in range(rows // 2):
            spots = [(r, h) for r in (2 * pair, 2 * pair + 1) for h in range(2)]

            def part(r, col):
                sl = slice(r * ROW, (r + 1) * ROW)
                return (acc[sl, col * HS:(col + 1) * HS] * scale[sl]).astype(BF)

            scores = [
                lax.dot_general(
                    part(r, h), part(r, 2 + h), (((1,), (1,)), ((), ())), preferred_element_type=F32
                ) * LOG_SCALE
                for r, h in spots
            ]
            tops = [jnp.max(s, axis=1, keepdims=True) for s in scores]
            probs = [jnp.exp2(s - m) for s, m in zip(scores, tops)]
            sums = [jnp.sum(p, axis=1, keepdims=True) for p in probs]
            atts = [
                (jnp.dot(p.astype(BF), part(r, 4 + h), preferred_element_type=F32) * (1.0 / total_p)).astype(BF)
                for (r, h), p, total_p in zip(spots, probs, sums)
            ]
            done.append([jnp.concatenate(atts[2 * i:2 * i + 2], axis=1) for i in range(2)])
        for i in range(2):
            own = jnp.where(core == 0, done[0][i], done[1][i])
            send = jnp.where(core == 0, done[1][i], done[0][i])
            for half in range(2):
                k = jnp.bitwise_and(2 * i + half - my_y, NY - 1)
                spot = pl.ds(pl.multiple_of(k * 64, 64), 64)
                own_ref[spot, :] = own[half * 64:(half + 1) * 64]
                send_ref[spot, :] = send[half * 64:(half + 1) * 64]


def encode(corpus_flat, w_rows, gain, core, my_y):
    tokens, width = corpus_flat.shape
    steps = 4
    depth = width // steps
    return pl.pallas_call(
        encoder_kernel,
        grid_spec=pltpu.PrefetchScalarGridSpec(
            num_scalar_prefetch=2,
            grid=(steps,),
            in_specs=[
                pl.BlockSpec((tokens, depth), lambda i, c, y: (0, i)),
                pl.BlockSpec((depth * 6, HS), lambda i, c, y: (i, 0)),
                pl.BlockSpec((1, depth), lambda i, c, y: (0, i)),
            ],
            out_specs=[pl.BlockSpec((2 * ROW, 2 * HS), lambda i, c, y: (0, 0))] * 2,
            scratch_shapes=[
                pltpu.VMEM((depth * 6, HS), F32),
                pltpu.VMEM((depth, 6 * HS), BF),
                pltpu.VMEM((tokens, 6 * HS), F32),
                pltpu.VMEM((tokens, 1), F32),
            ],
        ),
        out_shape=[jax.ShapeDtypeStruct((2 * ROW, 2 * HS), BF)] * 2,
        cost_estimate=pl.CostEstimate(
            flops=2 * tokens * width * 6 * HS, bytes_accessed=(tokens + 768) * width * 2, transcendentals=0
        ),
        compiler_params=pltpu.CompilerParams(vmem_limit_bytes=60 * MIB),
        name="encoder",
    )(core, my_y, corpus_flat, w_rows, gain)


def project_kernel(a_ref, b_ref, ea_ref, eb_ref, *outs):
    rows = a_ref.shape[0] // NY
    value = jnp.dot(a_ref[...], ea_ref[...], preferred_element_type=F32)
    value += jnp.dot(b_ref[...], eb_ref[...], preferred_element_type=F32)
    for k in range(NY):
        outs[k][...] = value[k * rows:(k + 1) * rows].astype(BF)


def project(att, att_other, e_own, e_other):
    tokens, depth = att_other.shape
    width = e_own.shape[1]
    cols = 1024
    rows = tokens // NY
    return pl.pallas_call(
        project_kernel,
        grid=(width // cols,),
        in_specs=[
            pl.BlockSpec((tokens, depth), lambda i: (0, 0)),
            pl.BlockSpec((tokens, depth), lambda i: (0, 0)),
            pl.BlockSpec((depth, cols), lambda i: (0, i)),
            pl.BlockSpec((depth, cols), lambda i: (0, i)),
        ],
        out_specs=[pl.BlockSpec((rows, cols), lambda i: (0, i))] * NY,
        out_shape=[jax.ShapeDtypeStruct((rows, width), BF)] * NY,
        cost_estimate=pl.CostEstimate(
            flops=4 * tokens * depth * width, bytes_accessed=4 * depth * width, transcendentals=0
        ),
        compiler_params=pltpu.CompilerParams(vmem_limit_bytes=60 * MIB),
        name="project",
    )(att, att_other, e_own, e_other)


def norm_kernel(block_ref, t0, t1, t2, t3, x_ref, g_ref, out_ref):
    total = x_ref[...].astype(F32)
    for term in (t0, t1, t2, t3):
        total += term[...].astype(F32)
    rinv = lax.rsqrt(jnp.mean(total * total, axis=1, keepdims=True) + EPS)
    u = (total * rinv * g_ref[...]).astype(BF)
    for z in range(NZ):
        for x in range(NX):
            src, dst = (z * NX + x) * HS, (x * NZ + z) * HS
            out_ref[:, dst:dst + HS] = u[:, src:src + HS]


def normalise(terms, corpus_flat, gain, block):
    rows, width = terms[0].shape
    whole = pl.BlockSpec((rows, width), lambda i, b: (0, 0))
    return pl.pallas_call(
        norm_kernel,
        grid_spec=pltpu.PrefetchScalarGridSpec(
            num_scalar_prefetch=1,
            grid=(1,),
            in_specs=[whole] * NY
            + [
                pl.BlockSpec((rows, width), lambda i, b: (b[0], 0)),
                pl.BlockSpec((1, width), lambda i, b: (0, 0)),
            ],
            out_specs=whole,
        ),
        out_shape=jax.ShapeDtypeStruct((rows, width), BF),
        cost_estimate=pl.CostEstimate(flops=8 * rows * width, bytes_accessed=12 * rows * width, transcendentals=0),
        compiler_params=pltpu.CompilerParams(vmem_limit_bytes=60 * MIB),
        name="normalise",
    )(block, *terms, corpus_flat, gain)


ORDER = (0, NX - 1, 1, 2)


def memory_kernel(parts, at_ref, *refs):
    us = refs[:parts]
    k0, k1, k2, k3, k4 = refs[parts:parts + 5]
    out_ref = refs[parts + 5]
    rest = refs[parts + 6:]
    if parts > 1:
        whole, rest = rest[0], rest[1:]
    ua, kv, sem, out_sem = rest
    depth = NZ * HS
    rows = ua.shape[0] // parts
    u_copies = []
    for k in range(parts):
        first = pl.multiple_of(lax.rem(at_ref[1] - k + parts, parts) * rows, rows)
        u_copies.append(pltpu.make_async_copy(us[k], ua.at[pl.ds(first, rows)], sem.at[k]))
    near = [
        pltpu.make_async_copy(k_ref.at[pl.ds(0, depth)], kv.at[i], sem.at[NY + i])
        for i, k_ref in enumerate((k0, k1, k2))
    ]
    top, bottom = k3.shape[0], depth - k3.shape[0]
    far = [
        pltpu.make_async_copy(k3, kv.at[3, pl.ds(0, top)], sem.at[NY + 3]),
        pltpu.make_async_copy(k4.at[pl.ds(0, bottom)], kv.at[3, pl.ds(top, bottom)], sem.at[NY + 4]),
    ]
    for copy in u_copies + near + far:
        copy.start()
    for copy in u_copies:
        copy.wait()
    if parts > 1:
        back = pltpu.make_async_copy(ua, whole, out_sem)
        back.start()
    total = jnp.zeros(out_ref.shape, F32)
    for i in range(NX):
        for copy in (near[i:i + 1] if i < 3 else far):
            copy.wait()
        first = pl.multiple_of(lax.rem(at_ref[0] + ORDER[i], NX) * depth, depth)
        total += jnp.dot(ua[:, pl.ds(first, depth)], kv[i], preferred_element_type=F32)
    out_ref[...] = total.astype(BF)
    if parts > 1:
        back.wait()


def memorise(at, us, payloads):
    width = us[0].shape[1]
    tokens = us[0].shape[0] * len(us)
    cols = payloads[0].shape[1]
    depth = width // NX
    memory = jax.ShapeDtypeStruct((tokens, cols), BF)
    assembled = [jax.ShapeDtypeStruct((tokens, width), BF)] if len(us) > 1 else []
    return pl.pallas_call(
        functools.partial(memory_kernel, len(us)),
        in_specs=[pl.BlockSpec(memory_space=pltpu.SMEM)] + [ANY] * (len(us) + 5),
        out_specs=[VMEM_ALL] + [ANY] * len(assembled),
        scratch_shapes=[
            pltpu.VMEM((tokens, width), BF),
            pltpu.VMEM((NX, depth, cols), BF),
            pltpu.SemaphoreType.DMA((NY + 5,)),
            pltpu.SemaphoreType.DMA,
        ],
        out_shape=[memory] + assembled,
        cost_estimate=pl.CostEstimate(
            flops=2 * tokens * width * cols, bytes_accessed=2 * width * cols, transcendentals=0
        ),
        compiler_params=pltpu.CompilerParams(vmem_limit_bytes=12 * MIB),
        name="memorise",
    )(at, *us, *payloads)


def ring_pieces(block, base):
    rows = block.shape[0]
    half = rows // 2
    pieces = [(0, base, rows, block)]
    up = down = block
    for s in range(1, NZ // 2):
        up = shifted(up, "z", 1)
        down = shifted(down, "z", -1)
        pieces += [(s, base, rows, up), (NZ - s, base, rows, down)]
    pieces += [
        (NZ // 2, base, half, shifted(up[:half], "z", 1)),
        (NZ // 2, base + half, half, shifted(down[half:], "z", -1)),
    ]
    return pieces


PAD = 8


def plan_kernel(ids_ref, z_ref, x_ref, core_ref, one_list, two_list, counts_ref):
    my_z, my_x, core = z_ref[0], x_ref[0], core_ref[0]

    def held(row):
        return jnp.logical_and(row >= 0, jnp.bitwise_and(jnp.right_shift(row, 2), NX - 1) == my_x)

    def wanted(w, n):
        group = jnp.maximum(w - 1, 0)
        step = jnp.bitwise_and(jnp.right_shift(group, 3) - my_x, NX - 1)
        here = step * 16 + jnp.bitwise_and(group, 7) * 2
        under = NX * 16 + jnp.bitwise_and(NX - 1 - my_x, NX - 1) * 16 + 14
        row = ids_ref[jnp.where(w == 0, under, here) + n]
        return jnp.where(jnp.logical_and(w == 0, my_z == 0), -1, row)

    def place(row):
        distance = jnp.bitwise_and(my_z - jnp.right_shift(row, 4), NZ - 1)
        local = jnp.bitwise_and(row, 3)
        half = jnp.bitwise_and(jnp.right_shift(local, 1) + core, 1)
        return distance * 512 + half * 256 + jnp.bitwise_and(local, 1) * 128

    def note(w, counts):
        ones, twos = counts
        rows = [wanted(w, n) for n in range(2)]
        ok = [held(row).astype(jnp.int32) for row in rows]
        single, both = ok[0] + ok[1] == 1, ok[0] + ok[1] == 2
        spot = place(jnp.maximum(jnp.where(ok[0] == 1, rows[0], rows[1]), 0))
        one_list[2 * ones] = w
        one_list[2 * ones + 1] = spot
        two_list[3 * twos] = w
        two_list[3 * twos + 1] = spot
        two_list[3 * twos + 2] = place(jnp.maximum(rows[1], 0))
        return ones + single.astype(jnp.int32), twos + both.astype(jnp.int32)

    ones, twos = lax.fori_loop(0, NX * 8 + 1, note, (0, 0))
    counts_ref[0] = ones
    counts_ref[1] = twos


def plan(ids, my_z, my_x, core):
    smem = pl.BlockSpec(memory_space=pltpu.SMEM)
    return pl.pallas_call(
        plan_kernel,
        in_specs=[smem] * 4,
        out_specs=[smem] * 3,
        out_shape=[
            jax.ShapeDtypeStruct((128,), jnp.int32),
            jax.ShapeDtypeStruct((128,), jnp.int32),
            jax.ShapeDtypeStruct((2,), jnp.int32),
        ],
        name="plan",
    )(ids, my_z, my_x, core)


def window_kernel(layout, one_list, two_list, counts_ref, x_ref, *refs):
    q_refs, refs = refs[:NX], refs[NX:]
    pieces = refs[:len(layout)]
    out_ref = refs[len(layout)]
    table, q_in, qs, outs, stats, sem, q_sem = refs[len(layout) + 1:]
    ones, twos = counts_ref[0], counts_ref[1]
    plane_rows = NX * 1024
    total_rows = qs.shape[0]
    q_copies = [pltpu.make_async_copy(q_refs[d].at[pl.ds(0, 1024)], q_in.at[d], q_sem.at[d]) for d in range(NX)]
    copies = [
        pltpu.make_async_copy(pieces[i], table.at[pl.ds(distance * 512 + first, rows)], sem.at[i])
        for i, (distance, first, rows) in enumerate(layout)
    ]
    for copy in q_copies + copies:
        copy.start()
    outs[...] = jnp.zeros_like(outs)
    stats[...] = jnp.full_like(stats, MASKED)
    qs[0:PAD, :] = jnp.zeros((PAD, HS), F32)
    qs[PAD + plane_rows:, :] = jnp.zeros((total_rows - PAD - plane_rows, HS), F32)
    for d in range(NX):
        q_copies[d].wait()
        first = pl.multiple_of(PAD + jnp.bitwise_and(x_ref[0] + d, NX - 1) * 1024, 8)
        qs[pl.ds(first, 1024), :] = q_in[d].astype(F32)
    for copy in copies:
        copy.wait()

    def attend(items):
        jobs = []
        for start, spots in items:
            for h in range(2):
                q = qs[pl.ds(start + h, GROUP, stride=2), :].astype(BF)
                k = [table[pl.ds(pl.multiple_of(f, ROW), ROW), h * 256:h * 256 + HS] for f in spots]
                k = k[0] if len(k) == 1 else jnp.concatenate(k, axis=0)
                s = lax.dot_general(q, k, (((1,), (1,)), ((), ())), preferred_element_type=F32)
                jobs.append([start + h, h, spots, s])
        for job in jobs:
            job[3] = job[3] * LOG_SCALE
            job.append(jnp.max(job[3], axis=1, keepdims=True))
        for job in jobs:
            job[3] = jnp.exp2(job[3] - job[4])
            job.append(jnp.sum(job[3], axis=1, keepdims=True))
        for first, h, spots, p, m, total in jobs:
            v = [table[pl.ds(pl.multiple_of(f, ROW), ROW), h * 256 + HS:h * 256 + 2 * HS] for f in spots]
            v = v[0] if len(v) == 1 else jnp.concatenate(v, axis=0)
            out = jnp.dot(p.astype(BF), v, preferred_element_type=F32) * (1.0 / total)
            outs[pl.ds(first, GROUP, stride=2), :] = out
            stats[pl.ds(first, GROUP, stride=2), :] = jnp.broadcast_to(m + jnp.log2(total), (GROUP, HS))

    def query_row(w):
        return PAD + 2 * (GROUP * w - 1)

    def one_pair(i, carry):
        items = []
        for lane in range(2):
            at = jnp.minimum(2 * i + lane, ones - 1)
            items.append((query_row(one_list[2 * at]), [one_list[2 * at + 1]]))
        attend(items)
        return carry

    def two(i, carry):
        attend([(query_row(two_list[3 * i]), [two_list[3 * i + 1], two_list[3 * i + 2]])])
        return carry

    lax.fori_loop(0, (ones + 1) // 2, one_pair, 0)
    lax.fori_loop(0, twos, two, 0)
    eye = lax.broadcasted_iota(jnp.int32, (HS, HS), 0) == lax.broadcasted_iota(jnp.int32, (HS, HS), 1)
    for x in range(NX):
        base = PAD + x * 1024
        out_ref[x, 0:1024] = outs[base:base + 1024, :].astype(BF)
        lines = []
        for b in range(8):
            block = stats[base + b * HS:base + (b + 1) * HS, :]
            lines.append(jnp.sum(jnp.where(eye, block, 0.0), axis=0, keepdims=True))
        lse = jnp.concatenate(lines, axis=0)
        high = lse.astype(BF)
        rest = lse - high.astype(F32)
        middle = rest.astype(BF)
        low = (rest - middle.astype(F32)).astype(BF)
        tail = jnp.concatenate([high.astype(F32), middle.astype(F32), low.astype(F32), jnp.zeros((8, HS), F32)], axis=0)
        out_ref[x, 1024:1056] = tail.astype(BF)


def windows(lists, my_x, queries, pieces):
    layout = tuple((d, first, rows) for d, first, rows, _ in pieces)
    total = PAD + NX * 1024 + 2 * GROUP
    smem = pl.BlockSpec(memory_space=pltpu.SMEM)
    return pl.pallas_call(
        functools.partial(window_kernel, layout),
        in_specs=[smem] * 4 + [ANY] * (NX + len(pieces)),
        out_specs=VMEM_ALL,
        scratch_shapes=[
            pltpu.VMEM((NZ * 4 * ROW, 512), BF),
            pltpu.VMEM((NX, 1024, HS), BF),
            pltpu.VMEM((total, HS), F32),
            pltpu.VMEM((total, HS), F32),
            pltpu.VMEM((total, HS), F32),
            pltpu.SemaphoreType.DMA((len(pieces),)),
            pltpu.SemaphoreType.DMA((NX,)),
        ],
        out_shape=jax.ShapeDtypeStruct((NX, 1056, HS), BF),
        cost_estimate=pl.CostEstimate(flops=10**9, bytes_accessed=8 * 2**20, transcendentals=10**6),
        compiler_params=pltpu.CompilerParams(vmem_limit_bytes=58 * MIB),
        name="windows",
    )(*lists, my_x, *queries, *[piece[-1] for piece in pieces])


def combine_kernel(parts_ref, out_ref):
    logs = []
    for x in range(NX):
        tail = parts_ref[x, 1024:1056].astype(F32)
        logs.append(tail[0:8] + tail[8:16] + tail[16:24])
    m = functools.reduce(jnp.maximum, logs)
    weights = [jnp.exp2(v - m) for v in logs]
    inv = 1.0 / functools.reduce(jnp.add, weights)
    weights = [w * inv for w in weights]
    eye = lax.broadcasted_iota(jnp.int32, (HS, HS), 0) == lax.broadcasted_iota(jnp.int32, (HS, HS), 1)
    for b in range(8):
        total = jnp.zeros((HS, HS), F32)
        for x in range(NX):
            line = jnp.broadcast_to(weights[x][b:b + 1, :], (HS, HS))
            column = jnp.sum(jnp.where(eye, line, 0.0), axis=1, keepdims=True)
            total += column * parts_ref[x, b * HS:(b + 1) * HS].astype(F32)
        out_ref[b * HS:(b + 1) * HS, :] = total.astype(BF)


def combine(parts):
    return pl.pallas_call(
        combine_kernel,
        in_specs=[VMEM_ALL],
        out_specs=VMEM_ALL,
        out_shape=jax.ShapeDtypeStruct((1024, HS), BF),
        cost_estimate=pl.CostEstimate(flops=10**7, bytes_accessed=2 * 2**20, transcendentals=0),
        compiler_params=pltpu.CompilerParams(vmem_limit_bytes=8 * MIB),
        name="combine",
    )(parts)


def as_index(*values):
    return jnp.stack(values).astype(jnp.int32)


def on_device(corpus, enc_qkv, enc_out, cca_kv, gain_in, gain_out, queries, nbr_ids):
    width = corpus.shape[2]
    my_z, my_x, my_y, core = (lax.axis_index(a) for a in ("z", "x", "y", "c"))
    corpus_flat = corpus.reshape(-1, width)
    e_own = enc_out.reshape(2 * HS, width)
    e_other = shifted(e_own, "c", 1)

    kv = lax.optimization_barrier(cca_kv.reshape(cca_kv.shape[0], 512))
    kv = spread(kv, "z").reshape(-1, 512)

    w_rows = enc_qkv.transpose(0, 2, 1, 3).reshape(width * 6, HS)
    att_own, att_send = encode(corpus_flat, w_rows, gain_in.reshape(1, width), as_index(core), as_index(my_y))
    nbr_ids, queries, att_send = lax.optimization_barrier((nbr_ids, queries, att_send))
    att_other = shifted(att_send, "c", 1)

    id_rows = jnp.pad(nbr_ids.astype(BF), ((0, 8), (0, HS - 2)))
    q_rows = jnp.concatenate([queries.reshape(1024, HS), id_rows], axis=0)
    qs = [q_rows] + [shifted(q_rows, "x", -d) for d in range(1, NX)]
    terms = project(att_own, att_other, e_own, e_other)

    terms = [terms[0]] + [shifted(terms[k], "y", k) for k in range(1, NY)]
    kv, terms[1], terms[3], qs = lax.optimization_barrier((kv, terms[1], terms[3], qs))
    got = jnp.stack([q[1024:1032, 0:2] for q in qs]).astype(jnp.int32).reshape(-1)
    below = shifted(got, "z", 1)
    from_left = shifted(kv, "x", 1)
    from_right = shifted(kv, "x", -1)

    u = normalise(terms, corpus_flat, gain_out.reshape(1, width), as_index(core * NY + my_y))
    us = [u] + [shifted(u, "y", k) for k in range(1, NY)]
    lists = plan(jnp.concatenate([got, below]), as_index(my_z), as_index(my_x), as_index(core))
    us[1], lists, from_left, from_right = lax.optimization_barrier((us[1], lists, from_left, from_right))
    half = kv.shape[0] // 2
    far_top = shifted(from_left[:half], "x", 1)
    far_bottom = shifted(from_right[half:], "x", -1)
    weights = [kv, from_left, from_right, far_top, far_bottom]
    us[1], us[3], lists, weights = lax.optimization_barrier((us[1], us[3], lists, weights))
    at = as_index(my_x, my_y)
    memory_own, u_own = memorise(at, us, weights)
    u_other = shifted(u_own, "c", 1)
    pieces = ring_pieces(memory_own, 0)
    (memory_other,) = memorise(at, [u_other], weights)
    pieces += ring_pieces(memory_other, 2 * ROW)

    parts = windows(lists, as_index(my_x), qs, pieces)
    parts = lax.all_to_all(parts, "x", split_axis=0, concat_axis=0, tiled=True)
    return combine(parts).reshape(512, 2, HS)


def solution(mesh):
    inner = Mesh(mesh.devices.reshape(NZ, NX, NY, NC), ("z", "x", "y", "c"))
    seq, head = ("z", "x"), ("y", "c")
    placed = (
        P(seq, None, None),
        P(None, head, None, None),
        P(head, None, None),
        P(seq, head, None, None),
        P(),
        P(),
        P(seq, head, None),
        P(seq, None),
    )
    return jax.shard_map(
        on_device, mesh=inner, in_specs=placed, out_specs=P(seq, head, None), check_vma=False
    )
```

```python
import functools

import jax
import jax.numpy as jnp
from jax import lax
from jax.experimental import pallas as pl
from jax.experimental.pallas import tpu as pltpu
from jax.sharding import Mesh, PartitionSpec as P

GROUP = 64
EPS = 1e-06
MIB = 2**20
NZ, NX, NY, NC = 8, 4, 4, 2
ROW = 128
HS = 128
MASKED = -1e30
LOG_SCALE = HS ** -0.5 * 1.4426950408889634
BF = jnp.bfloat16
F32 = jnp.float32
ANY = pl.BlockSpec(memory_space=pl.ANY)
VMEM_ALL = pl.BlockSpec(memory_space=pltpu.VMEM)


def shifted(value, axis, steps):
    n = lax.axis_size(axis)
    return lax.ppermute(value, axis, [(i, (i + steps) % n) for i in range(n)])


def spread(value, axis):
    n = lax.axis_size(axis)
    copies = jnp.broadcast_to(value[None], (n,) + value.shape)
    return lax.all_to_all(copies, axis, split_axis=0, concat_axis=0, tiled=True)


def encoder_kernel(core_ref, y_ref, x_ref, w_ref, g_ref, own_ref, send_ref, wide, wmat, acc, ssq):
    step = pl.program_id(0)
    depth = x_ref.shape[1]

    @pl.when(step == 0)
    def _():
        acc[...] = jnp.zeros_like(acc)
        ssq[...] = jnp.zeros_like(ssq)

    wide[...] = w_ref[...].astype(F32)
    for col in range(6):
        wmat[:, col * HS:(col + 1) * HS] = wide[pl.ds(col, depth, stride=6), :].astype(BF)
    x = x_ref[...].astype(F32)
    ssq[...] += jnp.sum(x * x, axis=1, keepdims=True)
    xg = (x * g_ref[...]).astype(BF)
    acc[...] += jnp.dot(xg, wmat[...], preferred_element_type=F32)

    @pl.when(step == pl.num_programs(0) - 1)
    def _():
        core, my_y = core_ref[0], y_ref[0]
        done = []
        total = depth * pl.num_programs(0)
        scale = lax.rsqrt(ssq[...] / total + EPS)
        rows = x_ref.shape[0] // ROW
        for pair in range(rows // 2):
            spots = [(r, h) for r in (2 * pair, 2 * pair + 1) for h in range(2)]

            def part(r, col):
                sl = slice(r * ROW, (r + 1) * ROW)
                return (acc[sl, col * HS:(col + 1) * HS] * scale[sl]).astype(BF)

            scores = [
                lax.dot_general(
                    part(r, h), part(r, 2 + h), (((1,), (1,)), ((), ())), preferred_element_type=F32
                ) * LOG_SCALE
                for r, h in spots
            ]
            tops = [jnp.max(s, axis=1, keepdims=True) for s in scores]
            probs = [jnp.exp2(s - m) for s, m in zip(scores, tops)]
            sums = [jnp.sum(p, axis=1, keepdims=True) for p in probs]
            atts = [
                (jnp.dot(p.astype(BF), part(r, 4 + h), preferred_element_type=F32) * (1.0 / total_p)).astype(BF)
                for (r, h), p, total_p in zip(spots, probs, sums)
            ]
            done.append([jnp.concatenate(atts[2 * i:2 * i + 2], axis=1) for i in range(2)])
        for i in range(2):
            own = jnp.where(core == 0, done[0][i], done[1][i])
            send = jnp.where(core == 0, done[1][i], done[0][i])
            for half in range(2):
                k = jnp.bitwise_and(2 * i + half - my_y, NY - 1)
                spot = pl.ds(pl.multiple_of(k * 64, 64), 64)
                own_ref[spot, :] = own[half * 64:(half + 1) * 64]
                send_ref[spot, :] = send[half * 64:(half + 1) * 64]


def encode(corpus_flat, w_rows, gain, core, my_y):
    tokens, width = corpus_flat.shape
    steps = 4
    depth = width // steps
    return pl.pallas_call(
        encoder_kernel,
        grid_spec=pltpu.PrefetchScalarGridSpec(
            num_scalar_prefetch=2,
            grid=(steps,),
            in_specs=[
                pl.BlockSpec((tokens, depth), lambda i, c, y: (0, i)),
                pl.BlockSpec((depth * 6, HS), lambda i, c, y: (i, 0)),
                pl.BlockSpec((1, depth), lambda i, c, y: (0, i)),
            ],
            out_specs=[pl.BlockSpec((2 * ROW, 2 * HS), lambda i, c, y: (0, 0))] * 2,
            scratch_shapes=[
                pltpu.VMEM((depth * 6, HS), F32),
                pltpu.VMEM((depth, 6 * HS), BF),
                pltpu.VMEM((tokens, 6 * HS), F32),
                pltpu.VMEM((tokens, 1), F32),
            ],
        ),
        out_shape=[jax.ShapeDtypeStruct((2 * ROW, 2 * HS), BF)] * 2,
        cost_estimate=pl.CostEstimate(
            flops=2 * tokens * width * 6 * HS, bytes_accessed=(tokens + 768) * width * 2, transcendentals=0
        ),
        compiler_params=pltpu.CompilerParams(vmem_limit_bytes=60 * MIB),
        name="encoder",
    )(core, my_y, corpus_flat, w_rows, gain)


def project_kernel(a_ref, b_ref, ea_ref, eb_ref, *outs):
    rows = a_ref.shape[0] // NY
    value = jnp.dot(a_ref[...], ea_ref[...], preferred_element_type=F32)
    value += jnp.dot(b_ref[...], eb_ref[...], preferred_element_type=F32)
    for k in range(NY):
        outs[k][...] = value[k * rows:(k + 1) * rows].astype(BF)


def project(att, att_other, e_own, e_other):
    tokens, depth = att_other.shape
    width = e_own.shape[1]
    cols = 1024
    rows = tokens // NY
    return pl.pallas_call(
        project_kernel,
        grid=(width // cols,),
        in_specs=[
            pl.BlockSpec((tokens, depth), lambda i: (0, 0)),
            pl.BlockSpec((tokens, depth), lambda i: (0, 0)),
            pl.BlockSpec((depth, cols), lambda i: (0, i)),
            pl.BlockSpec((depth, cols), lambda i: (0, i)),
        ],
        out_specs=[pl.BlockSpec((rows, cols), lambda i: (0, i))] * NY,
        out_shape=[jax.ShapeDtypeStruct((rows, width), BF)] * NY,
        cost_estimate=pl.CostEstimate(
            flops=4 * tokens * depth * width, bytes_accessed=4 * depth * width, transcendentals=0
        ),
        compiler_params=pltpu.CompilerParams(vmem_limit_bytes=60 * MIB),
        name="project",
    )(att, att_other, e_own, e_other)


def norm_kernel(block_ref, t0, t1, t2, t3, x_ref, g_ref, out_ref):
    total = x_ref[...].astype(F32)
    for term in (t0, t1, t2, t3):
        total += term[...].astype(F32)
    rinv = lax.rsqrt(jnp.mean(total * total, axis=1, keepdims=True) + EPS)
    u = (total * rinv * g_ref[...]).astype(BF)
    for z in range(NZ):
        for x in range(NX):
            src, dst = (z * NX + x) * HS, (x * NZ + z) * HS
            out_ref[:, dst:dst + HS] = u[:, src:src + HS]


def normalise(terms, corpus_flat, gain, block):
    rows, width = terms[0].shape
    whole = pl.BlockSpec((rows, width), lambda i, b: (0, 0))
    return pl.pallas_call(
        norm_kernel,
        grid_spec=pltpu.PrefetchScalarGridSpec(
            num_scalar_prefetch=1,
            grid=(1,),
            in_specs=[whole] * NY
            + [
                pl.BlockSpec((rows, width), lambda i, b: (b[0], 0)),
                pl.BlockSpec((1, width), lambda i, b: (0, 0)),
            ],
            out_specs=whole,
        ),
        out_shape=jax.ShapeDtypeStruct((rows, width), BF),
        cost_estimate=pl.CostEstimate(flops=8 * rows * width, bytes_accessed=12 * rows * width, transcendentals=0),
        compiler_params=pltpu.CompilerParams(vmem_limit_bytes=60 * MIB),
        name="normalise",
    )(block, *terms, corpus_flat, gain)


ORDER = (0, NX - 1, 1, 2)


def memory_kernel(parts, at_ref, *refs):
    us = refs[:parts]
    k0, k1, k2, k3, k4 = refs[parts:parts + 5]
    out_ref = refs[parts + 5]
    rest = refs[parts + 6:]
    if parts > 1:
        whole, rest = rest[0], rest[1:]
    ua, kv, sem, out_sem = rest
    depth = NZ * HS
    rows = ua.shape[0] // parts
    u_copies = []
    for k in range(parts):
        first = pl.multiple_of(lax.rem(at_ref[1] - k + parts, parts) * rows, rows)
        u_copies.append(pltpu.make_async_copy(us[k], ua.at[pl.ds(first, rows)], sem.at[k]))
    near = [
        pltpu.make_async_copy(k_ref.at[pl.ds(0, depth)], kv.at[i], sem.at[NY + i])
        for i, k_ref in enumerate((k0, k1, k2))
    ]
    top, bottom = k3.shape[0], depth - k3.shape[0]
    far = [
        pltpu.make_async_copy(k3, kv.at[3, pl.ds(0, top)], sem.at[NY + 3]),
        pltpu.make_async_copy(k4.at[pl.ds(0, bottom)], kv.at[3, pl.ds(top, bottom)], sem.at[NY + 4]),
    ]
    for copy in u_copies + near + far:
        copy.start()
    for copy in u_copies:
        copy.wait()
    if parts > 1:
        back = pltpu.make_async_copy(ua, whole, out_sem)
        back.start()
    total = jnp.zeros(out_ref.shape, F32)
    for i in range(NX):
        for copy in (near[i:i + 1] if i < 3 else far):
            copy.wait()
        first = pl.multiple_of(lax.rem(at_ref[0] + ORDER[i], NX) * depth, depth)
        total += jnp.dot(ua[:, pl.ds(first, depth)], kv[i], preferred_element_type=F32)
    out_ref[...] = total.astype(BF)
    if parts > 1:
        back.wait()


def memorise(at, us, payloads):
    width = us[0].shape[1]
    tokens = us[0].shape[0] * len(us)
    cols = payloads[0].shape[1]
    depth = width // NX
    memory = jax.ShapeDtypeStruct((tokens, cols), BF)
    assembled = [jax.ShapeDtypeStruct((tokens, width), BF)] if len(us) > 1 else []
    return pl.pallas_call(
        functools.partial(memory_kernel, len(us)),
        in_specs=[pl.BlockSpec(memory_space=pltpu.SMEM)] + [ANY] * (len(us) + 5),
        out_specs=[VMEM_ALL] + [ANY] * len(assembled),
        scratch_shapes=[
            pltpu.VMEM((tokens, width), BF),
            pltpu.VMEM((NX, depth, cols), BF),
            pltpu.SemaphoreType.DMA((NY + 5,)),
            pltpu.SemaphoreType.DMA,
        ],
        out_shape=[memory] + assembled,
        cost_estimate=pl.CostEstimate(
            flops=2 * tokens * width * cols, bytes_accessed=2 * width * cols, transcendentals=0
        ),
        compiler_params=pltpu.CompilerParams(vmem_limit_bytes=12 * MIB),
        name="memorise",
    )(at, *us, *payloads)


def ring_pieces(block, base):
    rows = block.shape[0]
    half = rows // 2
    pieces = [(0, base, rows, block)]
    up = down = block
    for s in range(1, NZ // 2):
        up = shifted(up, "z", 1)
        down = shifted(down, "z", -1)
        pieces += [(s, base, rows, up), (NZ - s, base, rows, down)]
    pieces += [
        (NZ // 2, base, half, shifted(up[:half], "z", 1)),
        (NZ // 2, base + half, half, shifted(down[half:], "z", -1)),
    ]
    return pieces


PAD = 8


def plan_kernel(ids_ref, z_ref, x_ref, core_ref, one_list, two_list, counts_ref):
    my_z, my_x, core = z_ref[0], x_ref[0], core_ref[0]

    def held(row):
        return jnp.logical_and(row >= 0, jnp.bitwise_and(jnp.right_shift(row, 2), NX - 1) == my_x)

    def wanted(w, n):
        group = jnp.maximum(w - 1, 0)
        step = jnp.bitwise_and(jnp.right_shift(group, 3) - my_x, NX - 1)
        here = step * 16 + jnp.bitwise_and(group, 7) * 2
        under = NX * 16 + jnp.bitwise_and(NX - 1 - my_x, NX - 1) * 16 + 14
        row = ids_ref[jnp.where(w == 0, under, here) + n]
        return jnp.where(jnp.logical_and(w == 0, my_z == 0), -1, row)

    def place(row):
        distance = jnp.bitwise_and(my_z - jnp.right_shift(row, 4), NZ - 1)
        local = jnp.bitwise_and(row, 3)
        half = jnp.bitwise_and(jnp.right_shift(local, 1) + core, 1)
        return distance * 512 + half * 256 + jnp.bitwise_and(local, 1) * 128

    def note(w, counts):
        ones, twos = counts
        rows = [wanted(w, n) for n in range(2)]
        ok = [held(row).astype(jnp.int32) for row in rows]
        single, both = ok[0] + ok[1] == 1, ok[0] + ok[1] == 2
        spot = place(jnp.maximum(jnp.where(ok[0] == 1, rows[0], rows[1]), 0))
        one_list[2 * ones] = w
        one_list[2 * ones + 1] = spot
        two_list[3 * twos] = w
        two_list[3 * twos + 1] = spot
        two_list[3 * twos + 2] = place(jnp.maximum(rows[1], 0))
        return ones + single.astype(jnp.int32), twos + both.astype(jnp.int32)

    ones, twos = lax.fori_loop(0, NX * 8 + 1, note, (0, 0))
    counts_ref[0] = ones
    counts_ref[1] = twos


def plan(ids, my_z, my_x, core):
    smem = pl.BlockSpec(memory_space=pltpu.SMEM)
    return pl.pallas_call(
        plan_kernel,
        in_specs=[smem] * 4,
        out_specs=[smem] * 3,
        out_shape=[
            jax.ShapeDtypeStruct((128,), jnp.int32),
            jax.ShapeDtypeStruct((128,), jnp.int32),
            jax.ShapeDtypeStruct((2,), jnp.int32),
        ],
        name="plan",
    )(ids, my_z, my_x, core)


def window_kernel(layout, one_list, two_list, counts_ref, x_ref, *refs):
    q_refs, refs = refs[:NX], refs[NX:]
    pieces = refs[:len(layout)]
    out_ref = refs[len(layout)]
    table, q_in, qs, outs, stats, sem, q_sem = refs[len(layout) + 1:]
    ones, twos = counts_ref[0], counts_ref[1]
    plane_rows = NX * 1024
    total_rows = qs.shape[0]
    q_copies = [pltpu.make_async_copy(q_refs[d].at[pl.ds(0, 1024)], q_in.at[d], q_sem.at[d]) for d in range(NX)]
    copies = [
        pltpu.make_async_copy(pieces[i], table.at[pl.ds(distance * 512 + first, rows)], sem.at[i])
        for i, (distance, first, rows) in enumerate(layout)
    ]
    for copy in q_copies + copies:
        copy.start()
    outs[...] = jnp.zeros_like(outs)
    stats[...] = jnp.full_like(stats, MASKED)
    qs[0:PAD, :] = jnp.zeros((PAD, HS), F32)
    qs[PAD + plane_rows:, :] = jnp.zeros((total_rows - PAD - plane_rows, HS), F32)
    for d in range(NX):
        q_copies[d].wait()
        first = pl.multiple_of(PAD + jnp.bitwise_and(x_ref[0] + d, NX - 1) * 1024, 8)
        qs[pl.ds(first, 1024), :] = q_in[d].astype(F32)
    for copy in copies:
        copy.wait()

    def attend(items):
        jobs = []
        for start, spots in items:
            for h in range(2):
                q = qs[pl.ds(start + h, GROUP, stride=2), :].astype(BF)
                k = [table[pl.ds(pl.multiple_of(f, ROW), ROW), h * 256:h * 256 + HS] for f in spots]
                k = k[0] if len(k) == 1 else jnp.concatenate(k, axis=0)
                s = lax.dot_general(q, k, (((1,), (1,)), ((), ())), preferred_element_type=F32)
                jobs.append([start + h, h, spots, s])
        for job in jobs:
            job[3] = job[3] * LOG_SCALE
            job.append(jnp.max(job[3], axis=1, keepdims=True))
        for job in jobs:
            job[3] = jnp.exp2(job[3] - job[4])
            job.append(jnp.sum(job[3], axis=1, keepdims=True))
        for first, h, spots, p, m, total in jobs:
            v = [table[pl.ds(pl.multiple_of(f, ROW), ROW), h * 256 + HS:h * 256 + 2 * HS] for f in spots]
            v = v[0] if len(v) == 1 else jnp.concatenate(v, axis=0)
            out = jnp.dot(p.astype(BF), v, preferred_element_type=F32) * (1.0 / total)
            outs[pl.ds(first, GROUP, stride=2), :] = out
            stats[pl.ds(first, GROUP, stride=2), :] = jnp.broadcast_to(m + jnp.log2(total), (GROUP, HS))

    def query_row(w):
        return PAD + 2 * (GROUP * w - 1)

    def one_pair(i, carry):
        items = []
        for lane in range(2):
            at = jnp.minimum(2 * i + lane, ones - 1)
            items.append((query_row(one_list[2 * at]), [one_list[2 * at + 1]]))
        attend(items)
        return carry

    def two(i, carry):
        attend([(query_row(two_list[3 * i]), [two_list[3 * i + 1], two_list[3 * i + 2]])])
        return carry

    lax.fori_loop(0, (ones + 1) // 2, one_pair, 0)
    lax.fori_loop(0, twos, two, 0)
    eye = lax.broadcasted_iota(jnp.int32, (HS, HS), 0) == lax.broadcasted_iota(jnp.int32, (HS, HS), 1)
    for x in range(NX):
        base = PAD + x * 1024
        out_ref[x, 0:1024] = outs[base:base + 1024, :].astype(BF)
        lines = []
        for b in range(8):
            block = stats[base + b * HS:base + (b + 1) * HS, :]
            lines.append(jnp.sum(jnp.where(eye, block, 0.0), axis=0, keepdims=True))
        lse = jnp.concatenate(lines, axis=0)
        high = lse.astype(BF)
        rest = lse - high.astype(F32)
        middle = rest.astype(BF)
        low = (rest - middle.astype(F32)).astype(BF)
        tail = jnp.concatenate([high.astype(F32), middle.astype(F32), low.astype(F32), jnp.zeros((8, HS), F32)], axis=0)
        out_ref[x, 1024:1056] = tail.astype(BF)


def windows(lists, my_x, queries, pieces):
    layout = tuple((d, first, rows) for d, first, rows, _ in pieces)
    total = PAD + NX * 1024 + 2 * GROUP
    smem = pl.BlockSpec(memory_space=pltpu.SMEM)
    return pl.pallas_call(
        functools.partial(window_kernel, layout),
        in_specs=[smem] * 4 + [ANY] * (NX + len(pieces)),
        out_specs=VMEM_ALL,
        scratch_shapes=[
            pltpu.VMEM((NZ * 4 * ROW, 512), BF),
            pltpu.VMEM((NX, 1024, HS), BF),
            pltpu.VMEM((total, HS), F32),
            pltpu.VMEM((total, HS), F32),
            pltpu.VMEM((total, HS), F32),
            pltpu.SemaphoreType.DMA((len(pieces),)),
            pltpu.SemaphoreType.DMA((NX,)),
        ],
        out_shape=jax.ShapeDtypeStruct((NX, 1056, HS), BF),
        cost_estimate=pl.CostEstimate(flops=10**9, bytes_accessed=8 * 2**20, transcendentals=10**6),
        compiler_params=pltpu.CompilerParams(vmem_limit_bytes=44 * MIB),
        name="windows",
    )(*lists, my_x, *queries, *[piece[-1] for piece in pieces])


def combine_kernel(parts_ref, out_ref):
    logs = []
    for x in range(NX):
        tail = parts_ref[x, 1024:1056].astype(F32)
        logs.append(tail[0:8] + tail[8:16] + tail[16:24])
    m = functools.reduce(jnp.maximum, logs)
    weights = [jnp.exp2(v - m) for v in logs]
    inv = 1.0 / functools.reduce(jnp.add, weights)
    weights = [w * inv for w in weights]
    eye = lax.broadcasted_iota(jnp.int32, (HS, HS), 0) == lax.broadcasted_iota(jnp.int32, (HS, HS), 1)
    for b in range(8):
        total = jnp.zeros((HS, HS), F32)
        for x in range(NX):
            line = jnp.broadcast_to(weights[x][b:b + 1, :], (HS, HS))
            column = jnp.sum(jnp.where(eye, line, 0.0), axis=1, keepdims=True)
            total += column * parts_ref[x, b * HS:(b + 1) * HS].astype(F32)
        out_ref[b * HS:(b + 1) * HS, :] = total.astype(BF)


def combine(parts):
    return pl.pallas_call(
        combine_kernel,
        in_specs=[VMEM_ALL],
        out_specs=VMEM_ALL,
        out_shape=jax.ShapeDtypeStruct((1024, HS), BF),
        cost_estimate=pl.CostEstimate(flops=10**7, bytes_accessed=2 * 2**20, transcendentals=0),
        compiler_params=pltpu.CompilerParams(vmem_limit_bytes=8 * MIB),
        name="combine",
    )(parts)


def as_index(*values):
    return jnp.stack(values).astype(jnp.int32)


def on_device(corpus, enc_qkv, enc_out, cca_kv, gain_in, gain_out, queries, nbr_ids):
    width = corpus.shape[2]
    my_z, my_x, my_y, core = (lax.axis_index(a) for a in ("z", "x", "y", "c"))
    corpus_flat = corpus.reshape(-1, width)
    e_own = enc_out.reshape(2 * HS, width)
    e_other = shifted(e_own, "c", 1)

    kv = lax.optimization_barrier(cca_kv.reshape(cca_kv.shape[0], 512))
    kv = spread(kv, "z").reshape(-1, 512)

    w_rows = enc_qkv.transpose(0, 2, 1, 3).reshape(width * 6, HS)
    att_own, att_send = encode(corpus_flat, w_rows, gain_in.reshape(1, width), as_index(core), as_index(my_y))
    nbr_ids, queries, att_send = lax.optimization_barrier((nbr_ids, queries, att_send))
    att_other = shifted(att_send, "c", 1)

    id_rows = jnp.pad(nbr_ids.astype(BF), ((0, 8), (0, HS - 2)))
    q_rows = jnp.concatenate([queries.reshape(1024, HS), id_rows], axis=0)
    qs = [q_rows] + [shifted(q_rows, "x", -d) for d in range(1, NX)]
    terms = project(att_own, att_other, e_own, e_other)

    terms = [terms[0]] + [shifted(terms[k], "y", k) for k in range(1, NY)]
    kv, terms[1], terms[3], qs = lax.optimization_barrier((kv, terms[1], terms[3], qs))
    got = jnp.stack([q[1024:1032, 0:2] for q in qs]).astype(jnp.int32).reshape(-1)
    below = shifted(got, "z", 1)
    from_left = shifted(kv, "x", 1)
    from_right = shifted(kv, "x", -1)

    u = normalise(terms, corpus_flat, gain_out.reshape(1, width), as_index(core * NY + my_y))
    us = [u] + [shifted(u, "y", k) for k in range(1, NY)]
    lists = plan(jnp.concatenate([got, below]), as_index(my_z), as_index(my_x), as_index(core))
    us[1], lists, from_left, from_right = lax.optimization_barrier((us[1], lists, from_left, from_right))
    half = kv.shape[0] // 2
    far_top = shifted(from_left[:half], "x", 1)
    far_bottom = shifted(from_right[half:], "x", -1)
    weights = [kv, from_left, from_right, far_top, far_bottom]
    us[1], us[3], lists, weights = lax.optimization_barrier((us[1], us[3], lists, weights))
    at = as_index(my_x, my_y)
    memory_own, u_own = memorise(at, us, weights)
    u_other = shifted(u_own, "c", 1)
    pieces = ring_pieces(memory_own, 0)
    (memory_other,) = memorise(at, [u_other], weights)
    pieces += ring_pieces(memory_other, 2 * ROW)

    parts = windows(lists, as_index(my_x), qs, pieces)
    parts = lax.all_to_all(parts, "x", split_axis=0, concat_axis=0, tiled=True)
    return combine(parts).reshape(512, 2, HS)


def solution(mesh):
    inner = Mesh(mesh.devices.reshape(NZ, NX, NY, NC), ("z", "x", "y", "c"))
    seq, head = ("z", "x"), ("y", "c")
    placed = (
        P(seq, None, None),
        P(None, head, None, None),
        P(head, None, None),
        P(seq, head, None, None),
        P(),
        P(),
        P(seq, head, None),
        P(seq, None),
    )
    return jax.shard_map(
        on_device, mesh=inner, in_specs=placed, out_specs=P(seq, head, None), check_vma=False
    )
```

```python
import functools

import jax
import jax.numpy as jnp
from jax import lax
from jax.experimental import pallas as pl
from jax.experimental.pallas import tpu as pltpu
from jax.sharding import Mesh, PartitionSpec as P

GROUP = 64
EPS = 1e-06
MIB = 2**20
NZ, NX, NY, NC = 8, 4, 4, 2
ROW = 128
HS = 128
MASKED = -1e30
LOG_SCALE = HS ** -0.5 * 1.4426950408889634
BF = jnp.bfloat16
F32 = jnp.float32
ANY = pl.BlockSpec(memory_space=pl.ANY)
VMEM_ALL = pl.BlockSpec(memory_space=pltpu.VMEM)


def shifted(value, axis, steps):
    n = lax.axis_size(axis)
    return lax.ppermute(value, axis, [(i, (i + steps) % n) for i in range(n)])


def spread(value, axis):
    n = lax.axis_size(axis)
    copies = jnp.broadcast_to(value[None], (n,) + value.shape)
    return lax.all_to_all(copies, axis, split_axis=0, concat_axis=0, tiled=True)


def encoder_kernel(core_ref, y_ref, x_ref, w_ref, g_ref, own_ref, send_ref, wide, wmat, acc, ssq):
    step = pl.program_id(0)
    depth = x_ref.shape[1]

    @pl.when(step == 0)
    def _():
        acc[...] = jnp.zeros_like(acc)
        ssq[...] = jnp.zeros_like(ssq)

    wide[...] = w_ref[...].astype(F32)
    for col in range(6):
        wmat[:, col * HS:(col + 1) * HS] = wide[pl.ds(col, depth, stride=6), :].astype(BF)
    x = x_ref[...].astype(F32)
    ssq[...] += jnp.sum(x * x, axis=1, keepdims=True)
    xg = (x * g_ref[...]).astype(BF)
    acc[...] += jnp.dot(xg, wmat[...], preferred_element_type=F32)

    @pl.when(step == pl.num_programs(0) - 1)
    def _():
        core, my_y = core_ref[0], y_ref[0]
        done = []
        total = depth * pl.num_programs(0)
        scale = lax.rsqrt(ssq[...] / total + EPS)
        rows = x_ref.shape[0] // ROW
        for pair in range(rows // 2):
            spots = [(r, h) for r in (2 * pair, 2 * pair + 1) for h in range(2)]

            def part(r, col):
                sl = slice(r * ROW, (r + 1) * ROW)
                return (acc[sl, col * HS:(col + 1) * HS] * scale[sl]).astype(BF)

            scores = [
                lax.dot_general(
                    part(r, h), part(r, 2 + h), (((1,), (1,)), ((), ())), preferred_element_type=F32
                ) * LOG_SCALE
                for r, h in spots
            ]
            tops = [jnp.max(s, axis=1, keepdims=True) for s in scores]
            probs = [jnp.exp2(s - m) for s, m in zip(scores, tops)]
            sums = [jnp.sum(p, axis=1, keepdims=True) for p in probs]
            atts = [
                (jnp.dot(p.astype(BF), part(r, 4 + h), preferred_element_type=F32) * (1.0 / total_p)).astype(BF)
                for (r, h), p, total_p in zip(spots, probs, sums)
            ]
            done.append([jnp.concatenate(atts[2 * i:2 * i + 2], axis=1) for i in range(2)])
        for i in range(2):
            own = jnp.where(core == 0, done[0][i], done[1][i])
            send = jnp.where(core == 0, done[1][i], done[0][i])
            for half in range(2):
                k = jnp.bitwise_and(2 * i + half - my_y, NY - 1)
                spot = pl.ds(pl.multiple_of(k * 64, 64), 64)
                own_ref[spot, :] = own[half * 64:(half + 1) * 64]
                send_ref[spot, :] = send[half * 64:(half + 1) * 64]


def encode(corpus_flat, w_rows, gain, core, my_y):
    tokens, width = corpus_flat.shape
    steps = 4
    depth = width // steps
    return pl.pallas_call(
        encoder_kernel,
        grid_spec=pltpu.PrefetchScalarGridSpec(
            num_scalar_prefetch=2,
            grid=(steps,),
            in_specs=[
                pl.BlockSpec((tokens, depth), lambda i, c, y: (0, i)),
                pl.BlockSpec((depth * 6, HS), lambda i, c, y: (i, 0)),
                pl.BlockSpec((1, depth), lambda i, c, y: (0, i)),
            ],
            out_specs=[pl.BlockSpec((2 * ROW, 2 * HS), lambda i, c, y: (0, 0))] * 2,
            scratch_shapes=[
                pltpu.VMEM((depth * 6, HS), F32),
                pltpu.VMEM((depth, 6 * HS), BF),
                pltpu.VMEM((tokens, 6 * HS), F32),
                pltpu.VMEM((tokens, 1), F32),
            ],
        ),
        out_shape=[jax.ShapeDtypeStruct((2 * ROW, 2 * HS), BF)] * 2,
        cost_estimate=pl.CostEstimate(
            flops=2 * tokens * width * 6 * HS, bytes_accessed=(tokens + 768) * width * 2, transcendentals=0
        ),
        compiler_params=pltpu.CompilerParams(vmem_limit_bytes=60 * MIB),
        name="encoder",
    )(core, my_y, corpus_flat, w_rows, gain)


def project_kernel(a_ref, b_ref, ea_ref, eb_ref, *outs):
    rows = a_ref.shape[0] // NY
    value = jnp.dot(a_ref[...], ea_ref[...], preferred_element_type=F32)
    value += jnp.dot(b_ref[...], eb_ref[...], preferred_element_type=F32)
    for k in range(NY):
        outs[k][...] = value[k * rows:(k + 1) * rows].astype(BF)


def project(att, att_other, e_own, e_other):
    tokens, depth = att_other.shape
    width = e_own.shape[1]
    cols = 1024
    rows = tokens // NY
    return pl.pallas_call(
        project_kernel,
        grid=(width // cols,),
        in_specs=[
            pl.BlockSpec((tokens, depth), lambda i: (0, 0)),
            pl.BlockSpec((tokens, depth), lambda i: (0, 0)),
            pl.BlockSpec((depth, cols), lambda i: (0, i)),
            pl.BlockSpec((depth, cols), lambda i: (0, i)),
        ],
        out_specs=[pl.BlockSpec((rows, cols), lambda i: (0, i))] * NY,
        out_shape=[jax.ShapeDtypeStruct((rows, width), BF)] * NY,
        cost_estimate=pl.CostEstimate(
            flops=4 * tokens * depth * width, bytes_accessed=4 * depth * width, transcendentals=0
        ),
        compiler_params=pltpu.CompilerParams(vmem_limit_bytes=44 * MIB),
        name="project",
    )(att, att_other, e_own, e_other)


def norm_kernel(block_ref, t0, t1, t2, t3, x_ref, g_ref, out_ref):
    total = x_ref[...].astype(F32)
    for term in (t0, t1, t2, t3):
        total += term[...].astype(F32)
    rinv = lax.rsqrt(jnp.mean(total * total, axis=1, keepdims=True) + EPS)
    u = (total * rinv * g_ref[...]).astype(BF)
    for z in range(NZ):
        for x in range(NX):
            src, dst = (z * NX + x) * HS, (x * NZ + z) * HS
            out_ref[:, dst:dst + HS] = u[:, src:src + HS]


def normalise(terms, corpus_flat, gain, block):
    rows, width = terms[0].shape
    whole = pl.BlockSpec((rows, width), lambda i, b: (0, 0))
    return pl.pallas_call(
        norm_kernel,
        grid_spec=pltpu.PrefetchScalarGridSpec(
            num_scalar_prefetch=1,
            grid=(1,),
            in_specs=[whole] * NY
            + [
                pl.BlockSpec((rows, width), lambda i, b: (b[0], 0)),
                pl.BlockSpec((1, width), lambda i, b: (0, 0)),
            ],
            out_specs=whole,
        ),
        out_shape=jax.ShapeDtypeStruct((rows, width), BF),
        cost_estimate=pl.CostEstimate(flops=8 * rows * width, bytes_accessed=12 * rows * width, transcendentals=0),
        compiler_params=pltpu.CompilerParams(vmem_limit_bytes=60 * MIB),
        name="normalise",
    )(block, *terms, corpus_flat, gain)


ORDER = (0, NX - 1, 1, 2)


def memory_kernel(parts, at_ref, *refs):
    us = refs[:parts]
    k0, k1, k2, k3, k4 = refs[parts:parts + 5]
    out_ref = refs[parts + 5]
    rest = refs[parts + 6:]
    if parts > 1:
        whole, rest = rest[0], rest[1:]
    ua, kv, sem, out_sem = rest
    depth = NZ * HS
    rows = ua.shape[0] // parts
    u_copies = []
    for k in range(parts):
        first = pl.multiple_of(lax.rem(at_ref[1] - k + parts, parts) * rows, rows)
        u_copies.append(pltpu.make_async_copy(us[k], ua.at[pl.ds(first, rows)], sem.at[k]))
    near = [
        pltpu.make_async_copy(k_ref.at[pl.ds(0, depth)], kv.at[i], sem.at[NY + i])
        for i, k_ref in enumerate((k0, k1, k2))
    ]
    top, bottom = k3.shape[0], depth - k3.shape[0]
    far = [
        pltpu.make_async_copy(k3, kv.at[3, pl.ds(0, top)], sem.at[NY + 3]),
        pltpu.make_async_copy(k4.at[pl.ds(0, bottom)], kv.at[3, pl.ds(top, bottom)], sem.at[NY + 4]),
    ]
    for copy in u_copies + near + far:
        copy.start()
    for copy in u_copies:
        copy.wait()
    if parts > 1:
        back = pltpu.make_async_copy(ua, whole, out_sem)
        back.start()
    total = jnp.zeros(out_ref.shape, F32)
    for i in range(NX):
        for copy in (near[i:i + 1] if i < 3 else far):
            copy.wait()
        first = pl.multiple_of(lax.rem(at_ref[0] + ORDER[i], NX) * depth, depth)
        total += jnp.dot(ua[:, pl.ds(first, depth)], kv[i], preferred_element_type=F32)
    out_ref[...] = total.astype(BF)
    if parts > 1:
        back.wait()


def memorise(at, us, payloads):
    width = us[0].shape[1]
    tokens = us[0].shape[0] * len(us)
    cols = payloads[0].shape[1]
    depth = width // NX
    memory = jax.ShapeDtypeStruct((tokens, cols), BF)
    assembled = [jax.ShapeDtypeStruct((tokens, width), BF)] if len(us) > 1 else []
    return pl.pallas_call(
        functools.partial(memory_kernel, len(us)),
        in_specs=[pl.BlockSpec(memory_space=pltpu.SMEM)] + [ANY] * (len(us) + 5),
        out_specs=[VMEM_ALL] + [ANY] * len(assembled),
        scratch_shapes=[
            pltpu.VMEM((tokens, width), BF),
            pltpu.VMEM((NX, depth, cols), BF),
            pltpu.SemaphoreType.DMA((NY + 5,)),
            pltpu.SemaphoreType.DMA,
        ],
        out_shape=[memory] + assembled,
        cost_estimate=pl.CostEstimate(
            flops=2 * tokens * width * cols, bytes_accessed=2 * width * cols, transcendentals=0
        ),
        compiler_params=pltpu.CompilerParams(vmem_limit_bytes=12 * MIB),
        name="memorise",
    )(at, *us, *payloads)


def ring_pieces(block, base):
    rows = block.shape[0]
    half = rows // 2
    pieces = [(0, base, rows, block)]
    up = down = block
    for s in range(1, NZ // 2):
        up = shifted(up, "z", 1)
        down = shifted(down, "z", -1)
        pieces += [(s, base, rows, up), (NZ - s, base, rows, down)]
    pieces += [
        (NZ // 2, base, half, shifted(up[:half], "z", 1)),
        (NZ // 2, base + half, half, shifted(down[half:], "z", -1)),
    ]
    return pieces


PAD = 8


def plan_kernel(ids_ref, z_ref, x_ref, core_ref, one_list, two_list, counts_ref):
    my_z, my_x, core = z_ref[0], x_ref[0], core_ref[0]

    def held(row):
        return jnp.logical_and(row >= 0, jnp.bitwise_and(jnp.right_shift(row, 2), NX - 1) == my_x)

    def wanted(w, n):
        group = jnp.maximum(w - 1, 0)
        step = jnp.bitwise_and(jnp.right_shift(group, 3) - my_x, NX - 1)
        here = step * 16 + jnp.bitwise_and(group, 7) * 2
        under = NX * 16 + jnp.bitwise_and(NX - 1 - my_x, NX - 1) * 16 + 14
        row = ids_ref[jnp.where(w == 0, under, here) + n]
        return jnp.where(jnp.logical_and(w == 0, my_z == 0), -1, row)

    def place(row):
        distance = jnp.bitwise_and(my_z - jnp.right_shift(row, 4), NZ - 1)
        local = jnp.bitwise_and(row, 3)
        half = jnp.bitwise_and(jnp.right_shift(local, 1) + core, 1)
        return distance * 512 + half * 256 + jnp.bitwise_and(local, 1) * 128

    def note(w, counts):
        ones, twos = counts
        rows = [wanted(w, n) for n in range(2)]
        ok = [held(row).astype(jnp.int32) for row in rows]
        single, both = ok[0] + ok[1] == 1, ok[0] + ok[1] == 2
        spot = place(jnp.maximum(jnp.where(ok[0] == 1, rows[0], rows[1]), 0))
        one_list[2 * ones] = w
        one_list[2 * ones + 1] = spot
        two_list[3 * twos] = w
        two_list[3 * twos + 1] = spot
        two_list[3 * twos + 2] = place(jnp.maximum(rows[1], 0))
        return ones + single.astype(jnp.int32), twos + both.astype(jnp.int32)

    ones, twos = lax.fori_loop(0, NX * 8 + 1, note, (0, 0))
    counts_ref[0] = ones
    counts_ref[1] = twos


def plan(ids, my_z, my_x, core):
    smem = pl.BlockSpec(memory_space=pltpu.SMEM)
    return pl.pallas_call(
        plan_kernel,
        in_specs=[smem] * 4,
        out_specs=[smem] * 3,
        out_shape=[
            jax.ShapeDtypeStruct((128,), jnp.int32),
            jax.ShapeDtypeStruct((128,), jnp.int32),
            jax.ShapeDtypeStruct((2,), jnp.int32),
        ],
        name="plan",
    )(ids, my_z, my_x, core)


def window_kernel(layout, one_list, two_list, counts_ref, x_ref, *refs):
    q_refs, refs = refs[:NX], refs[NX:]
    pieces = refs[:len(layout)]
    out_ref = refs[len(layout)]
    table, q_in, qs, outs, stats, sem, q_sem = refs[len(layout) + 1:]
    ones, twos = counts_ref[0], counts_ref[1]
    plane_rows = NX * 1024
    total_rows = qs.shape[0]
    q_copies = [pltpu.make_async_copy(q_refs[d].at[pl.ds(0, 1024)], q_in.at[d], q_sem.at[d]) for d in range(NX)]
    copies = [
        pltpu.make_async_copy(pieces[i], table.at[pl.ds(distance * 512 + first, rows)], sem.at[i])
        for i, (distance, first, rows) in enumerate(layout)
    ]
    for copy in q_copies + copies:
        copy.start()
    outs[...] = jnp.zeros_like(outs)
    stats[...] = jnp.full_like(stats, MASKED)
    qs[0:PAD, :] = jnp.zeros((PAD, HS), F32)
    qs[PAD + plane_rows:, :] = jnp.zeros((total_rows - PAD - plane_rows, HS), F32)
    for d in range(NX):
        q_copies[d].wait()
        first = pl.multiple_of(PAD + jnp.bitwise_and(x_ref[0] + d, NX - 1) * 1024, 8)
        qs[pl.ds(first, 1024), :] = q_in[d].astype(F32)
    for copy in copies:
        copy.wait()

    def attend(items):
        jobs = []
        for start, spots in items:
            for h in range(2):
                q = qs[pl.ds(start + h, GROUP, stride=2), :].astype(BF)
                k = [table[pl.ds(pl.multiple_of(f, ROW), ROW), h * 256:h * 256 + HS] for f in spots]
                k = k[0] if len(k) == 1 else jnp.concatenate(k, axis=0)
                s = lax.dot_general(q, k, (((1,), (1,)), ((), ())), preferred_element_type=F32)
                jobs.append([start + h, h, spots, s])
        for job in jobs:
            job[3] = job[3] * LOG_SCALE
            job.append(jnp.max(job[3], axis=1, keepdims=True))
        for job in jobs:
            job[3] = jnp.exp2(job[3] - job[4])
            job.append(jnp.sum(job[3], axis=1, keepdims=True))
        for first, h, spots, p, m, total in jobs:
            v = [table[pl.ds(pl.multiple_of(f, ROW), ROW), h * 256 + HS:h * 256 + 2 * HS] for f in spots]
            v = v[0] if len(v) == 1 else jnp.concatenate(v, axis=0)
            out = jnp.dot(p.astype(BF), v, preferred_element_type=F32) * (1.0 / total)
            outs[pl.ds(first, GROUP, stride=2), :] = out
            stats[pl.ds(first, GROUP, stride=2), :] = jnp.broadcast_to(m + jnp.log2(total), (GROUP, HS))

    def query_row(w):
        return PAD + 2 * (GROUP * w - 1)

    def one_pair(i, carry):
        items = []
        for lane in range(2):
            at = jnp.minimum(2 * i + lane, ones - 1)
            items.append((query_row(one_list[2 * at]), [one_list[2 * at + 1]]))
        attend(items)
        return carry

    def two(i, carry):
        attend([(query_row(two_list[3 * i]), [two_list[3 * i + 1], two_list[3 * i + 2]])])
        return carry

    lax.fori_loop(0, (ones + 1) // 2, one_pair, 0)
    lax.fori_loop(0, twos, two, 0)
    eye = lax.broadcasted_iota(jnp.int32, (HS, HS), 0) == lax.broadcasted_iota(jnp.int32, (HS, HS), 1)
    for x in range(NX):
        base = PAD + x * 1024
        out_ref[x, 0:1024] = outs[base:base + 1024, :].astype(BF)
        lines = []
        for b in range(8):
            block = stats[base + b * HS:base + (b + 1) * HS, :]
            lines.append(jnp.sum(jnp.where(eye, block, 0.0), axis=0, keepdims=True))
        lse = jnp.concatenate(lines, axis=0)
        high = lse.astype(BF)
        rest = lse - high.astype(F32)
        middle = rest.astype(BF)
        low = (rest - middle.astype(F32)).astype(BF)
        tail = jnp.concatenate([high.astype(F32), middle.astype(F32), low.astype(F32), jnp.zeros((8, HS), F32)], axis=0)
        out_ref[x, 1024:1056] = tail.astype(BF)


def windows(lists, my_x, queries, pieces):
    layout = tuple((d, first, rows) for d, first, rows, _ in pieces)
    total = PAD + NX * 1024 + 2 * GROUP
    smem = pl.BlockSpec(memory_space=pltpu.SMEM)
    return pl.pallas_call(
        functools.partial(window_kernel, layout),
        in_specs=[smem] * 4 + [ANY] * (NX + len(pieces)),
        out_specs=VMEM_ALL,
        scratch_shapes=[
            pltpu.VMEM((NZ * 4 * ROW, 512), BF),
            pltpu.VMEM((NX, 1024, HS), BF),
            pltpu.VMEM((total, HS), F32),
            pltpu.VMEM((total, HS), F32),
            pltpu.VMEM((total, HS), F32),
            pltpu.SemaphoreType.DMA((len(pieces),)),
            pltpu.SemaphoreType.DMA((NX,)),
        ],
        out_shape=jax.ShapeDtypeStruct((NX, 1056, HS), BF),
        cost_estimate=pl.CostEstimate(flops=10**9, bytes_accessed=8 * 2**20, transcendentals=10**6),
        compiler_params=pltpu.CompilerParams(vmem_limit_bytes=44 * MIB),
        name="windows",
    )(*lists, my_x, *queries, *[piece[-1] for piece in pieces])


def combine_kernel(parts_ref, out_ref):
    logs = []
    for x in range(NX):
        tail = parts_ref[x, 1024:1056].astype(F32)
        logs.append(tail[0:8] + tail[8:16] + tail[16:24])
    m = functools.reduce(jnp.maximum, logs)
    weights = [jnp.exp2(v - m) for v in logs]
    inv = 1.0 / functools.reduce(jnp.add, weights)
    weights = [w * inv for w in weights]
    eye = lax.broadcasted_iota(jnp.int32, (HS, HS), 0) == lax.broadcasted_iota(jnp.int32, (HS, HS), 1)
    for b in range(8):
        total = jnp.zeros((HS, HS), F32)
        for x in range(NX):
            line = jnp.broadcast_to(weights[x][b:b + 1, :], (HS, HS))
            column = jnp.sum(jnp.where(eye, line, 0.0), axis=1, keepdims=True)
            total += column * parts_ref[x, b * HS:(b + 1) * HS].astype(F32)
        out_ref[b * HS:(b + 1) * HS, :] = total.astype(BF)


def combine(parts):
    return pl.pallas_call(
        combine_kernel,
        in_specs=[VMEM_ALL],
        out_specs=VMEM_ALL,
        out_shape=jax.ShapeDtypeStruct((1024, HS), BF),
        cost_estimate=pl.CostEstimate(flops=10**7, bytes_accessed=2 * 2**20, transcendentals=0),
        compiler_params=pltpu.CompilerParams(vmem_limit_bytes=8 * MIB),
        name="combine",
    )(parts)


def as_index(*values):
    return jnp.stack(values).astype(jnp.int32)


def on_device(corpus, enc_qkv, enc_out, cca_kv, gain_in, gain_out, queries, nbr_ids):
    width = corpus.shape[2]
    my_z, my_x, my_y, core = (lax.axis_index(a) for a in ("z", "x", "y", "c"))
    corpus_flat = corpus.reshape(-1, width)
    e_own = enc_out.reshape(2 * HS, width)
    e_other = shifted(e_own, "c", 1)

    kv = lax.optimization_barrier(cca_kv.reshape(cca_kv.shape[0], 512))
    kv = spread(kv, "z").reshape(-1, 512)

    w_rows = enc_qkv.transpose(0, 2, 1, 3).reshape(width * 6, HS)
    att_own, att_send = encode(corpus_flat, w_rows, gain_in.reshape(1, width), as_index(core), as_index(my_y))
    nbr_ids, queries, att_send = lax.optimization_barrier((nbr_ids, queries, att_send))
    att_other = shifted(att_send, "c", 1)

    id_rows = jnp.pad(nbr_ids.astype(BF), ((0, 8), (0, HS - 2)))
    q_rows = jnp.concatenate([queries.reshape(1024, HS), id_rows], axis=0)
    qs = [q_rows] + [shifted(q_rows, "x", -d) for d in range(1, NX)]
    terms = project(att_own, att_other, e_own, e_other)

    terms = [terms[0]] + [shifted(terms[k], "y", k) for k in range(1, NY)]
    kv, terms[1], terms[3], qs = lax.optimization_barrier((kv, terms[1], terms[3], qs))
    got = jnp.stack([q[1024:1032, 0:2] for q in qs]).astype(jnp.int32).reshape(-1)
    below = shifted(got, "z", 1)
    from_left = shifted(kv, "x", 1)
    from_right = shifted(kv, "x", -1)

    u = normalise(terms, corpus_flat, gain_out.reshape(1, width), as_index(core * NY + my_y))
    us = [u] + [shifted(u, "y", k) for k in range(1, NY)]
    lists = plan(jnp.concatenate([got, below]), as_index(my_z), as_index(my_x), as_index(core))
    us[1], lists, from_left, from_right = lax.optimization_barrier((us[1], lists, from_left, from_right))
    half = kv.shape[0] // 2
    far_top = shifted(from_left[:half], "x", 1)
    far_bottom = shifted(from_right[half:], "x", -1)
    weights = [kv, from_left, from_right, far_top, far_bottom]
    us[1], us[3], lists, weights = lax.optimization_barrier((us[1], us[3], lists, weights))
    at = as_index(my_x, my_y)
    memory_own, u_own = memorise(at, us, weights)
    u_other = shifted(u_own, "c", 1)
    pieces = ring_pieces(memory_own, 0)
    (memory_other,) = memorise(at, [u_other], weights)
    pieces += ring_pieces(memory_other, 2 * ROW)

    parts = windows(lists, as_index(my_x), qs, pieces)
    parts = lax.all_to_all(parts, "x", split_axis=0, concat_axis=0, tiled=True)
    return combine(parts).reshape(512, 2, HS)


def solution(mesh):
    inner = Mesh(mesh.devices.reshape(NZ, NX, NY, NC), ("z", "x", "y", "c"))
    seq, head = ("z", "x"), ("y", "c")
    placed = (
        P(seq, None, None),
        P(None, head, None, None),
        P(head, None, None),
        P(seq, head, None, None),
        P(),
        P(),
        P(seq, head, None),
        P(seq, None),
    )
    return jax.shard_map(
        on_device, mesh=inner, in_specs=placed, out_specs=P(seq, head, None), check_vma=False
    )
```
